32 devices in a mesh: fsdp: 16 (over z, x, core), rep: 2 (over y).
Axes of the slice: x: 2, y: 2, z: 4, core: 2. Of those that a mesh axis runs over, the one named last changes fastest.
Arguments:
- tokens: bfloat16 [65536, 768], P(('fsdp', 'rep')), may hold values from -6 to 6
- piece_start: int32 [64, 2], P(('fsdp', 'rep')), may hold values from 1 to 960, as said below
- piece_length: int32 [64, 2], P(('fsdp', 'rep')), may hold values from 64 to 256, as said below
- query_key_value: bfloat16 [768, 2304], P('fsdp'), as said below
- output_weight: bfloat16 [768, 768], P('fsdp'), may hold values from -0.4375 to 0.4375
- up_weight: bfloat16 [768, 3072], P('fsdp'), may hold values from -0.21875 to 0.21875
- down_weight: bfloat16 [3072, 768], P('fsdp'), may hold values from -0.109375 to 0.109375
- first_gain: bfloat16 [768], P('fsdp'), may hold values from 0.099609375 to 1.8984375
- first_shift: bfloat16 [768], P('fsdp'), may hold values from -3 to 3
- second_gain: bfloat16 [768], P('fsdp'), may hold values from 0.099609375 to 1.8984375
- second_shift: bfloat16 [768], P('fsdp'), may hold values from -3 to 3
- up_bias: bfloat16 [3072], P('fsdp'), may hold values from -3 to 3
- down_bias: bfloat16 [768], P('fsdp'), may hold values from -3 to 3
- cotangent: bfloat16 [65536, 768], P(('fsdp', 'rep')), may hold values from -6 to 6
Outputs:
- block_output: bfloat16 [65536, 768], P(('fsdp', 'rep'))
- grad_tokens: float32 [65536, 768], P(('fsdp', 'rep'))
- grad_query_key_value: float32 [768, 2304], P('fsdp')
- grad_output_weight: float32 [768, 768], P('fsdp')
- grad_up_weight: float32 [768, 3072], P('fsdp')
- grad_down_weight: float32 [3072, 768], P('fsdp')
- grad_first_gain: float32 [768], P('fsdp')
- grad_first_shift: float32 [768], P('fsdp')
- grad_second_gain: float32 [768], P('fsdp')
- grad_second_shift: float32 [768], P('fsdp')
- grad_up_bias: float32 [3072], P('fsdp')
- grad_down_bias: float32 [768], P('fsdp')
The draws below stay inside these ranges and needn't reach their ends.
Inputs may be any that keep to these rules, and one draw needn't show every extreme that they name: `piece_start`: piece p of a sequence starts in positions p * 512 + 1 to (p + 1) * 512 - 1 and ends before (p + 1) * 512; pieces never intersect and never hold position 0. `piece_length`: the first piece of every sequence has exactly 256 tokens. `query_key_value`: entries have a deviation of about 1 / sqrt(768) and lie within four such deviations; columns 0 to 64 - 1 (head 0's queries) are a hundred times smaller.
All inputs are finite; a program needn't handle non-finite values.
Results may differ from the reference program's by a relative error of at most 0.023.
The reference program's roundings to bfloat16 on the way count: a program that leaves them out, or rounds other values in their place, can miss the bound.
Values may be sent and summed in bfloat16 or wider, within the bound.
A program may use at most 512 MiB of HBM per device.

```python
import jax
import jax.numpy as jnp
from jax import lax

D = 768
HEADS = 12
HEAD_DIM = 64
FF = 3072
SEQ = 1024
PIECES = 2
PIECE = 256
SEQS = 64
TOKENS = 65536


def piece_layout(key):
    slot_width = SEQ // PIECES
    lengths = jax.random.randint(jax.random.fold_in(key, 11), (SEQS, PIECES), PIECE // 4, PIECE + 1)
    leading = jnp.arange(PIECES, dtype=jnp.int32)[None, :] == 0
    trailing = jnp.arange(PIECES, dtype=jnp.int32)[None, :] == PIECES - 1
    first_row = jnp.arange(SEQS, dtype=jnp.int32)[:, None] == 0
    corner = first_row & trailing & jnp.logical_not(leading)
    lengths = jnp.where(corner, PIECE // 4, lengths)
    lengths = jnp.where(leading, PIECE, lengths).astype(jnp.int32)
    room = slot_width - lengths
    offsets = jax.random.randint(jax.random.fold_in(key, 23), (SEQS, PIECES), 0, room)
    offsets = jnp.where(first_row & trailing, room - 1, offsets)
    offsets = jnp.where(first_row & leading & jnp.logical_not(trailing), 0, offsets)
    bases = jnp.arange(PIECES, dtype=jnp.int32)[None, :] * slot_width
    starts = (bases + 1 + offsets).astype(jnp.int32)
    return (starts, lengths)


def draw_piece_start(key, part):
    return piece_layout(key)[0]


def draw_piece_length(key, part):
    return piece_layout(key)[1]


def draw_query_key_value(key, part):
    deviation = D ** (-0.5)
    raw = jax.random.truncated_normal(jax.random.fold_in(key, 37), -4.0, 4.0, (D, 3 * D), jnp.float32)
    columns = jnp.arange(3 * D, dtype=jnp.int32)[None, :]
    factor = jnp.where(columns < HEAD_DIM, 0.01, 1.0).astype(jnp.float32)
    return (raw * deviation * factor).astype(jnp.bfloat16)


def steps_of(key, extent, split, low, high):
    def one(position, parts):
        heights = jax.random.uniform(jax.random.fold_in(jax.random.fold_in(key, 6), position), (parts,), jnp.float32, low / len(split), high / len(split))
        return jnp.repeat(jnp.exp(heights), extent[position] // parts).reshape((-1,) + (1,) * (len(extent) - position - 1))

    level = one(*split[0])
    for cut in split[1:]:
        level = level * one(*cut)
    return level


def normal_values(key, extent, scale, limit, shards=(), kind=jnp.bfloat16):
    entries = jax.random.normal(key, extent, jnp.float32) * scale
    if len(shards) > 0:
        entries = steps_of(key, extent, shards, -0.22, 0.18) * entries
    return jnp.clip(entries, min=-limit, max=limit).astype(kind)


def setup_inputs(seed: int = 0) -> dict:
    arg_keys = jax.random.split(jax.random.key(seed), 15)
    tokens = normal_values(arg_keys[0], (TOKENS, D), 1.0, 6.0, ((0, 32),))
    piece_start = draw_piece_start(jax.random.fold_in(arg_keys[14], 71), 0)
    piece_length = draw_piece_length(jax.random.fold_in(arg_keys[14], 71), 0)
    query_key_value = draw_query_key_value(jax.random.fold_in(arg_keys[14], 71), 0)
    output_weight = normal_values(arg_keys[4], (D, D), (D // 4) ** -0.5, 0.4375, ((0, 16),))
    up_weight = normal_values(arg_keys[5], (D, FF), D ** -0.5, 0.21875, ((0, 16),))
    down_weight = normal_values(arg_keys[6], (FF, D), FF ** -0.5, 0.109375, ((0, 16),))
    first_gain = jnp.clip(1.0 + 0.18 * jax.random.normal(arg_keys[7], (D,), jnp.float32), 0.099609375, 1.8984375).astype(jnp.bfloat16)
    first_shift = normal_values(arg_keys[8], (D,), 0.3, 3.0, ((0, 16),))
    second_gain = jnp.clip(1.0 + 0.18 * jax.random.normal(arg_keys[9], (D,), jnp.float32), 0.099609375, 1.8984375).astype(jnp.bfloat16)
    second_shift = normal_values(arg_keys[10], (D,), 0.3, 3.0, ((0, 16),))
    up_bias = normal_values(arg_keys[11], (FF,), 0.5, 3.0, ((0, 16),))
    down_bias = normal_values(arg_keys[12], (D,), 0.5, 3.0, ((0, 16),))
    cotangent = normal_values(arg_keys[13], (TOKENS, D), 1.0, 6.0, ((0, 32),))
    return {"tokens": tokens, "piece_start": piece_start, "piece_length": piece_length, "query_key_value": query_key_value, "output_weight": output_weight, "up_weight": up_weight, "down_weight": down_weight, "first_gain": first_gain, "first_shift": first_shift, "second_gain": second_gain, "second_shift": second_shift, "up_bias": up_bias, "down_bias": down_bias, "cotangent": cotangent}


@jax.custom_vjp
def low(v):
    return lax.optimization_barrier(v.astype(jnp.bfloat16)).astype(jnp.float32)

@jax.custom_vjp
def low_back(v):
    return v

def low_keep(v):
    return (low(v), None)

def low_pass(kept, grad):
    return (grad,)

def back_keep(v):
    return (v, None)

def back_low(kept, grad):
    return (low(grad),)
low.defvjp(low_keep, low_pass)
low_back.defvjp(back_keep, back_low)
PRECISE = lax.Precision.HIGHEST
MASKED_VALUE = -1e+30
EPSILON = 1e-05

def layer_norm(values, gain, shift):
    center = values - lax.optimization_barrier(jnp.mean(values, axis=-1, keepdims=True))
    spread = lax.optimization_barrier(jnp.mean(center * center, axis=-1, keepdims=True))
    return center * lax.rsqrt(spread + EPSILON) * gain + shift

def piece_labels(starts, lengths, length):
    positions = jnp.arange(length, dtype=jnp.int32)
    inside = (positions[:, None] >= starts[None, :]) & (positions[:, None] < starts[None, :] + lengths[None, :])
    numbers = jnp.arange(1, starts.shape[0] + 1, dtype=jnp.int32)
    return lax.optimization_barrier(jnp.sum(jnp.where(inside, numbers[None, :], 0), axis=1)).astype(jnp.int32)

def sequence(rows_in, starts, lengths, query_key_value, output_weight, up_weight, down_weight, first_gain, first_shift, second_gain, second_shift, up_bias, down_bias):
    length = rows_in.shape[0]
    positions = jnp.arange(length, dtype=jnp.int32)
    labels = piece_labels(starts, lengths, length)
    allowed = (positions[None, :] <= positions[:, None]) | (labels[:, None] == labels[None, :]) & (labels[:, None] > 0)
    chosen_mask = allowed & (positions[None, :] != 0) & (positions[None, :] != positions[:, None])
    normed_first = low(layer_norm(rows_in, first_gain, first_shift))
    projected = low(low_back(jnp.dot(normed_first, query_key_value, precision=PRECISE)))
    split_parts = projected.reshape(length, 3, HEADS, HEAD_DIM)
    queries = split_parts[:, 0]
    key_rows = split_parts[:, 1]
    value_rows = split_parts[:, 2]
    scores = low_back(jnp.einsum('qhd,khd->hqk', queries, key_rows, precision=PRECISE) * HEAD_DIM ** (-0.5))
    selected = jnp.where(chosen_mask & (scores[0] > 0), scores[0], 0.0)
    penalty = jnp.cumsum(selected, axis=0) - selected
    logits = jnp.where(allowed[None], scores - penalty[None], MASKED_VALUE)
    largest = lax.optimization_barrier(jnp.max(logits, axis=-1, keepdims=True))
    raised = jnp.exp(logits - largest)
    attention = low(raised / lax.optimization_barrier(jnp.sum(raised, axis=-1, keepdims=True)))
    mixed_heads = jnp.einsum('hqk,khd->qhd', attention, value_rows, precision=PRECISE)
    mixed_rows = low(low_back(mixed_heads.reshape(length, HEADS * HEAD_DIM)))
    branch_out = low_back(jnp.dot(mixed_rows, output_weight, precision=PRECISE))
    middle = rows_in + branch_out
    normed_second = low(layer_norm(middle, second_gain, second_shift))
    before_act = low_back(jnp.dot(normed_second, up_weight, precision=PRECISE) + up_bias)
    hidden = low(low_back(jax.nn.gelu(before_act, approximate=True)))
    return middle + low_back(jnp.dot(hidden, down_weight, precision=PRECISE) + down_bias)

def reference(tokens, piece_start, piece_length, query_key_value, output_weight, up_weight, down_weight, first_gain, first_shift, second_gain, second_shift, up_bias, down_bias, cotangent):
    params = tuple((item.astype(jnp.float32) for item in (query_key_value, output_weight, up_weight, down_weight, first_gain, first_shift, second_gain, second_shift, up_bias, down_bias)))
    inputs_all = tokens.astype(jnp.float32).reshape(SEQS, SEQ, D)

    def forward(inputs_seq, *weights):

        def advance(carry, item):
            rows_in, starts, lengths = item
            return (carry, jax.checkpoint(sequence)(rows_in, starts, lengths, *weights))
        _, results = lax.scan(advance, jnp.zeros((), jnp.float32), (inputs_seq, piece_start, piece_length))
        return results
    results, pullback = jax.vjp(forward, inputs_all, *params)
    grads = pullback(cotangent.astype(jnp.float32).reshape(SEQS, SEQ, D))
    return (results.reshape(SEQS * SEQ, D).astype(jnp.bfloat16), grads[0].reshape(SEQS * SEQ, D), grads[1], grads[2], grads[3], grads[4], grads[5], grads[6], grads[7], grads[8], grads[9], grads[10])
```

```python
import functools

import jax
import jax.numpy as jnp
from jax import lax
from jax.experimental import pallas as pl
from jax.experimental.pallas import tpu as pltpu
from jax.sharding import PartitionSpec as P

HEAD_DIM = 64
PAIR = 2 * HEAD_DIM
ROWS = 256
MASKED_VALUE = -1e30
EPSILON = 1e-05
SCALE = HEAD_DIM**-0.5
GELU_IN = 0.7978845608028654
GELU_CUBE = 0.044715
VMEM_LIMIT = 60 * 1024 * 1024

F32 = jnp.float32
BF16 = jnp.bfloat16


def dot(left, right):
    return lax.dot_general(left, right, (((1,), (0,)), ((), ())), preferred_element_type=F32)


def dot_nt(left, right):
    return lax.dot_general(left, right, (((1,), (1,)), ((), ())), preferred_element_type=F32)


def dot_tn(left, right):
    return lax.dot_general(left, right, (((0,), (0,)), ((), ())), preferred_element_type=F32)


def row_mean(values):
    return jnp.mean(values, axis=-1, keepdims=True)


def normalize(values):
    center = values - row_mean(values)
    inverse = lax.rsqrt(row_mean(center * center) + EPSILON)
    return (center * inverse, inverse)


def norm_back(grad, normed, inverse):
    return (grad - row_mean(grad) - normed * row_mean(grad * normed)) * inverse


def column_sum(values):
    return jnp.sum(values, axis=0, keepdims=True)


def params(*semantics):
    return pltpu.CompilerParams(dimension_semantics=semantics, vmem_limit_bytes=VMEM_LIMIT)


def project_kernel(x_ref, gain_ref, shift_ref, w_ref, o_ref):
    normed, _ = normalize(x_ref[...].astype(F32))
    normed = (normed * gain_ref[...] + shift_ref[...]).astype(BF16)
    o_ref[...] = dot(normed, w_ref[...]).astype(BF16)


def project(tokens, gain, shift, weight):
    count, width = tokens.shape
    columns = weight.shape[1]
    block = 512
    return pl.pallas_call(
        project_kernel,
        out_shape=jax.ShapeDtypeStruct((count, columns), BF16),
        grid=(count // block,),
        in_specs=[
            pl.BlockSpec((block, width), lambda i: (i, 0)),
            pl.BlockSpec((1, width), lambda i: (0, 0)),
            pl.BlockSpec((1, width), lambda i: (0, 0)),
            pl.BlockSpec((width, columns), lambda i: (0, 0)),
        ],
        out_specs=pl.BlockSpec((block, columns), lambda i: (i, 0)),
        compiler_params=params("arbitrary"),
        name="project",
    )(tokens, gain, shift, weight)


def label_of(position, start_ref, length_ref, seq, pieces):
    label = jnp.zeros(position.shape, jnp.int32)
    for piece in range(pieces):
        start = start_ref[seq, piece]
        inside = (position >= start) & (position < start + length_ref[seq, piece])
        label = jnp.where(inside, piece + 1, label)
    return label


def key_count(first_row, slot):
    return (first_row // slot + 1) * slot


def block_masks(start_ref, length_ref, seq, pieces, first_row, keys):
    query_pos = first_row + lax.broadcasted_iota(jnp.int32, (ROWS, 1), 0)
    key_pos = lax.broadcasted_iota(jnp.int32, (1, keys), 1)
    query_label = label_of(query_pos, start_ref, length_ref, seq, pieces)
    key_label = label_of(key_pos, start_ref, length_ref, seq, pieces)
    query_label = jnp.where(query_label > 0, query_label, -1)
    allowed = (key_pos <= query_pos) | (query_label == key_label)
    chosen = allowed & (key_pos != 0) & (key_pos != query_pos)
    return (allowed, chosen)


def triangle_sum(triangle, values):
    upper = values.astype(BF16)
    rest = values - upper.astype(F32)
    middle = rest.astype(BF16)
    lower = (rest - middle.astype(F32)).astype(BF16)
    return dot(triangle, upper) + dot(triangle, middle) + dot(triangle, lower)


def head_mask(half):
    lane = lax.broadcasted_iota(jnp.int32, (1, PAIR), 1)
    return (lane >= HEAD_DIM) if half else (lane < HEAD_DIM)


def attend_kernel(
    slot, pieces, start_ref, length_ref, q_ref, k_ref, v_ref, o_ref, *rest
):
    att_refs, (bias_ref, prefix_ref) = rest[:-2], rest[-2:]
    seq = pl.program_id(0)
    length = q_ref.shape[0]
    zero = jnp.zeros((), BF16)

    @pl.when(pl.program_id(1) == 0)
    def _():
        prefix_ref[...] = jnp.zeros_like(prefix_ref)
        row = lax.broadcasted_iota(jnp.int32, (ROWS, ROWS), 0)
        col = lax.broadcasted_iota(jnp.int32, (ROWS, ROWS), 1)
        triangle = (col < row).astype(BF16)
        for first_row in range(0, length, ROWS):
            keys = key_count(first_row, slot)
            rows = pl.ds(first_row, ROWS)
            query = jnp.where(head_mask(0), q_ref[rows, :], zero)
            scores = dot_nt(query, k_ref[:keys, :]) * SCALE
            allowed, chosen = block_masks(start_ref, length_ref, seq, pieces, first_row, keys)
            selected = jnp.where(chosen & (scores > 0), scores, 0.0)
            penalty = prefix_ref[:, :keys] + triangle_sum(triangle, selected)
            bias_ref[rows, :keys] = jnp.where(allowed, -penalty, MASKED_VALUE)
            prefix_ref[:, :keys] += column_sum(selected)

    for first_row in range(0, length, ROWS):
        keys = key_count(first_row, slot)
        rows = pl.ds(first_row, ROWS)
        slot_rows = pl.ds(first_row % slot, ROWS)
        mixed = None
        for half in range(2):
            mask = head_mask(half)
            query = jnp.where(mask, q_ref[rows, :], zero) * jnp.asarray(SCALE, BF16)
            logits = dot_nt(query, k_ref[:keys, :]) + bias_ref[rows, :keys]
            largest = jnp.max(logits, axis=-1, keepdims=True)
            raised = jnp.exp(logits - largest)
            inverse = 1.0 / jnp.sum(raised, axis=-1, keepdims=True)
            attention = (raised * inverse).astype(BF16)
            att_refs[first_row // slot][half, slot_rows, :] = attention
            value = jnp.where(mask, v_ref[:keys, :], zero)
            part = dot(attention, value)
            mixed = part if mixed is None else mixed + part
        o_ref[rows, :] = mixed.astype(BF16)


def attend(projected, starts, lengths):
    sequences, pieces = starts.shape
    count, columns = projected.shape
    length = count // sequences
    slot = length // pieces
    width = columns // 3
    pairs = width // PAIR

    def part(which):
        return pl.BlockSpec((length, PAIR), lambda s, p, a, b: (s, which * pairs + p))

    att_shapes = [
        jax.ShapeDtypeStruct((sequences, 2 * pairs, slot, (i + 1) * slot), BF16)
        for i in range(pieces)
    ]
    att_specs = [
        pl.BlockSpec((None, 2, slot, (i + 1) * slot), lambda s, p, a, b: (s, p, 0, 0))
        for i in range(pieces)
    ]
    results = pl.pallas_call(
        functools.partial(attend_kernel, slot, pieces),
        out_shape=[jax.ShapeDtypeStruct((count, width), BF16)] + att_shapes,
        grid_spec=pltpu.PrefetchScalarGridSpec(
            num_scalar_prefetch=2,
            grid=(sequences, pairs),
            in_specs=[part(0), part(1), part(2)],
            out_specs=[pl.BlockSpec((length, PAIR), lambda s, p, a, b: (s, p))] + att_specs,
            scratch_shapes=[
                pltpu.VMEM((length, length), F32),
                pltpu.VMEM((1, length), F32),
            ],
        ),
        compiler_params=params("arbitrary", "arbitrary"),
        name="attend",
    )(starts, lengths, projected, projected, projected)
    return (results[0], results[1:])


def attend_back_kernel(
    slot, pieces, start_ref, length_ref, q_ref, k_ref, v_ref, gm_ref, o_ref, *rest
):
    att_refs = rest[:pieces]
    gq_ref, gk_ref, gv_ref, sum_ref, later_ref, dq_ref, dk_ref, dv_ref = rest[pieces:]
    seq, step = pl.program_id(0), pl.program_id(1)
    last = step == pl.num_programs(1) - 1
    length = q_ref.shape[0]
    zero = jnp.zeros((), BF16)
    scale = jnp.asarray(SCALE, BF16)

    @pl.when(step == 0)
    def _():
        sum_ref[...] = jnp.zeros_like(sum_ref)

    dk_ref[...] = jnp.zeros_like(dk_ref)
    dv_ref[...] = jnp.zeros_like(dv_ref)

    def head(half, first_head):
        mask = head_mask(half)
        if first_head:
            later_ref[...] = jnp.zeros_like(later_ref)
            row = lax.broadcasted_iota(jnp.int32, (ROWS, ROWS), 0)
            col = lax.broadcasted_iota(jnp.int32, (ROWS, ROWS), 1)
            triangle = (col > row).astype(BF16)
        for first_row in reversed(range(0, length, ROWS)):
            keys = key_count(first_row, slot)
            rows = pl.ds(first_row, ROWS)
            slot_rows = pl.ds(first_row % slot, ROWS)
            grad = jnp.where(mask, gm_ref[rows, :], zero)
            delta = jnp.sum(
                grad.astype(F32) * o_ref[rows, :].astype(F32), axis=-1, keepdims=True
            )
            attention = att_refs[first_row // slot][half, slot_rows, :]
            grad_attention = dot_nt(grad, v_ref[:keys, :])
            grad_logits = attention.astype(F32) * (grad_attention - delta)
            query = jnp.where(mask, q_ref[rows, :], zero) * scale
            if first_head:
                total = sum_ref[rows, :keys] + grad_logits
                grad_selected = -(later_ref[:, :keys] + triangle_sum(triangle, total))
                later_ref[:, :keys] += column_sum(total)
                _, chosen = block_masks(start_ref, length_ref, seq, pieces, first_row, keys)
                positive = dot_nt(query, k_ref[:keys, :]) > 0
                grad_logits = grad_logits + jnp.where(chosen & positive, grad_selected, 0.0)
            else:
                sum_ref[rows, :keys] += grad_logits
            grad_scores = grad_logits.astype(BF16)
            key = jnp.where(mask, k_ref[:keys, :], zero) * scale
            part = dot(grad_scores, key)
            if half == 1:
                dq_ref[rows, :] = part
            else:
                dq_ref[rows, :] += part
            dk_ref[:keys, :] += dot_tn(grad_scores, query)
            dv_ref[:keys, :] += dot_tn(attention, grad)

    head(1, False)

    @pl.when(jnp.logical_not(last))
    def _():
        head(0, False)

    @pl.when(last)
    def _():
        head(0, True)

    gq_ref[...] = dq_ref[...].astype(BF16)
    gk_ref[...] = dk_ref[...].astype(BF16)
    gv_ref[...] = dv_ref[...].astype(BF16)


def attend_back(projected, starts, lengths, grad_mixed, mixed, attention):
    sequences, pieces = starts.shape
    count, columns = projected.shape
    length = count // sequences
    slot = length // pieces
    width = columns // 3
    pairs = width // PAIR

    def part(which):
        return pl.BlockSpec(
            (length, PAIR), lambda s, p, a, b: (s, which * pairs + pairs - 1 - p)
        )

    att_specs = [
        pl.BlockSpec(
            (None, 2, slot, (i + 1) * slot), lambda s, p, a, b: (s, pairs - 1 - p, 0, 0)
        )
        for i in range(pieces)
    ]
    return pl.pallas_call(
        functools.partial(attend_back_kernel, slot, pieces),
        out_shape=[jax.ShapeDtypeStruct((count, width), BF16)] * 3,
        grid_spec=pltpu.PrefetchScalarGridSpec(
            num_scalar_prefetch=2,
            grid=(sequences, pairs),
            in_specs=[part(0), part(1), part(2), part(0), part(0)] + att_specs,
            out_specs=[part(0), part(0), part(0)],
            scratch_shapes=[
                pltpu.VMEM((length, length), F32),
                pltpu.VMEM((1, length), F32),
                pltpu.VMEM((length, PAIR), F32),
                pltpu.VMEM((length, PAIR), F32),
                pltpu.VMEM((length, PAIR), F32),
            ],
        ),
        compiler_params=params("arbitrary", "arbitrary"),
        name="attend_back",
    )(starts, lengths, projected, projected, projected, grad_mixed, mixed, *attention)


def gelu_and_slope(values):
    square = values * values
    inner = GELU_IN * values * (1.0 + GELU_CUBE * square)
    bent = jnp.tanh(inner)
    half = 0.5 * (1.0 + bent)
    slope = half + 0.5 * values * (1.0 - bent * bent) * (
        GELU_IN * (1.0 + 3.0 * GELU_CUBE * square)
    )
    return (values * half, slope)


def feed_kernel(
    chunk,
    x_ref,
    mixed_ref,
    cot_ref,
    gain_ref,
    shift_ref,
    up_bias_ref,
    down_bias_ref,
    wo_hbm,
    wu_hbm,
    wd_hbm,
    out_ref,
    gmid_ref,
    gmix_ref,
    small_ref,
    gwo_hbm,
    gwu_hbm,
    gwd_hbm,
    wo_ref,
    wu_ref,
    wd_ref,
    gwo_ref,
    gwu_ref,
    gwd_ref,
    acc_ref,
    gnorm_ref,
    n2_ref,
    mid_ref,
    stage_ref,
    load_sem,
    stage_sem,
):
    step = pl.program_id(0)
    steps = pl.num_programs(0)
    chunks = wu_ref.shape[0]
    width = x_ref.shape[1]

    def load_out():
        return pltpu.make_async_copy(wo_hbm, wo_ref, load_sem.at[0])

    def load_up(c):
        return pltpu.make_async_copy(
            wu_hbm.at[:, pl.ds(c * chunk, chunk)], wu_ref.at[c], load_sem.at[1]
        )

    def load_down(c):
        return pltpu.make_async_copy(
            wd_hbm.at[pl.ds(c * chunk, chunk), :], wd_ref.at[c], load_sem.at[2]
        )

    @pl.when(step == 0)
    def _():
        load_out().start()
        for c in range(chunks):
            load_up(c).start()
        for c in range(chunks):
            load_down(c).start()
        gwo_ref[...] = jnp.zeros_like(gwo_ref)
        gwu_ref[...] = jnp.zeros_like(gwu_ref)
        gwd_ref[...] = jnp.zeros_like(gwd_ref)
        small_ref[...] = jnp.zeros_like(small_ref)
        load_out().wait()

    mid_ref[...] = x_ref[...].astype(F32) + dot(mixed_ref[...], wo_ref[...])

    @pl.when(step == 0)
    def _():
        for c in range(chunks):
            load_up(c).wait()
        for c in range(chunks):
            load_down(c).wait()

    normed, _ = normalize(mid_ref[...])
    n2_ref[...] = (normed * gain_ref[...] + shift_ref[...]).astype(BF16)
    acc_ref[...] = jnp.zeros_like(acc_ref)
    gnorm_ref[...] = jnp.zeros_like(gnorm_ref)

    def one_chunk(c, carry):
        before = dot(n2_ref[...], wu_ref[c]) + up_bias_ref[c]
        hidden, slope = gelu_and_slope(before)
        hidden = hidden.astype(BF16)
        acc_ref[...] += dot(hidden, wd_ref[c])
        gwd_ref[c] += dot_tn(hidden, cot_ref[...])
        grad_hidden = dot_nt(cot_ref[...], wd_ref[c]).astype(BF16)
        grad_before = (grad_hidden.astype(F32) * slope).astype(BF16)
        small_ref[3 + c] += column_sum(grad_before.astype(F32))
        gnorm_ref[...] += dot_nt(grad_before, wu_ref[c])
        gwu_ref[c] += dot_tn(n2_ref[...], grad_before)
        return carry

    lax.fori_loop(0, chunks, one_chunk, 0)

    out_ref[...] = (mid_ref[...] + (acc_ref[...] + down_bias_ref[...])).astype(BF16)
    grad_normed = gnorm_ref[...]
    normed, inverse = normalize(mid_ref[...])
    cot = cot_ref[...].astype(F32)
    small_ref[0] += column_sum(grad_normed * normed)
    small_ref[1] += column_sum(grad_normed)
    small_ref[2] += column_sum(cot)
    grad_middle = cot + norm_back(grad_normed * gain_ref[...], normed, inverse)
    gmid_ref[...] = grad_middle
    grad_proj = grad_middle.astype(BF16)
    gwo_ref[...] += dot_tn(mixed_ref[...], grad_proj)
    gmix_ref[...] = dot_nt(grad_proj, wo_ref[...]).astype(BF16)

    @pl.when(step == steps - 1)
    def _():
        copies = []

        def put(value, target):
            i = len(copies)
            if i >= 2:
                copies[i - 2].wait()
            stage_ref[i % 2] = value.astype(BF16)
            copy = pltpu.make_async_copy(stage_ref.at[i % 2], target, stage_sem.at[i % 2])
            copy.start()
            copies.append(copy)

        put(gwo_ref[...], gwo_hbm)
        for c in range(chunks):
            put(gwu_ref[c], gwu_hbm.at[:, pl.ds(c * chunk, chunk)])
            put(gwd_ref[c], gwd_hbm.at[pl.ds(c * chunk, chunk), :])
        copies[-2].wait()
        copies[-1].wait()


def feed(tokens, mixed, cotangent, gain, shift, up_bias, down_bias, wo, wu, wd):
    count, width = tokens.shape
    hidden = wu.shape[1]
    block = 512
    chunk = width
    chunks = hidden // chunk
    rows = pl.BlockSpec((block, width), lambda i: (i, 0))
    line = pl.BlockSpec((1, width), lambda i: (0, 0))
    anywhere = pl.BlockSpec(memory_space=pl.ANY)
    return pl.pallas_call(
        functools.partial(feed_kernel, chunk),
        out_shape=[
            jax.ShapeDtypeStruct((count, width), BF16),
            jax.ShapeDtypeStruct((count, width), F32),
            jax.ShapeDtypeStruct((count, width), BF16),
            jax.ShapeDtypeStruct((3 + chunks, 1, width), F32),
            jax.ShapeDtypeStruct(wo.shape, BF16),
            jax.ShapeDtypeStruct(wu.shape, BF16),
            jax.ShapeDtypeStruct(wd.shape, BF16),
        ],
        grid=(count // block,),
        in_specs=[
            rows,
            rows,
            rows,
            line,
            line,
            pl.BlockSpec((chunks, 1, chunk), lambda i: (0, 0, 0)),
            line,
            anywhere,
            anywhere,
            anywhere,
        ],
        out_specs=[
            rows,
            rows,
            rows,
            pl.BlockSpec((3 + chunks, 1, width), lambda i: (0, 0, 0)),
            anywhere,
            anywhere,
            anywhere,
        ],
        scratch_shapes=[
            pltpu.VMEM(wo.shape, BF16),
            pltpu.VMEM((chunks, width, chunk), BF16),
            pltpu.VMEM((chunks, chunk, width), BF16),
            pltpu.VMEM(wo.shape, F32),
            pltpu.VMEM((chunks, width, chunk), F32),
            pltpu.VMEM((chunks, chunk, width), F32),
            pltpu.VMEM((block, width), F32),
            pltpu.VMEM((block, width), F32),
            pltpu.VMEM((block, width), BF16),
            pltpu.VMEM((block, width), F32),
            pltpu.VMEM((2, width, chunk), BF16),
            pltpu.SemaphoreType.DMA((3,)),
            pltpu.SemaphoreType.DMA((2,)),
        ],
        compiler_params=params("arbitrary"),
        name="feed",
    )(
        tokens,
        mixed,
        cotangent,
        gain,
        shift,
        up_bias.reshape(chunks, 1, chunk),
        down_bias,
        wo,
        wu,
        wd,
    )


def input_kernel(
    x_ref,
    gmid_ref,
    gq_ref,
    gk_ref,
    gv_ref,
    gain_ref,
    shift_ref,
    w_ref,
    gx_ref,
    small_ref,
    gw_ref,
    acc_ref,
):
    step = pl.program_id(0)
    width = x_ref.shape[1]

    @pl.when(step == 0)
    def _():
        acc_ref[...] = jnp.zeros_like(acc_ref)
        small_ref[...] = jnp.zeros_like(small_ref)

    normed, inverse = normalize(x_ref[...].astype(F32))
    low = (normed * gain_ref[...] + shift_ref[...]).astype(BF16)
    grad_normed = None
    for which, ref in enumerate((gq_ref, gk_ref, gv_ref)):
        grad = ref[...]
        acc_ref[which] += dot_tn(low, grad)
        part = dot_nt(grad, w_ref[:, which * width : (which + 1) * width])
        grad_normed = part if grad_normed is None else grad_normed + part
    small_ref[0] += column_sum(grad_normed * normed)
    small_ref[1] += column_sum(grad_normed)
    gx_ref[...] = gmid_ref[...] + norm_back(grad_normed * gain_ref[...], normed, inverse)

    @pl.when(step == pl.num_programs(0) - 1)
    def _():
        for which in range(3):
            gw_ref[:, which * width : (which + 1) * width] = acc_ref[which].astype(BF16)


def input_back(tokens, grad_middle, grads, gain, shift, weight):
    count, width = tokens.shape
    block = 512
    rows = pl.BlockSpec((block, width), lambda i: (i, 0))
    line = pl.BlockSpec((1, width), lambda i: (0, 0))
    return pl.pallas_call(
        input_kernel,
        out_shape=[
            jax.ShapeDtypeStruct((count, width), F32),
            jax.ShapeDtypeStruct((2, 1, width), F32),
            jax.ShapeDtypeStruct(weight.shape, BF16),
        ],
        grid=(count // block,),
        in_specs=[rows] * 5 + [line, line, pl.BlockSpec(weight.shape, lambda i: (0, 0))],
        out_specs=[
            rows,
            pl.BlockSpec((2, 1, width), lambda i: (0, 0, 0)),
            pl.BlockSpec(weight.shape, lambda i: (0, 0)),
        ],
        scratch_shapes=[pltpu.VMEM((3, width, width), F32)],
        compiler_params=params("arbitrary"),
        name="input_back",
    )(tokens, grad_middle, *grads, gain, shift, weight)


def gather(value):
    return lax.all_gather(value, "fsdp", axis=0, tiled=True)


def local(
    tokens,
    piece_start,
    piece_length,
    query_key_value,
    output_weight,
    up_weight,
    down_weight,
    first_gain,
    first_shift,
    second_gain,
    second_shift,
    up_bias,
    down_bias,
    cotangent,
):
    width = tokens.shape[1]
    vectors = (first_gain, first_shift, second_gain, second_shift, up_bias, down_bias)
    sizes = [v.shape[0] for v in vectors]
    total = sum(sizes)
    padded = -(-total // 1024) * 1024
    flat = jnp.pad(jnp.concatenate(vectors), (0, padded - total)).reshape(1, 8, padded // 8)
    flat = gather(flat).reshape(-1, padded)
    vectors, at = ([], 0)
    for size in sizes:
        vectors.append(flat[:, at : at + size].reshape(1, -1))
        at += size
    gain1, shift1, gain2, shift2, up_bias, down_bias = (v.astype(F32) for v in vectors)

    wqkv = gather(query_key_value)
    wo = gather(output_weight)
    wu = gather(up_weight)
    wd = gather(down_weight)

    projected = project(tokens, gain1, shift1, wqkv)
    mixed, attention = attend(projected, piece_start, piece_length)
    block_output, grad_middle, grad_mixed, small2, gwo, gwu, gwd = feed(
        tokens, mixed, cotangent, gain2, shift2, up_bias, down_bias, wo, wu, wd
    )
    grads = attend_back(projected, piece_start, piece_length, grad_mixed, mixed, attention)
    grad_tokens, small1, gwqkv = input_back(tokens, grad_middle, grads, gain1, shift1, wqkv)

    devices = lax.axis_size("fsdp")
    small = jnp.concatenate([small1.reshape(-1, width), small2.reshape(-1, width)], axis=0)

    def scatter(value):
        return lax.psum_scatter(value, "fsdp", scatter_dimension=0, tiled=True)

    def across(value):
        return lax.psum(value, "rep").astype(F32)

    small = small.astype(BF16)
    hidden = up_bias.shape[1]
    order = [small[0], small[1], small[2], small[3], small[5:].reshape(-1), small[4]]
    packed = jnp.concatenate([v.reshape(devices, -1) for v in order], axis=1)
    packed = jnp.pad(packed, ((0, 0), (0, padded - total))).reshape(devices * 8, padded // 8)
    packed = across(scatter(packed)).reshape(-1)
    tails, at = ([], 0)
    for size in sizes:
        tails.append(packed[at : at + size])
        at += size
    gfg, gfs, gsg, gss, gub, gdb = tails
    return (
        block_output,
        grad_tokens,
        across(scatter(gwqkv)),
        across(scatter(gwo)),
        across(scatter(gwu)),
        across(scatter(gwd)),
        gfg,
        gfs,
        gsg,
        gss,
        gub,
        gdb,
    )


def solution(mesh):
    rows = P(("fsdp", "rep"), None)
    matrix = P("fsdp", None)
    vector = P("fsdp")
    return jax.shard_map(
        local,
        mesh=mesh,
        in_specs=(rows,) * 3 + (matrix,) * 4 + (vector,) * 6 + (rows,),
        out_specs=(rows,) * 2 + (matrix,) * 4 + (vector,) * 6,
        check_vma=False,
    )
```

```python
import functools

import jax
import jax.numpy as jnp
from jax import lax
from jax.experimental import pallas as pl
from jax.experimental.pallas import tpu as pltpu
from jax.sharding import PartitionSpec as P

HEAD_DIM = 64
PAIR = 2 * HEAD_DIM
ROWS = 256
MASKED_VALUE = -1e30
EPSILON = 1e-05
SCALE = HEAD_DIM**-0.5
GAIN1, SHIFT1, GAIN2, SHIFT2, DOWN_BIAS = (4, 5, 6, 7, 8)
LINES = 16
GELU_IN = 0.7978845608028654
GELU_CUBE = 0.044715
VMEM_LIMIT = 60 * 1024 * 1024

F32 = jnp.float32
BF16 = jnp.bfloat16


def dot(left, right):
    return lax.dot_general(left, right, (((1,), (0,)), ((), ())), preferred_element_type=F32)


def dot_nt(left, right):
    return lax.dot_general(left, right, (((1,), (1,)), ((), ())), preferred_element_type=F32)


def dot_tn(left, right):
    return lax.dot_general(left, right, (((0,), (0,)), ((), ())), preferred_element_type=F32)


def row_mean(values):
    return jnp.mean(values, axis=-1, keepdims=True)


def normalize(values):
    center = values - row_mean(values)
    inverse = lax.rsqrt(row_mean(center * center) + EPSILON)
    return (center * inverse, inverse)


def norm_back(grad, normed, inverse):
    return (grad - row_mean(grad) - normed * row_mean(grad * normed)) * inverse


def column_sum(values):
    return jnp.sum(values, axis=0, keepdims=True)


def params(*semantics):
    return pltpu.CompilerParams(dimension_semantics=semantics, vmem_limit_bytes=VMEM_LIMIT)


def comm_params(number, *semantics):
    return pltpu.CompilerParams(
        dimension_semantics=semantics,
        vmem_limit_bytes=VMEM_LIMIT,
        collective_id=number,
        has_side_effects=True,
    )


MESH = pl.DeviceIdType.MESH
LEVELS = 4
CORES = 2


class Place:
    def __init__(self, count, copies):
        self.count, self.copies = (count, copies)
        self.columns = count // (LEVELS * CORES)
        self.index = lax.axis_index("fsdp")
        self.rep = lax.axis_index("rep")
        self.core = lax.rem(self.index, CORES)
        chip = lax.div(self.index, CORES)
        self.column = lax.rem(chip, self.columns)
        self.level = lax.div(chip, self.columns)
        self.half = lax.rem(self.rep, 2)

    def block(self, up=0, across=0, other=0):
        level = lax.rem(self.level + (up + LEVELS), LEVELS)
        column = lax.rem(self.column + (across + self.columns), self.columns)
        core = lax.rem(self.core + other, CORES)
        return (level * self.columns + column) * CORES + core

    def device(self, up=0, across=0, other=0, copy=0):
        return (self.block(up, across, other), lax.rem(self.rep + copy, self.copies))

    def twin(self):
        return (self.index, self.rep + 1 - 2 * self.half)

    def meet(self, twin=False, copies=False):
        others = [self.device(up=up) for up in range(1, LEVELS)]
        others += [self.device(across=across) for across in range(1, self.columns)]
        others += [self.device(other=1)]
        if twin:
            others += [self.twin()]
        if copies:
            others += [self.device(copy=copy) for copy in range(1, self.copies)]
        barrier = pltpu.get_barrier_semaphore()
        for other in others:
            pl.semaphore_signal(barrier, inc=1, device_id=other, device_id_type=MESH)
        pl.semaphore_wait(barrier, len(others))


def send(source, target, sems, slot, device):
    return pltpu.make_async_remote_copy(
        src_ref=source,
        dst_ref=target,
        send_sem=sems.at[2 * slot],
        recv_sem=sems.at[2 * slot + 1],
        device_id=device,
        device_id_type=MESH,
    )


def gather_sems(count):
    return 2 * (LEVELS - 1 + 3 * count // CORES) + 1


class Gather:
    def __init__(self, place, source, target, rows, shared, sems):
        self.place, self.source, self.target = (place, source, target)
        self.sems, self.shared = (sems, shared)
        if shared:
            third = rows // 3
            half = place.half
            self.part = pl.ds(pl.multiple_of(half * third, third), 2 * third)
            self.give = pl.ds(pl.multiple_of(half * (2 * third), third), third)
        else:
            self.part = pl.ds(0, rows)

    def held(self, up, across):
        if up == 0 and across == 0:
            return self.source
        return self.target(self.place.block(-up, -across))

    def slot(self, phase, up, across):
        area = self.place.count // CORES
        return LEVELS - 1 + phase * area + across * LEVELS + up

    def level_copies(self):
        target = self.target(self.place.block()).at[self.part, :]
        source = self.source.at[self.part, :]
        return [
            send(source, target, self.sems, up - 1, self.place.device(up=up))
            for up in range(1, LEVELS)
        ]

    def column_copies(self, ups):
        place = self.place
        return [
            send(
                self.held(up, 0).at[self.part, :],
                self.target(place.block(-up)).at[self.part, :],
                self.sems,
                self.slot(0, up, across),
                place.device(across=across),
            )
            for up in ups
            for across in range(1, place.columns)
        ]

    def twin_copies(self, acrosses):
        if not self.shared:
            return []
        place = self.place
        return [
            send(
                self.held(up, across).at[self.give, :],
                self.target(place.block(-up, -across)).at[self.give, :],
                self.sems,
                self.slot(1, up, across),
                place.twin(),
            )
            for across in acrosses
            for up in range(LEVELS)
            if up or across
        ]

    def core_copies(self, first):
        place = self.place
        return [
            send(
                self.held(up, across),
                self.target(place.block(-up, -across)),
                self.sems,
                self.slot(2, up, across),
                place.device(other=1),
            )
            for across in range(place.columns)
            for up in range(LEVELS)
            if (up == 0 and across == 0) == first
        ]

    def own(self):
        last = gather_sems(self.place.count) - 1
        return pltpu.make_async_copy(
            self.source, self.target(self.place.block()), self.sems.at[last]
        )

    def start(self):
        for copy in self.level_copies() + self.column_copies([0]) + self.core_copies(True):
            copy.start()
        self.own().start()

    def after_levels(self):
        for copy in self.level_copies():
            copy.wait_recv()
        for copy in self.column_copies(range(1, LEVELS)) + self.twin_copies([0]):
            copy.start()

    def after_columns(self):
        for copy in self.column_copies(range(LEVELS)):
            copy.wait_recv()
        for copy in self.twin_copies(range(1, self.place.columns)):
            copy.start()
        if not self.shared:
            self.to_cores()

    def after_twins(self):
        for copy in self.twin_copies(range(self.place.columns)):
            copy.wait_recv()
        if self.shared:
            self.to_cores()

    def to_cores(self):
        for copy in self.core_copies(False):
            copy.start()

    def finish(self):
        for copy in self.core_copies(True) + self.core_copies(False):
            copy.wait_recv()
        self.own().wait()

    def drain(self):
        columns = range(self.place.columns)
        copies = self.level_copies() + self.column_copies(range(LEVELS))
        copies += self.twin_copies(columns) + self.core_copies(True) + self.core_copies(False)
        for copy in copies:
            copy.wait_send()


def project_kernel(
    count,
    copies,
    x_ref,
    w_hbm,
    vec_hbm,
    o_ref,
    full_hbm,
    vec_ref,
    n1_ref,
    w_ref,
    all_ref,
    sems,
    load_sem,
):
    step = pl.program_id(0)
    width = x_ref.shape[1]
    rows = w_hbm.shape[0]
    lines = vec_hbm.shape[0]
    place = Place(count, copies)
    pieces = [
        Gather(
            place,
            vec_hbm,
            lambda block: all_ref.at[pl.ds(pl.multiple_of(block * lines, lines), lines), :],
            lines,
            False,
            sems.at[0],
        )
    ]
    for which in range(3):
        columns = pl.ds(which * width, width)

        def target(block, columns=columns):
            return full_hbm.at[pl.ds(pl.multiple_of(block * rows, rows), rows), columns]

        pieces.append(
            Gather(place, w_hbm.at[:, columns], target, rows, False, sems.at[1 + which])
        )

    def multiply(which):
        pieces[1 + which].finish()
        copy = pltpu.make_async_copy(
            full_hbm.at[:, pl.ds(which * width, width)], w_ref, load_sem
        )
        copy.start()
        copy.wait()
        o_ref[...] = dot(n1_ref[...], w_ref[...]).astype(BF16)

    @pl.when(step == 0)
    def _():
        place.meet()
        for piece in pieces:
            piece.start()
        pieces[0].after_levels()
        pieces[0].after_columns()
        pieces[1].after_levels()
        pieces[0].finish()
        vectors = all_ref[0:lines, :].astype(F32)
        for other in range(1, count):
            vectors = vectors + all_ref[other * lines : (other + 1) * lines, :].astype(F32)
        for line in range(lines):
            vec_ref[line] = vectors[line : line + 1, :]
        total = x_ref.shape[0]
        gain, shift = (vec_ref[GAIN1], vec_ref[SHIFT1])
        block = 256

        def norm_rows(i, carry):
            at = pl.ds(pl.multiple_of(i * block, block), block)
            normed, _ = normalize(x_ref[at, :].astype(F32))
            n1_ref[at, :] = (normed * gain + shift).astype(BF16)
            return carry

        lax.fori_loop(0, total // block, norm_rows, 0)
        pieces[1].after_columns()
        pieces[2].after_levels()
        pieces[2].after_columns()
        multiply(0)

    @pl.when(step == 1)
    def _():
        pieces[3].after_levels()
        pieces[3].after_columns()
        multiply(1)

    @pl.when(step == 2)
    def _():
        multiply(2)
        for piece in pieces:
            piece.drain()


def project(tokens, weight, vectors, count, copies):
    total, width = tokens.shape
    rows, columns = weight.shape
    lines = vectors.shape[0]
    anywhere = pl.BlockSpec(memory_space=pl.ANY)
    return pl.pallas_call(
        functools.partial(project_kernel, count, copies),
        out_shape=[
            jax.ShapeDtypeStruct((total, columns), BF16),
            jax.ShapeDtypeStruct((rows * count, columns), BF16),
            jax.ShapeDtypeStruct((lines, 1, width), F32),
        ],
        grid=(3,),
        in_specs=[pl.BlockSpec((total, width), lambda i: (0, 0)), anywhere, anywhere],
        out_specs=[
            pl.BlockSpec((total, width), lambda i: (0, i)),
            anywhere,
            pl.BlockSpec((lines, 1, width), lambda i: (0, 0, 0)),
        ],
        scratch_shapes=[
            pltpu.VMEM((total, width), BF16),
            pltpu.VMEM((width, width), BF16),
            pltpu.VMEM((count * lines, width), BF16),
            pltpu.SemaphoreType.DMA((4, gather_sems(count))),
            pltpu.SemaphoreType.DMA,
        ],
        compiler_params=comm_params(0, "arbitrary"),
        name="project",
    )(tokens, weight, vectors)


def label_of(position, start_ref, length_ref, seq, pieces):
    label = jnp.zeros(position.shape, jnp.int32)
    for piece in range(pieces):
        start = start_ref[seq, piece]
        inside = (position >= start) & (position < start + length_ref[seq, piece])
        label = jnp.where(inside, piece + 1, label)
    return label


def key_count(first_row, slot):
    return (first_row // slot + 1) * slot


def block_masks(start_ref, length_ref, seq, pieces, first_row, keys):
    query_pos = first_row + lax.broadcasted_iota(jnp.int32, (ROWS, 1), 0)
    key_pos = lax.broadcasted_iota(jnp.int32, (1, keys), 1)
    query_label = label_of(query_pos, start_ref, length_ref, seq, pieces)
    key_label = label_of(key_pos, start_ref, length_ref, seq, pieces)
    query_label = jnp.where(query_label > 0, query_label, -1)
    allowed = (key_pos <= query_pos) | (query_label == key_label)
    chosen = allowed & (key_pos != 0) & (key_pos != query_pos)
    return (allowed, chosen)


def triangle_sum(triangle, values):
    upper = values.astype(BF16)
    rest = values - upper.astype(F32)
    middle = rest.astype(BF16)
    lower = (rest - middle.astype(F32)).astype(BF16)
    return dot(triangle, upper) + dot(triangle, middle) + dot(triangle, lower)


def head_mask(half):
    lane = lax.broadcasted_iota(jnp.int32, (1, PAIR), 1)
    return (lane >= HEAD_DIM) if half else (lane < HEAD_DIM)


def attend_kernel(
    slot, pieces, start_ref, length_ref, q_ref, k_ref, v_ref, o_ref, *rest
):
    att_refs, (bias_ref, prefix_ref) = rest[:-2], rest[-2:]
    seq = pl.program_id(0)
    length = q_ref.shape[0]
    zero = jnp.zeros((), BF16)

    @pl.when(pl.program_id(1) == 0)
    def _():
        prefix_ref[...] = jnp.zeros_like(prefix_ref)
        row = lax.broadcasted_iota(jnp.int32, (ROWS, ROWS), 0)
        col = lax.broadcasted_iota(jnp.int32, (ROWS, ROWS), 1)
        triangle = (col < row).astype(BF16)
        for first_row in range(0, length, ROWS):
            keys = key_count(first_row, slot)
            rows = pl.ds(first_row, ROWS)
            query = jnp.where(head_mask(0), q_ref[rows, :], zero)
            scores = dot_nt(query, k_ref[:keys, :]) * SCALE
            allowed, chosen = block_masks(start_ref, length_ref, seq, pieces, first_row, keys)
            selected = jnp.where(chosen & (scores > 0), scores, 0.0)
            penalty = prefix_ref[:, :keys] + triangle_sum(triangle, selected)
            bias_ref[rows, :keys] = jnp.where(allowed, -penalty, MASKED_VALUE)
            prefix_ref[:, :keys] += column_sum(selected)

    for first_row in range(0, length, ROWS):
        keys = key_count(first_row, slot)
        rows = pl.ds(first_row, ROWS)
        slot_rows = pl.ds(first_row % slot, ROWS)
        mixed = None
        for half in range(2):
            mask = head_mask(half)
            query = jnp.where(mask, q_ref[rows, :], zero) * jnp.asarray(SCALE, BF16)
            logits = dot_nt(query, k_ref[:keys, :]) + bias_ref[rows, :keys]
            largest = jnp.max(logits, axis=-1, keepdims=True)
            raised = jnp.exp(logits - largest)
            inverse = 1.0 / jnp.sum(raised, axis=-1, keepdims=True)
            attention = (raised * inverse).astype(BF16)
            att_refs[first_row // slot][half, slot_rows, :] = attention
            value = jnp.where(mask, v_ref[:keys, :], zero)
            part = dot(attention, value)
            mixed = part if mixed is None else mixed + part
        o_ref[rows, :] = mixed.astype(BF16)


def attend(projected, starts, lengths):
    sequences, pieces = starts.shape
    count, columns = projected.shape
    length = count // sequences
    slot = length // pieces
    width = columns // 3
    pairs = width // PAIR

    def part(which):
        return pl.BlockSpec((length, PAIR), lambda s, p, a, b: (s, which * pairs + p))

    att_shapes = [
        jax.ShapeDtypeStruct((sequences, 2 * pairs, slot, (i + 1) * slot), BF16)
        for i in range(pieces)
    ]
    att_specs = [
        pl.BlockSpec((None, 2, slot, (i + 1) * slot), lambda s, p, a, b: (s, p, 0, 0))
        for i in range(pieces)
    ]
    results = pl.pallas_call(
        functools.partial(attend_kernel, slot, pieces),
        out_shape=[jax.ShapeDtypeStruct((count, width), BF16)] + att_shapes,
        grid_spec=pltpu.PrefetchScalarGridSpec(
            num_scalar_prefetch=2,
            grid=(sequences, pairs),
            in_specs=[part(0), part(1), part(2)],
            out_specs=[pl.BlockSpec((length, PAIR), lambda s, p, a, b: (s, p))] + att_specs,
            scratch_shapes=[
                pltpu.VMEM((length, length), F32),
                pltpu.VMEM((1, length), F32),
            ],
        ),
        compiler_params=params("arbitrary", "arbitrary"),
        name="attend",
    )(starts, lengths, projected, projected, projected)
    return (results[0], results[1:])


def attend_back_kernel(
    slot, pieces, start_ref, length_ref, q_ref, k_ref, v_ref, gm_ref, o_ref, *rest
):
    att_refs = rest[:pieces]
    gq_ref, gk_ref, gv_ref, sum_ref, later_ref, dq_ref, dk_ref, dv_ref = rest[pieces:]
    seq, step = pl.program_id(0), pl.program_id(1)
    last = step == pl.num_programs(1) - 1
    length = q_ref.shape[0]
    zero = jnp.zeros((), BF16)
    scale = jnp.asarray(SCALE, BF16)

    @pl.when(step == 0)
    def _():
        sum_ref[...] = jnp.zeros_like(sum_ref)

    dk_ref[...] = jnp.zeros_like(dk_ref)
    dv_ref[...] = jnp.zeros_like(dv_ref)

    def head(half, first_head):
        mask = head_mask(half)
        if first_head:
            later_ref[...] = jnp.zeros_like(later_ref)
            row = lax.broadcasted_iota(jnp.int32, (ROWS, ROWS), 0)
            col = lax.broadcasted_iota(jnp.int32, (ROWS, ROWS), 1)
            triangle = (col > row).astype(BF16)
        for first_row in reversed(range(0, length, ROWS)):
            keys = key_count(first_row, slot)
            rows = pl.ds(first_row, ROWS)
            slot_rows = pl.ds(first_row % slot, ROWS)
            grad = jnp.where(mask, gm_ref[rows, :], zero)
            delta = jnp.sum(
                grad.astype(F32) * o_ref[rows, :].astype(F32), axis=-1, keepdims=True
            )
            attention = att_refs[first_row // slot][half, slot_rows, :]
            grad_attention = dot_nt(grad, v_ref[:keys, :])
            grad_logits = attention.astype(F32) * (grad_attention - delta)
            query = jnp.where(mask, q_ref[rows, :], zero) * scale
            if first_head:
                total = sum_ref[rows, :keys] + grad_logits
                grad_selected = -(later_ref[:, :keys] + triangle_sum(triangle, total))
                later_ref[:, :keys] += column_sum(total)
                _, chosen = block_masks(start_ref, length_ref, seq, pieces, first_row, keys)
                positive = dot_nt(query, k_ref[:keys, :]) > 0
                grad_logits = grad_logits + jnp.where(chosen & positive, grad_selected, 0.0)
            else:
                sum_ref[rows, :keys] += grad_logits
            grad_scores = grad_logits.astype(BF16)
            key = jnp.where(mask, k_ref[:keys, :], zero) * scale
            part = dot(grad_scores, key)
            if half == 1:
                dq_ref[rows, :] = part
            else:
                dq_ref[rows, :] += part
            dk_ref[:keys, :] += dot_tn(grad_scores, query)
            dv_ref[:keys, :] += dot_tn(attention, grad)

    head(1, False)

    @pl.when(jnp.logical_not(last))
    def _():
        head(0, False)

    @pl.when(last)
    def _():
        head(0, True)

    gq_ref[...] = dq_ref[...].astype(BF16)
    gk_ref[...] = dk_ref[...].astype(BF16)
    gv_ref[...] = dv_ref[...].astype(BF16)


def attend_back(projected, starts, lengths, grad_mixed, mixed, attention):
    sequences, pieces = starts.shape
    count, columns = projected.shape
    length = count // sequences
    slot = length // pieces
    width = columns // 3
    pairs = width // PAIR

    def part(which):
        return pl.BlockSpec(
            (length, PAIR), lambda s, p, a, b: (s, which * pairs + pairs - 1 - p)
        )

    att_specs = [
        pl.BlockSpec(
            (None, 2, slot, (i + 1) * slot), lambda s, p, a, b: (s, pairs - 1 - p, 0, 0)
        )
        for i in range(pieces)
    ]
    return pl.pallas_call(
        functools.partial(attend_back_kernel, slot, pieces),
        out_shape=[jax.ShapeDtypeStruct((count, width), BF16)] * 3,
        grid_spec=pltpu.PrefetchScalarGridSpec(
            num_scalar_prefetch=2,
            grid=(sequences, pairs),
            in_specs=[part(0), part(1), part(2), part(0), part(0)] + att_specs,
            out_specs=[part(0), part(0), part(0)],
            scratch_shapes=[
                pltpu.VMEM((length, length), F32),
                pltpu.VMEM((1, length), F32),
                pltpu.VMEM((length, PAIR), F32),
                pltpu.VMEM((length, PAIR), F32),
                pltpu.VMEM((length, PAIR), F32),
            ],
        ),
        compiler_params=params("arbitrary", "arbitrary"),
        name="attend_back",
    )(starts, lengths, projected, projected, projected, grad_mixed, mixed, *attention)


def gelu_and_slope(values):
    square = values * values
    inner = GELU_IN * values * (1.0 + GELU_CUBE * square)
    bent = jnp.tanh(inner)
    half = 0.5 * (1.0 + bent)
    slope = half + 0.5 * values * (1.0 - bent * bent) * (
        GELU_IN * (1.0 + 3.0 * GELU_CUBE * square)
    )
    return (values * half, slope)


def feed_kernel(
    chunk,
    x_ref,
    mixed_ref,
    cot_ref,
    gain_ref,
    shift_ref,
    up_bias_ref,
    down_bias_ref,
    wo_hbm,
    wu_hbm,
    wd_hbm,
    out_ref,
    gmid_ref,
    gmix_ref,
    small_ref,
    gwo_hbm,
    gwu_hbm,
    gwd_hbm,
    wo_ref,
    wu_ref,
    wd_ref,
    gwo_ref,
    gwu_ref,
    gwd_ref,
    acc_ref,
    gnorm_ref,
    n2_ref,
    mid_ref,
    stage_ref,
    load_sem,
    stage_sem,
):
    step = pl.program_id(0)
    steps = pl.num_programs(0)
    chunks = wu_ref.shape[0]
    width = x_ref.shape[1]

    def load_out():
        return pltpu.make_async_copy(wo_hbm, wo_ref, load_sem.at[0])

    def load_up(c):
        return pltpu.make_async_copy(
            wu_hbm.at[:, pl.ds(c * chunk, chunk)], wu_ref.at[c], load_sem.at[1]
        )

    def load_down(c):
        return pltpu.make_async_copy(
            wd_hbm.at[pl.ds(c * chunk, chunk), :], wd_ref.at[c], load_sem.at[2]
        )

    @pl.when(step == 0)
    def _():
        load_out().start()
        for c in range(chunks):
            load_up(c).start()
        for c in range(chunks):
            load_down(c).start()
        gwo_ref[...] = jnp.zeros_like(gwo_ref)
        gwu_ref[...] = jnp.zeros_like(gwu_ref)
        gwd_ref[...] = jnp.zeros_like(gwd_ref)
        small_ref[...] = jnp.zeros_like(small_ref)
        load_out().wait()

    mid_ref[...] = x_ref[...].astype(F32) + dot(mixed_ref[...], wo_ref[...])

    @pl.when(step == 0)
    def _():
        for c in range(chunks):
            load_up(c).wait()
        for c in range(chunks):
            load_down(c).wait()

    normed, _ = normalize(mid_ref[...])
    n2_ref[...] = (normed * gain_ref[...] + shift_ref[...]).astype(BF16)
    acc_ref[...] = jnp.zeros_like(acc_ref)
    gnorm_ref[...] = jnp.zeros_like(gnorm_ref)

    def one_chunk(c, carry):
        before = dot(n2_ref[...], wu_ref[c]) + up_bias_ref[c]
        hidden, slope = gelu_and_slope(before)
        hidden = hidden.astype(BF16)
        acc_ref[...] += dot(hidden, wd_ref[c])
        gwd_ref[c] += dot_tn(hidden, cot_ref[...])
        grad_hidden = dot_nt(cot_ref[...], wd_ref[c]).astype(BF16)
        grad_before = (grad_hidden.astype(F32) * slope).astype(BF16)
        small_ref[3 + c] += column_sum(grad_before.astype(F32))
        gnorm_ref[...] += dot_nt(grad_before, wu_ref[c])
        gwu_ref[c] += dot_tn(n2_ref[...], grad_before)
        return carry

    lax.fori_loop(0, chunks, one_chunk, 0)

    out_ref[...] = (mid_ref[...] + (acc_ref[...] + down_bias_ref[...])).astype(BF16)
    grad_normed = gnorm_ref[...]
    normed, inverse = normalize(mid_ref[...])
    cot = cot_ref[...].astype(F32)
    small_ref[0] += column_sum(grad_normed * normed)
    small_ref[1] += column_sum(grad_normed)
    small_ref[2] += column_sum(cot)
    grad_middle = cot + norm_back(grad_normed * gain_ref[...], normed, inverse)
    gmid_ref[...] = grad_middle
    grad_proj = grad_middle.astype(BF16)
    gwo_ref[...] += dot_tn(mixed_ref[...], grad_proj)
    gmix_ref[...] = dot_nt(grad_proj, wo_ref[...]).astype(BF16)

    @pl.when(step == steps - 1)
    def _():
        copies = []

        def put(value, target):
            i = len(copies)
            if i >= 2:
                copies[i - 2].wait()
            stage_ref[i % 2] = value.astype(BF16)
            copy = pltpu.make_async_copy(stage_ref.at[i % 2], target, stage_sem.at[i % 2])
            copy.start()
            copies.append(copy)

        put(gwo_ref[...], gwo_hbm)
        for c in range(chunks):
            put(gwu_ref[c], gwu_hbm.at[:, pl.ds(c * chunk, chunk)])
            put(gwd_ref[c], gwd_hbm.at[pl.ds(c * chunk, chunk), :])
        copies[-2].wait()
        copies[-1].wait()


def vector_line(row):
    return lambda width: pl.BlockSpec((None, 1, width), lambda *_: (row, 0, 0))


def feed(tokens, mixed, cotangent, vectors, wo, wu, wd):
    count, width = tokens.shape
    hidden = wu.shape[1]
    block = 512
    chunk = width
    chunks = hidden // chunk
    rows = pl.BlockSpec((block, width), lambda i: (i, 0))
    anywhere = pl.BlockSpec(memory_space=pl.ANY)
    return pl.pallas_call(
        functools.partial(feed_kernel, chunk),
        out_shape=[
            jax.ShapeDtypeStruct((count, width), BF16),
            jax.ShapeDtypeStruct((count, width), F32),
            jax.ShapeDtypeStruct((count, width), BF16),
            jax.ShapeDtypeStruct((3 + chunks, 1, width), F32),
            jax.ShapeDtypeStruct(wo.shape, BF16),
            jax.ShapeDtypeStruct(wu.shape, BF16),
            jax.ShapeDtypeStruct(wd.shape, BF16),
        ],
        grid=(count // block,),
        in_specs=[
            rows,
            rows,
            rows,
            vector_line(GAIN2)(width),
            vector_line(SHIFT2)(width),
            pl.BlockSpec((chunks, 1, chunk), lambda i: (0, 0, 0)),
            vector_line(DOWN_BIAS)(width),
            anywhere,
            anywhere,
            anywhere,
        ],
        out_specs=[
            rows,
            rows,
            rows,
            pl.BlockSpec((3 + chunks, 1, width), lambda i: (0, 0, 0)),
            anywhere,
            anywhere,
            anywhere,
        ],
        scratch_shapes=[
            pltpu.VMEM(wo.shape, BF16),
            pltpu.VMEM((chunks, width, chunk), BF16),
            pltpu.VMEM((chunks, chunk, width), BF16),
            pltpu.VMEM(wo.shape, F32),
            pltpu.VMEM((chunks, width, chunk), F32),
            pltpu.VMEM((chunks, chunk, width), F32),
            pltpu.VMEM((block, width), F32),
            pltpu.VMEM((block, width), F32),
            pltpu.VMEM((block, width), BF16),
            pltpu.VMEM((block, width), F32),
            pltpu.VMEM((2, width, chunk), BF16),
            pltpu.SemaphoreType.DMA((3,)),
            pltpu.SemaphoreType.DMA((2,)),
        ],
        compiler_params=params("arbitrary"),
        name="feed",
    )(
        tokens,
        mixed,
        cotangent,
        vectors,
        vectors,
        vectors,
        vectors,
        wo,
        wu,
        wd,
    )


def input_kernel(
    x_ref,
    gmid_ref,
    gq_ref,
    gk_ref,
    gv_ref,
    gain_ref,
    shift_ref,
    w_ref,
    gx_ref,
    small_ref,
    gw_ref,
    acc_ref,
):
    step = pl.program_id(0)
    width = x_ref.shape[1]

    @pl.when(step == 0)
    def _():
        acc_ref[...] = jnp.zeros_like(acc_ref)
        small_ref[...] = jnp.zeros_like(small_ref)

    normed, inverse = normalize(x_ref[...].astype(F32))
    low = (normed * gain_ref[...] + shift_ref[...]).astype(BF16)
    grad_normed = None
    for which, ref in enumerate((gq_ref, gk_ref, gv_ref)):
        grad = ref[...]
        acc_ref[which] += dot_tn(low, grad)
        part = dot_nt(grad, w_ref[:, which * width : (which + 1) * width])
        grad_normed = part if grad_normed is None else grad_normed + part
    small_ref[0] += column_sum(grad_normed * normed)
    small_ref[1] += column_sum(grad_normed)
    gx_ref[...] = gmid_ref[...] + norm_back(grad_normed * gain_ref[...], normed, inverse)

    @pl.when(step == pl.num_programs(0) - 1)
    def _():
        for which in range(3):
            gw_ref[:, which * width : (which + 1) * width] = acc_ref[which].astype(BF16)


def input_back(tokens, grad_middle, grads, vectors, weight):
    count, width = tokens.shape
    block = 512
    rows = pl.BlockSpec((block, width), lambda i: (i, 0))
    return pl.pallas_call(
        input_kernel,
        out_shape=[
            jax.ShapeDtypeStruct((count, width), F32),
            jax.ShapeDtypeStruct((2, 1, width), F32),
            jax.ShapeDtypeStruct(weight.shape, BF16),
        ],
        grid=(count // block,),
        in_specs=[rows] * 5
        + [vector_line(GAIN1)(width), vector_line(SHIFT1)(width)]
        + [pl.BlockSpec(weight.shape, lambda i: (0, 0))],
        out_specs=[
            rows,
            pl.BlockSpec((2, 1, width), lambda i: (0, 0, 0)),
            pl.BlockSpec(weight.shape, lambda i: (0, 0)),
        ],
        scratch_shapes=[pltpu.VMEM((3, width, width), F32)],
        compiler_params=params("arbitrary"),
        name="input_back",
    )(tokens, grad_middle, *grads, vectors, vectors, weight)


def gather(value):
    return lax.all_gather(value, "fsdp", axis=0, tiled=True)


def local(
    tokens,
    piece_start,
    piece_length,
    query_key_value,
    output_weight,
    up_weight,
    down_weight,
    first_gain,
    first_shift,
    second_gain,
    second_shift,
    up_bias,
    down_bias,
    cotangent,
):
    width = tokens.shape[1]
    devices, copies = (lax.axis_size("fsdp"), lax.axis_size("rep"))
    index = lax.axis_index("fsdp")

    def placed(vector):
        flat = jnp.zeros((devices * vector.shape[0],), BF16)
        flat = lax.dynamic_update_slice(flat, vector, (index * vector.shape[0],))
        return flat.reshape(-1, width)

    own = [up_bias, first_gain, first_shift, second_gain, second_shift, down_bias]
    own = jnp.concatenate([placed(vector) for vector in own], axis=0)
    own = jnp.pad(own, ((0, LINES - own.shape[0]), (0, 0)))

    wo = gather(output_weight)
    wu = gather(up_weight)
    wd = gather(down_weight)

    projected, wqkv, vectors = project(tokens, query_key_value, own, devices, copies)
    mixed, attention = attend(projected, piece_start, piece_length)
    block_output, grad_middle, grad_mixed, small2, gwo, gwu, gwd = feed(
        tokens, mixed, cotangent, vectors, wo, wu, wd
    )
    grads = attend_back(projected, piece_start, piece_length, grad_mixed, mixed, attention)
    grad_tokens, small1, gwqkv = input_back(tokens, grad_middle, grads, vectors, wqkv)

    small = jnp.concatenate([small1.reshape(-1, width), small2.reshape(-1, width)], axis=0)

    def scatter(value):
        return lax.psum_scatter(value, "fsdp", scatter_dimension=0, tiled=True)

    def across(value):
        return lax.psum(value, "rep").astype(F32)

    small = small.astype(BF16)
    order = [small[0], small[1], small[2], small[3], small[5:].reshape(-1), small[4]]
    sizes = [v.size // devices for v in order]
    total = sum(sizes)
    padded = -(-total // 1024) * 1024
    packed = jnp.concatenate([v.reshape(devices, -1) for v in order], axis=1)
    packed = jnp.pad(packed, ((0, 0), (0, padded - total))).reshape(devices * 8, padded // 8)
    packed = across(scatter(packed)).reshape(-1)
    tails, at = ([], 0)
    for size in sizes:
        tails.append(packed[at : at + size])
        at += size
    gfg, gfs, gsg, gss, gub, gdb = tails
    return (
        block_output,
        grad_tokens,
        across(scatter(gwqkv)),
        across(scatter(gwo)),
        across(scatter(gwu)),
        across(scatter(gwd)),
        gfg,
        gfs,
        gsg,
        gss,
        gub,
        gdb,
    )


def solution(mesh):
    rows = P(("fsdp", "rep"), None)
    matrix = P("fsdp", None)
    vector = P("fsdp")
    return jax.shard_map(
        local,
        mesh=mesh,
        in_specs=(rows,) * 3 + (matrix,) * 4 + (vector,) * 6 + (rows,),
        out_specs=(rows,) * 2 + (matrix,) * 4 + (vector,) * 6,
        check_vma=False,
    )
```

```python
import functools

import jax
import jax.numpy as jnp
from jax import lax
from jax.experimental import pallas as pl
from jax.experimental.pallas import tpu as pltpu
from jax.sharding import PartitionSpec as P

HEAD_DIM = 64
PAIR = 2 * HEAD_DIM
ROWS = 256
MASKED_VALUE = -1e30
EPSILON = 1e-05
SCALE = HEAD_DIM**-0.5
GAIN1, SHIFT1, GAIN2, SHIFT2, DOWN_BIAS = (4, 5, 6, 7, 8)
LINES = 16
GELU_IN = 0.7978845608028654
GELU_CUBE = 0.044715
VMEM_LIMIT = 60 * 1024 * 1024

F32 = jnp.float32
BF16 = jnp.bfloat16


def dot(left, right):
    return lax.dot_general(left, right, (((1,), (0,)), ((), ())), preferred_element_type=F32)


def dot_nt(left, right):
    return lax.dot_general(left, right, (((1,), (1,)), ((), ())), preferred_element_type=F32)


def dot_tn(left, right):
    return lax.dot_general(left, right, (((0,), (0,)), ((), ())), preferred_element_type=F32)


def row_mean(values):
    return jnp.mean(values, axis=-1, keepdims=True)


def normalize(values):
    center = values - row_mean(values)
    inverse = lax.rsqrt(row_mean(center * center) + EPSILON)
    return (center * inverse, inverse)


def norm_back(grad, normed, inverse):
    return (grad - row_mean(grad) - normed * row_mean(grad * normed)) * inverse


def column_sum(values):
    return jnp.sum(values, axis=0, keepdims=True)


def params(*semantics):
    return pltpu.CompilerParams(dimension_semantics=semantics, vmem_limit_bytes=VMEM_LIMIT)


def comm_params(number, *semantics):
    return pltpu.CompilerParams(
        dimension_semantics=semantics,
        vmem_limit_bytes=VMEM_LIMIT,
        collective_id=number,
        has_side_effects=True,
    )


MESH = pl.DeviceIdType.MESH
LEVELS = 4
CORES = 2


class Place:
    def __init__(self, count, copies):
        self.count, self.copies = (count, copies)
        self.columns = count // (LEVELS * CORES)
        self.index = lax.axis_index("fsdp")
        self.rep = lax.axis_index("rep")
        self.core = lax.rem(self.index, CORES)
        chip = lax.div(self.index, CORES)
        self.column = lax.rem(chip, self.columns)
        self.level = lax.div(chip, self.columns)
        self.half = lax.rem(self.rep, 2)

    def block(self, up=0, across=0, other=0):
        level = lax.rem(self.level + (up + LEVELS), LEVELS)
        column = lax.rem(self.column + (across + self.columns), self.columns)
        core = lax.rem(self.core + other, CORES)
        return (level * self.columns + column) * CORES + core

    def device(self, up=0, across=0, other=0, copy=0):
        return (self.block(up, across, other), lax.rem(self.rep + copy, self.copies))

    def twin(self):
        return (self.index, self.rep + 1 - 2 * self.half)

    def meet(self, twin=False, copies=False):
        others = [self.device(up=up) for up in range(1, LEVELS)]
        others += [self.device(across=across) for across in range(1, self.columns)]
        others += [self.device(other=1)]
        if twin:
            others += [self.twin()]
        if copies:
            others += [self.device(copy=copy) for copy in range(1, self.copies)]
        barrier = pltpu.get_barrier_semaphore()
        for other in others:
            pl.semaphore_signal(barrier, inc=1, device_id=other, device_id_type=MESH)
        pl.semaphore_wait(barrier, len(others))


def send(source, target, sems, slot, device):
    return pltpu.make_async_remote_copy(
        src_ref=source,
        dst_ref=target,
        send_sem=sems.at[2 * slot],
        recv_sem=sems.at[2 * slot + 1],
        device_id=device,
        device_id_type=MESH,
    )


def gather_sems(count):
    return 2 * (LEVELS - 1 + 3 * count // CORES) + 1


class Gather:
    def __init__(self, place, source, target, rows, shared, sems):
        self.place, self.source, self.target = (place, source, target)
        self.sems, self.shared = (sems, shared)
        if shared:
            third = rows // 3
            half = place.half
            self.part = pl.ds(pl.multiple_of(half * third, third), 2 * third)
            self.give = pl.ds(pl.multiple_of(half * (2 * third), third), third)
        else:
            self.part = pl.ds(0, rows)

    def held(self, up, across):
        if up == 0 and across == 0:
            return self.source
        return self.target(self.place.block(-up, -across))

    def slot(self, phase, up, across):
        area = self.place.count // CORES
        return LEVELS - 1 + phase * area + across * LEVELS + up

    def level_copies(self):
        target = self.target(self.place.block()).at[self.part, :]
        source = self.source.at[self.part, :]
        return [
            send(source, target, self.sems, up - 1, self.place.device(up=up))
            for up in range(1, LEVELS)
        ]

    def column_copies(self, ups):
        place = self.place
        return [
            send(
                self.held(up, 0).at[self.part, :],
                self.target(place.block(-up)).at[self.part, :],
                self.sems,
                self.slot(0, up, across),
                place.device(across=across),
            )
            for up in ups
            for across in range(1, place.columns)
        ]

    def twin_copies(self, acrosses):
        if not self.shared:
            return []
        place = self.place
        return [
            send(
                self.held(up, across).at[self.give, :],
                self.target(place.block(-up, -across)).at[self.give, :],
                self.sems,
                self.slot(1, up, across),
                place.twin(),
            )
            for across in acrosses
            for up in range(LEVELS)
            if up or across
        ]

    def core_copies(self, first):
        place = self.place
        return [
            send(
                self.held(up, across),
                self.target(place.block(-up, -across)),
                self.sems,
                self.slot(2, up, across),
                place.device(other=1),
            )
            for across in range(place.columns)
            for up in range(LEVELS)
            if (up == 0 and across == 0) == first
        ]

    def own(self):
        last = gather_sems(self.place.count) - 1
        return pltpu.make_async_copy(
            self.source, self.target(self.place.block()), self.sems.at[last]
        )

    def start(self):
        for copy in self.level_copies() + self.column_copies([0]) + self.core_copies(True):
            copy.start()
        self.own().start()

    def after_levels(self):
        for copy in self.level_copies():
            copy.wait_recv()
        for copy in self.column_copies(range(1, LEVELS)) + self.twin_copies([0]):
            copy.start()

    def after_columns(self):
        for copy in self.column_copies(range(LEVELS)):
            copy.wait_recv()
        for copy in self.twin_copies(range(1, self.place.columns)):
            copy.start()
        if not self.shared:
            self.to_cores()

    def after_twins(self):
        for copy in self.twin_copies(range(self.place.columns)):
            copy.wait_recv()
        if self.shared:
            self.to_cores()

    def to_cores(self):
        for copy in self.core_copies(False):
            copy.start()

    def finish(self):
        for copy in self.core_copies(True) + self.core_copies(False):
            copy.wait_recv()
        self.own().wait()

    def drain(self):
        columns = range(self.place.columns)
        copies = self.level_copies() + self.column_copies(range(LEVELS))
        copies += self.twin_copies(columns) + self.core_copies(True) + self.core_copies(False)
        for copy in copies:
            copy.wait_send()


def scatter_slots(count, copies):
    area = count // CORES
    return area + (area - LEVELS) + (LEVELS - 1) + (copies - 1)


def scatter_scratch(count, copies, rows, columns):
    across = count // (CORES * LEVELS)
    return [
        pltpu.VMEM((count, rows, columns), BF16),
        pltpu.VMEM((across, LEVELS, rows, columns), BF16),
        pltpu.VMEM((max(across - 1, 1), LEVELS, rows, columns), BF16),
        pltpu.VMEM((LEVELS - 1, rows, columns), BF16),
        pltpu.VMEM((copies, rows, columns), BF16),
        pltpu.SemaphoreType.DMA((2 * scatter_slots(count, copies),)),
    ]


def add_low(left, right):
    return (left.astype(F32) + right.astype(F32)).astype(BF16)


class Scatter:
    def __init__(self, place, refs, write):
        self.place, self.write = (place, write)
        self.held, self.from_core, self.from_column, self.from_level, self.parts, self.sems = refs
        self.area = place.count // CORES

    def core_copies(self):
        place = self.place
        return [
            send(
                self.held.at[place.block(up, across, 1)],
                self.from_core.at[across, up],
                self.sems,
                across * LEVELS + up,
                place.device(other=1),
            )
            for across in range(place.columns)
            for up in range(LEVELS)
        ]

    def column_copies(self):
        place = self.place
        return [
            send(
                self.held.at[place.block(up, across)],
                self.from_column.at[across - 1, up],
                self.sems,
                self.area + (across - 1) * LEVELS + up,
                place.device(across=across),
            )
            for across in range(1, place.columns)
            for up in range(LEVELS)
        ]

    def level_copies(self):
        place = self.place
        base = 2 * self.area - LEVELS
        return [
            send(
                self.held.at[place.block(up)],
                self.from_level.at[up - 1],
                self.sems,
                base + up - 1,
                place.device(up=up),
            )
            for up in range(1, LEVELS)
        ]

    def rep_copies(self):
        place = self.place
        base = 2 * self.area - 1
        mine = self.parts.at[place.rep]
        return [
            send(mine, mine, self.sems, base + copy - 1, place.device(copy=copy))
            for copy in range(1, place.copies)
        ]

    def start(self):
        for copy in self.core_copies():
            copy.start()

    def after_cores(self):
        place = self.place
        for copy in self.core_copies():
            copy.wait_recv()

        def add(i, carry):
            across, up = (lax.div(i, LEVELS), lax.rem(i, LEVELS))
            block = place.block(up, across)
            self.held[block] = add_low(self.held[block], self.from_core[across, up])
            return carry

        lax.fori_loop(0, self.area, add, 0)
        for copy in self.column_copies():
            copy.start()

    def after_columns(self):
        place = self.place
        for copy in self.column_copies():
            copy.wait_recv()

        def add(up, carry):
            block = place.block(up)
            total = self.held[block].astype(F32)
            for across in range(place.columns - 1):
                total = total + self.from_column[across, up].astype(F32)
            self.held[block] = total.astype(BF16)
            return carry

        lax.fori_loop(0, LEVELS, add, 0)
        for copy in self.level_copies():
            copy.start()

    def after_levels(self):
        for copy in self.level_copies():
            copy.wait_recv()
        total = self.held[self.place.block()].astype(F32)
        for level in range(LEVELS - 1):
            total = total + self.from_level[level].astype(F32)
        self.parts[self.place.rep] = total.astype(BF16)
        for copy in self.rep_copies():
            copy.start()

    def after_copies(self):
        for copy in self.rep_copies():
            copy.wait_recv()
        total = self.parts[0].astype(F32)
        for rep in range(1, self.place.copies):
            total = total + self.parts[rep].astype(F32)
        self.write(total)

    def drain(self):
        copies = self.core_copies() + self.column_copies() + self.level_copies()
        for copy in copies + self.rep_copies():
            copy.wait_send()


def reduce_scratch(count, copies, lines, width):
    across = count // (CORES * LEVELS)
    slots = 1 + (across - 1) + (LEVELS - 1) + (copies - 1)
    return [
        pltpu.VMEM((3, lines, 1, width), F32),
        pltpu.VMEM((1 + across - 1 + LEVELS - 1, lines, 1, width), F32),
        pltpu.VMEM((copies, lines, 1, width), F32),
        pltpu.SemaphoreType.DMA((2 * slots,)),
    ]


class Reduce:
    def __init__(self, place, refs, out):
        self.place, self.out = (place, out)
        self.sums, self.landed, self.parts, self.sems = refs

    def group(self, phase):
        place = self.place
        if phase == 0:
            targets = [place.device(other=1)]
            first = 0
        elif phase == 1:
            targets = [place.device(across=across) for across in range(1, place.columns)]
            first = 1
        else:
            targets = [place.device(up=up) for up in range(1, LEVELS)]
            first = place.columns
        return [
            send(self.sums.at[phase], self.landed.at[first + i], self.sems, first + i, target)
            for i, target in enumerate(targets)
        ]

    def rep_copies(self):
        place = self.place
        base = place.columns + LEVELS - 1
        mine = self.parts.at[place.rep]
        return [
            send(mine, mine, self.sems, base + copy - 1, place.device(copy=copy))
            for copy in range(1, place.copies)
        ]

    def start(self, value):
        self.sums[0] = value
        for copy in self.group(0):
            copy.start()

    def next(self, phase):
        copies = self.group(phase)
        for copy in copies:
            copy.wait_recv()
        first = (0, 1, self.place.columns)[phase]
        total = self.sums[phase]
        for i in range(len(copies)):
            total = total + self.landed[first + i]
        if phase < 2:
            self.sums[phase + 1] = total
            for copy in self.group(phase + 1):
                copy.start()
        else:
            self.parts[self.place.rep] = total
            for copy in self.rep_copies():
                copy.start()

    def after_cores(self):
        self.next(0)

    def after_columns(self):
        self.next(1)

    def after_levels(self):
        self.next(2)

    def after_copies(self):
        for copy in self.rep_copies():
            copy.wait_recv()
        total = self.parts[0]
        for rep in range(1, self.place.copies):
            total = total + self.parts[rep]
        self.out[...] = total

    def drain(self):
        for copy in self.group(0) + self.group(1) + self.group(2) + self.rep_copies():
            copy.wait_send()


def project_kernel(
    count,
    copies,
    x_ref,
    w_hbm,
    vec_hbm,
    o_ref,
    full_hbm,
    vec_ref,
    n1_ref,
    w_ref,
    all_ref,
    sems,
    load_sem,
):
    step = pl.program_id(0)
    width = x_ref.shape[1]
    rows = w_hbm.shape[0]
    lines = vec_hbm.shape[0]
    place = Place(count, copies)
    pieces = [
        Gather(
            place,
            vec_hbm,
            lambda block: all_ref.at[pl.ds(pl.multiple_of(block * lines, lines), lines), :],
            lines,
            False,
            sems.at[0],
        )
    ]
    for which in range(3):
        columns = pl.ds(which * width, width)

        def target(block, columns=columns):
            return full_hbm.at[pl.ds(pl.multiple_of(block * rows, rows), rows), columns]

        pieces.append(
            Gather(place, w_hbm.at[:, columns], target, rows, False, sems.at[1 + which])
        )

    def multiply(which):
        pieces[1 + which].finish()
        copy = pltpu.make_async_copy(
            full_hbm.at[:, pl.ds(which * width, width)], w_ref, load_sem
        )
        copy.start()
        copy.wait()
        o_ref[...] = dot(n1_ref[...], w_ref[...]).astype(BF16)

    @pl.when(step == 0)
    def _():
        place.meet()
        for piece in pieces:
            piece.start()
        pieces[0].after_levels()
        pieces[0].after_columns()
        pieces[1].after_levels()
        pieces[0].finish()
        vectors = all_ref[0:lines, :].astype(F32)
        for other in range(1, count):
            vectors = vectors + all_ref[other * lines : (other + 1) * lines, :].astype(F32)
        for line in range(lines):
            vec_ref[line] = vectors[line : line + 1, :]
        total = x_ref.shape[0]
        gain, shift = (vec_ref[GAIN1], vec_ref[SHIFT1])
        block = 256

        def norm_rows(i, carry):
            at = pl.ds(pl.multiple_of(i * block, block), block)
            normed, _ = normalize(x_ref[at, :].astype(F32))
            n1_ref[at, :] = (normed * gain + shift).astype(BF16)
            return carry

        lax.fori_loop(0, total // block, norm_rows, 0)
        pieces[1].after_columns()
        pieces[2].after_levels()
        pieces[2].after_columns()
        multiply(0)

    @pl.when(step == 1)
    def _():
        pieces[3].after_levels()
        pieces[3].after_columns()
        multiply(1)

    @pl.when(step == 2)
    def _():
        multiply(2)
        for piece in pieces:
            piece.drain()


def project(tokens, weight, vectors, count, copies):
    total, width = tokens.shape
    rows, columns = weight.shape
    lines = vectors.shape[0]
    anywhere = pl.BlockSpec(memory_space=pl.ANY)
    return pl.pallas_call(
        functools.partial(project_kernel, count, copies),
        out_shape=[
            jax.ShapeDtypeStruct((total, columns), BF16),
            jax.ShapeDtypeStruct((rows * count, columns), BF16),
            jax.ShapeDtypeStruct((lines, 1, width), F32),
        ],
        grid=(3,),
        in_specs=[pl.BlockSpec((total, width), lambda i: (0, 0)), anywhere, anywhere],
        out_specs=[
            pl.BlockSpec((total, width), lambda i: (0, i)),
            anywhere,
            pl.BlockSpec((lines, 1, width), lambda i: (0, 0, 0)),
        ],
        scratch_shapes=[
            pltpu.VMEM((total, width), BF16),
            pltpu.VMEM((width, width), BF16),
            pltpu.VMEM((count * lines, width), BF16),
            pltpu.SemaphoreType.DMA((4, gather_sems(count))),
            pltpu.SemaphoreType.DMA,
        ],
        compiler_params=comm_params(0, "arbitrary"),
        name="project",
    )(tokens, weight, vectors)


def label_of(position, start_ref, length_ref, seq, pieces):
    label = jnp.zeros(position.shape, jnp.int32)
    for piece in range(pieces):
        start = start_ref[seq, piece]
        inside = (position >= start) & (position < start + length_ref[seq, piece])
        label = jnp.where(inside, piece + 1, label)
    return label


def key_count(first_row, slot):
    return (first_row // slot + 1) * slot


def block_masks(start_ref, length_ref, seq, pieces, first_row, keys):
    query_pos = first_row + lax.broadcasted_iota(jnp.int32, (ROWS, 1), 0)
    key_pos = lax.broadcasted_iota(jnp.int32, (1, keys), 1)
    query_label = label_of(query_pos, start_ref, length_ref, seq, pieces)
    key_label = label_of(key_pos, start_ref, length_ref, seq, pieces)
    query_label = jnp.where(query_label > 0, query_label, -1)
    allowed = (key_pos <= query_pos) | (query_label == key_label)
    chosen = allowed & (key_pos != 0) & (key_pos != query_pos)
    return (allowed, chosen)


def triangle_sum(triangle, values):
    upper = values.astype(BF16)
    rest = values - upper.astype(F32)
    middle = rest.astype(BF16)
    lower = (rest - middle.astype(F32)).astype(BF16)
    return dot(triangle, upper) + dot(triangle, middle) + dot(triangle, lower)


def head_mask(half):
    lane = lax.broadcasted_iota(jnp.int32, (1, PAIR), 1)
    return (lane >= HEAD_DIM) if half else (lane < HEAD_DIM)


def at_steps(step, table):
    for when in sorted(set(table)):
        @pl.when(step == when)
        def _(when=when):
            for action in table[when]:
                action()


def schedule(*entries):
    table = {}
    for when, action in entries:
        table.setdefault(when, []).append(action)
    return table


def attend_kernel(
    slot,
    pieces,
    count,
    copies,
    start_ref,
    length_ref,
    q_ref,
    k_ref,
    v_ref,
    wo_hbm,
    wu_hbm,
    wd_hbm,
    o_ref,
    *rest,
):
    att_refs = rest[:pieces]
    full_o, full_u, full_d, bias_ref, prefix_ref, sems = rest[pieces:]
    seq = pl.program_id(0)
    steps = pl.num_programs(0) * pl.num_programs(1)
    step = seq * pl.num_programs(1) + pl.program_id(1)
    length = q_ref.shape[0]
    zero = jnp.zeros((), BF16)

    place = Place(count, copies)
    cuts = []
    for shard, full, cut_rows, cut_columns in (
        (wo_hbm, full_o, 1, 1),
        (wu_hbm, full_u, 1, 2),
        (wd_hbm, full_d, 2, 1),
    ):
        rows, columns = (shard.shape[0] // cut_rows, shard.shape[1] // cut_columns)
        for i in range(cut_rows):
            for j in range(cut_columns):
                across = pl.ds(j * columns, columns)

                def target(block, full=full, i=i, rows=rows, cut=cut_rows, across=across):
                    first = pl.multiple_of(block * (rows * cut) + i * rows, rows)
                    return full.at[pl.ds(first, rows), across]

                source = shard.at[pl.ds(i * rows, rows), across]
                cuts.append(
                    Gather(place, source, target, rows, copies % 2 == 0, sems.at[len(cuts)])
                )

    def begin():
        place.meet(twin=copies % 2 == 0)
        for cut in cuts:
            cut.start()

    table = schedule(
        (0, begin),
        *[(2 * i + 2, cut.after_levels) for i, cut in enumerate(cuts)],
        *[(2 * i + 4, cut.after_columns) for i, cut in enumerate(cuts[:4])],
        *[(2 * i + 6, cut.after_twins) for i, cut in enumerate(cuts[:3])],
    )
    at_steps(step, table)

    @pl.when(pl.program_id(1) == 0)
    def _():
        prefix_ref[...] = jnp.zeros_like(prefix_ref)
        row = lax.broadcasted_iota(jnp.int32, (ROWS, ROWS), 0)
        col = lax.broadcasted_iota(jnp.int32, (ROWS, ROWS), 1)
        triangle = (col < row).astype(BF16)
        for first_row in range(0, length, ROWS):
            keys = key_count(first_row, slot)
            rows = pl.ds(first_row, ROWS)
            query = jnp.where(head_mask(0), q_ref[rows, :], zero)
            scores = dot_nt(query, k_ref[:keys, :]) * SCALE
            allowed, chosen = block_masks(start_ref, length_ref, seq, pieces, first_row, keys)
            selected = jnp.where(chosen & (scores > 0), scores, 0.0)
            penalty = prefix_ref[:, :keys] + triangle_sum(triangle, selected)
            bias_ref[rows, :keys] = jnp.where(allowed, -penalty, MASKED_VALUE)
            prefix_ref[:, :keys] += column_sum(selected)

    for first_row in range(0, length, ROWS):
        keys = key_count(first_row, slot)
        rows = pl.ds(first_row, ROWS)
        slot_rows = pl.ds(first_row % slot, ROWS)
        mixed = None
        for half in range(2):
            mask = head_mask(half)
            query = jnp.where(mask, q_ref[rows, :], zero) * jnp.asarray(SCALE, BF16)
            logits = dot_nt(query, k_ref[:keys, :]) + bias_ref[rows, :keys]
            largest = jnp.max(logits, axis=-1, keepdims=True)
            raised = jnp.exp(logits - largest)
            inverse = 1.0 / jnp.sum(raised, axis=-1, keepdims=True)
            attention = (raised * inverse).astype(BF16)
            att_refs[first_row // slot][half, slot_rows, :] = attention
            value = jnp.where(mask, v_ref[:keys, :], zero)
            part = dot(attention, value)
            mixed = part if mixed is None else mixed + part
        o_ref[rows, :] = mixed.astype(BF16)

    @pl.when(step == steps - 1)
    def _():
        cuts[4].after_columns()
        cuts[3].after_twins()
        cuts[4].after_twins()
        for cut in cuts:
            cut.finish()
        for cut in cuts:
            cut.drain()


def attend(projected, starts, lengths, wo, wu, wd, devices, copies):
    sequences, pieces = starts.shape
    count, columns = projected.shape
    length = count // sequences
    slot = length // pieces
    width = columns // 3
    pairs = width // PAIR

    def part(which):
        return pl.BlockSpec((length, PAIR), lambda s, p, a, b: (s, which * pairs + p))

    att_shapes = [
        jax.ShapeDtypeStruct((sequences, 2 * pairs, slot, (i + 1) * slot), BF16)
        for i in range(pieces)
    ]
    att_specs = [
        pl.BlockSpec((None, 2, slot, (i + 1) * slot), lambda s, p, a, b: (s, p, 0, 0))
        for i in range(pieces)
    ]
    anywhere = pl.BlockSpec(memory_space=pl.ANY)
    whole = [
        jax.ShapeDtypeStruct((devices * w.shape[0], w.shape[1]), BF16) for w in (wo, wu, wd)
    ]
    results = pl.pallas_call(
        functools.partial(attend_kernel, slot, pieces, devices, copies),
        out_shape=[jax.ShapeDtypeStruct((count, width), BF16)] + att_shapes + whole,
        grid_spec=pltpu.PrefetchScalarGridSpec(
            num_scalar_prefetch=2,
            grid=(sequences, pairs),
            in_specs=[part(0), part(1), part(2)] + [anywhere] * 3,
            out_specs=[pl.BlockSpec((length, PAIR), lambda s, p, a, b: (s, p))]
            + att_specs
            + [anywhere] * 3,
            scratch_shapes=[
                pltpu.VMEM((length, length), F32),
                pltpu.VMEM((1, length), F32),
                pltpu.SemaphoreType.DMA((5, gather_sems(devices))),
            ],
        ),
        compiler_params=comm_params(1, "arbitrary", "arbitrary"),
        name="attend",
    )(starts, lengths, projected, projected, projected, wo, wu, wd)
    return (results[0], results[1 : 1 + pieces], results[1 + pieces :])


def attend_back_kernel(
    slot,
    pieces,
    chunks,
    count,
    copies,
    pairs,
    start_ref,
    length_ref,
    q_ref,
    k_ref,
    v_ref,
    gm_ref,
    o_ref,
    *rest,
):
    att_refs = rest[:pieces]
    rest = rest[pieces:]
    n2_hbm, gb_hbm, hid_hbm, cot_hbm, mixed_hbm, gproj_hbm, small_ref = rest[:7]
    gq_ref, gk_ref, gv_ref, gwo_ref, gwu_ref, gwd_ref, gsmall_ref = rest[7:14]
    sum_ref, later_ref, dq_ref, dk_ref, dv_ref, left_ref, right_ref, load_sem = rest[14:22]
    rest = rest[22:]
    step = pl.program_id(0)
    first_step = 2 * chunks + 1
    turn = jnp.maximum(step - first_step, 0)
    seq = lax.div(turn, pairs)
    turn = lax.rem(turn, pairs)
    last = turn == pairs - 1
    width = left_ref.shape[2]

    place = Place(count, copies)
    parts = []
    for c in range(chunks):

        def write_up(value, c=c):
            gwu_ref[:, c * width : (c + 1) * width] = value

        parts.append(Scatter(place, rest[6 * c : 6 * c + 6], write_up))
    rest = rest[6 * chunks :]
    half_rows = gwd_ref.shape[0] // 2
    for h in range(2):

        def write_down(value, h=h):
            gwd_ref[h * half_rows : (h + 1) * half_rows, :] = value

        parts.append(Scatter(place, rest[6 * h : 6 * h + 6], write_down))
    rest = rest[12:]

    def write_out(value):
        gwo_ref[...] = value

    parts.append(Scatter(place, rest[:6], write_out))
    small = Reduce(place, rest[6:10], gsmall_ref)
    up_parts, (down0, down1, out_part) = (parts[:chunks], parts[chunks:])

    left_slot = [0] * chunks + [(c + 1) % 2 for c in range(chunks)] + [(chunks + 1) % 2]
    right_slot = [c % 2 for c in range(chunks)] + [chunks % 2] * chunks + [(chunks + 1) % 2]

    def chunk_of(ref, c):
        return ref.at[:, pl.ds(c * width, width)]

    left_loads = {0: n2_hbm, 2 * chunks: mixed_hbm}
    right_loads = {chunks: cot_hbm, 2 * chunks: gproj_hbm}
    for c in range(chunks):
        left_loads[chunks + c] = chunk_of(hid_hbm, c)
        right_loads[c] = chunk_of(gb_hbm, c)

    def loads(when):
        copies = []
        if when in left_loads:
            at = left_slot[when]
            copies.append(
                pltpu.make_async_copy(left_loads[when], left_ref.at[at], load_sem.at[at])
            )
        if when in right_loads:
            at = right_slot[when]
            copies.append(
                pltpu.make_async_copy(right_loads[when], right_ref.at[at], load_sem.at[2 + at])
            )
        return copies

    def begin():
        for copy in loads(0):
            copy.start()
        place.meet(copies=True)
        small.start(small_ref[...])

    entries = [(0, begin)]
    for c, part in enumerate(up_parts):
        entries += [
            (c + 2, part.after_cores),
            (2 * c + 5, part.after_columns),
            (2 * c + 8, part.after_levels),
            (2 * c + 10, part.after_copies),
        ]
    entries += [
        (3, small.after_cores),
        (6, small.after_columns),
        (10, small.after_levels),
        (13, small.after_copies),
        (first_step, down0.after_cores),
        (first_step + 1, down1.after_cores),
        (first_step + 1, out_part.after_cores),
        (first_step + 4, down0.after_columns),
        (first_step + 6, down1.after_columns),
        (first_step + 7, out_part.after_columns),
        (first_step + 7, down0.after_levels),
        (first_step + 9, down0.after_copies),
        (first_step + 9, down1.after_levels),
        (first_step + 10, out_part.after_levels),
        (first_step + 11, down1.after_copies),
    ]
    at_steps(step, schedule(*entries))

    @pl.when(step < first_step)
    def _():
        left_at = jnp.zeros((), jnp.int32)
        right_at = jnp.zeros((), jnp.int32)
        for when in range(first_step):

            @pl.when(step == when)
            def _(when=when):
                if when + 1 < first_step:
                    for copy in loads(when + 1):
                        copy.start()
                for copy in loads(when):
                    copy.wait()

            left_at = jnp.where(step == when, left_slot[when], left_at)
            right_at = jnp.where(step == when, right_slot[when], right_at)
        grad = dot_tn(left_ref[left_at], right_ref[right_at]).astype(BF16)
        for when in range(first_step):

            @pl.when(step == when)
            def _(when=when):
                if when < chunks or when == 2 * chunks:
                    part = out_part if when == 2 * chunks else up_parts[when]
                    rows = width // count
                    for block in range(count):
                        part.held[block] = grad[block * rows : (block + 1) * rows, :]
                    part.start()
                else:
                    blocks = count // chunks
                    for i in range(blocks):
                        block = (when - chunks) * blocks + i
                        for h, part in enumerate((down0, down1)):
                            at = (2 * i + h) * half_rows
                            part.held[block] = grad[at : at + half_rows, :]
                    if when == 2 * chunks - 1:
                        down0.start()
                        down1.start()

    @pl.when(step >= first_step)
    def _():
        attend_back_step(
            slot,
            pieces,
            seq,
            turn,
            last,
            start_ref,
            length_ref,
            (q_ref, k_ref, v_ref, gm_ref, o_ref),
            att_refs,
            (gq_ref, gk_ref, gv_ref),
            (sum_ref, later_ref, dq_ref, dk_ref, dv_ref),
        )

    @pl.when(step == pl.num_programs(0) - 1)
    def _():
        out_part.after_copies()
        for part in parts + [small]:
            part.drain()


def attend_back_step(
    slot, pieces, seq, turn, last, start_ref, length_ref, inputs, att_refs, outs, scratch
):
    q_ref, k_ref, v_ref, gm_ref, o_ref = inputs
    gq_ref, gk_ref, gv_ref = outs
    sum_ref, later_ref, dq_ref, dk_ref, dv_ref = scratch
    length = q_ref.shape[0]
    zero = jnp.zeros((), BF16)
    scale = jnp.asarray(SCALE, BF16)

    @pl.when(turn == 0)
    def _():
        sum_ref[...] = jnp.zeros_like(sum_ref)

    dk_ref[...] = jnp.zeros_like(dk_ref)
    dv_ref[...] = jnp.zeros_like(dv_ref)

    def head(half, first_head):
        mask = head_mask(half)
        if first_head:
            later_ref[...] = jnp.zeros_like(later_ref)
            row = lax.broadcasted_iota(jnp.int32, (ROWS, ROWS), 0)
            col = lax.broadcasted_iota(jnp.int32, (ROWS, ROWS), 1)
            triangle = (col > row).astype(BF16)
        for first_row in reversed(range(0, length, ROWS)):
            keys = key_count(first_row, slot)
            rows = pl.ds(first_row, ROWS)
            slot_rows = pl.ds(first_row % slot, ROWS)
            grad = jnp.where(mask, gm_ref[rows, :], zero)
            delta = jnp.sum(
                grad.astype(F32) * o_ref[rows, :].astype(F32), axis=-1, keepdims=True
            )
            attention = att_refs[first_row // slot][half, slot_rows, :]
            grad_attention = dot_nt(grad, v_ref[:keys, :])
            grad_logits = attention.astype(F32) * (grad_attention - delta)
            query = jnp.where(mask, q_ref[rows, :], zero) * scale
            if first_head:
                total = sum_ref[rows, :keys] + grad_logits
                grad_selected = -(later_ref[:, :keys] + triangle_sum(triangle, total))
                later_ref[:, :keys] += column_sum(total)
                _, chosen = block_masks(start_ref, length_ref, seq, pieces, first_row, keys)
                positive = dot_nt(query, k_ref[:keys, :]) > 0
                grad_logits = grad_logits + jnp.where(chosen & positive, grad_selected, 0.0)
            else:
                sum_ref[rows, :keys] += grad_logits
            grad_scores = grad_logits.astype(BF16)
            key = jnp.where(mask, k_ref[:keys, :], zero) * scale
            part = dot(grad_scores, key)
            if half == 1:
                dq_ref[rows, :] = part
            else:
                dq_ref[rows, :] += part
            dk_ref[:keys, :] += dot_tn(grad_scores, query)
            dv_ref[:keys, :] += dot_tn(attention, grad)

    head(1, False)

    @pl.when(jnp.logical_not(last))
    def _():
        head(0, False)

    @pl.when(last)
    def _():
        head(0, True)

    gq_ref[...] = dq_ref[...].astype(BF16)
    gk_ref[...] = dk_ref[...].astype(BF16)
    gv_ref[...] = dv_ref[...].astype(BF16)


def attend_back(
    projected, starts, lengths, grad_mixed, mixed, attention, kept, small, devices, copies
):
    n2, grad_before, hidden, cotangent, grad_proj = kept
    sequences, pieces = starts.shape
    count, columns = projected.shape
    length = count // sequences
    slot = length // pieces
    width = columns // 3
    pairs = width // PAIR
    chunks = hidden.shape[1] // width
    first_step = 2 * chunks + 1
    rows = width // devices
    down_rows = hidden.shape[1] // devices
    lines = small.shape[0]

    def turn(step):
        at = jnp.maximum(step - first_step, 0)
        return (lax.div(at, pairs), pairs - 1 - lax.rem(at, pairs))

    def part(which):
        def index(step, a, b):
            seq, pair = turn(step)
            return (seq, which * pairs + pair)

        return pl.BlockSpec((length, PAIR), index)

    def att_index(step, a, b):
        seq, pair = turn(step)
        return (seq, pair, 0, 0)

    att_specs = [pl.BlockSpec((None, 2, slot, (i + 1) * slot), att_index) for i in range(pieces)]
    anywhere = pl.BlockSpec(memory_space=pl.ANY)

    def fixed(shape):
        return pl.BlockSpec(shape, lambda *_: (0,) * len(shape))

    results = [(rows, width), (rows, chunks * width), (down_rows, width), (lines, 1, width)]
    scratch = [
        pltpu.VMEM((length, length), F32),
        pltpu.VMEM((1, length), F32),
        pltpu.VMEM((length, PAIR), F32),
        pltpu.VMEM((length, PAIR), F32),
        pltpu.VMEM((length, PAIR), F32),
        pltpu.VMEM((2, count, width), BF16),
        pltpu.VMEM((2, count, width), BF16),
        pltpu.SemaphoreType.DMA((4,)),
    ]
    for piece_rows in [rows] * chunks + [down_rows // 2] * 2 + [rows]:
        scratch += scatter_scratch(devices, copies, piece_rows, width)
    scratch += reduce_scratch(devices, copies, lines, width)
    return pl.pallas_call(
        functools.partial(
            attend_back_kernel, slot, pieces, chunks, devices, copies, pairs
        ),
        out_shape=[jax.ShapeDtypeStruct((count, width), BF16)] * 3
        + [jax.ShapeDtypeStruct(shape, F32) for shape in results],
        grid_spec=pltpu.PrefetchScalarGridSpec(
            num_scalar_prefetch=2,
            grid=(first_step + sequences * pairs,),
            in_specs=[part(0), part(1), part(2), part(0), part(0)]
            + att_specs
            + [anywhere] * 6
            + [fixed((lines, 1, width))],
            out_specs=[part(0), part(0), part(0)] + [fixed(shape) for shape in results],
            scratch_shapes=scratch,
        ),
        compiler_params=comm_params(2, "arbitrary"),
        name="attend_back",
    )(
        starts,
        lengths,
        projected,
        projected,
        projected,
        grad_mixed,
        mixed,
        *attention,
        n2,
        grad_before,
        hidden,
        cotangent,
        mixed,
        grad_proj,
        small,
    )


def gelu_and_slope(values):
    square = values * values
    inner = GELU_IN * values * (1.0 + GELU_CUBE * square)
    bent = jnp.tanh(inner)
    half = 0.5 * (1.0 + bent)
    slope = half + 0.5 * values * (1.0 - bent * bent) * (
        GELU_IN * (1.0 + 3.0 * GELU_CUBE * square)
    )
    return (values * half, slope)


def feed_kernel(
    chunk,
    x_ref,
    mixed_ref,
    cot_ref,
    gain_ref,
    shift_ref,
    up_bias_ref,
    down_bias_ref,
    wo_hbm,
    wu_hbm,
    wd_hbm,
    out_ref,
    gmid_ref,
    gmix_ref,
    small_ref,
    n2_ref,
    hid_ref,
    gb_ref,
    gproj_ref,
    wo_ref,
    wu_ref,
    wd_ref,
    acc_ref,
    gnorm_ref,
    mid_ref,
    load_sem,
):
    step = pl.program_id(0)
    chunks = wu_ref.shape[0]

    def load_out():
        return pltpu.make_async_copy(wo_hbm, wo_ref, load_sem.at[0])

    def load_up(c):
        return pltpu.make_async_copy(
            wu_hbm.at[:, pl.ds(c * chunk, chunk)], wu_ref.at[c], load_sem.at[1 + 2 * c]
        )

    def load_down(c):
        return pltpu.make_async_copy(
            wd_hbm.at[pl.ds(c * chunk, chunk), :], wd_ref.at[c], load_sem.at[2 + 2 * c]
        )

    @pl.when(step == 0)
    def _():
        load_out().start()
        for c in range(chunks):
            load_up(c).start()
            load_down(c).start()
        small_ref[...] = jnp.zeros_like(small_ref)
        load_out().wait()

    mid_ref[...] = x_ref[...].astype(F32) + dot(mixed_ref[...], wo_ref[...])

    @pl.when(step == 0)
    def _():
        for c in range(chunks):
            load_up(c).wait()
            load_down(c).wait()

    normed, _ = normalize(mid_ref[...])
    n2_ref[...] = (normed * gain_ref[...] + shift_ref[...]).astype(BF16)
    acc_ref[...] = jnp.zeros_like(acc_ref)
    gnorm_ref[...] = jnp.zeros_like(gnorm_ref)

    def one_chunk(c, carry):
        columns = pl.ds(pl.multiple_of(c * chunk, chunk), chunk)
        before = dot(n2_ref[...], wu_ref[c]) + up_bias_ref[c]
        hidden, slope = gelu_and_slope(before)
        hidden = hidden.astype(BF16)
        hid_ref[:, columns] = hidden
        acc_ref[...] += dot(hidden, wd_ref[c])
        grad_hidden = dot_nt(cot_ref[...], wd_ref[c]).astype(BF16)
        grad_before = (grad_hidden.astype(F32) * slope).astype(BF16)
        gb_ref[:, columns] = grad_before
        small_ref[3 + c] += column_sum(grad_before.astype(F32))
        gnorm_ref[...] += dot_nt(grad_before, wu_ref[c])
        return carry

    lax.fori_loop(0, chunks, one_chunk, 0)

    out_ref[...] = (mid_ref[...] + (acc_ref[...] + down_bias_ref[...])).astype(BF16)
    grad_normed = gnorm_ref[...]
    normed, inverse = normalize(mid_ref[...])
    cot = cot_ref[...].astype(F32)
    small_ref[0] += column_sum(grad_normed * normed)
    small_ref[1] += column_sum(grad_normed)
    small_ref[2] += column_sum(cot)
    grad_middle = cot + norm_back(grad_normed * gain_ref[...], normed, inverse)
    gmid_ref[...] = grad_middle
    grad_proj = grad_middle.astype(BF16)
    gproj_ref[...] = grad_proj
    gmix_ref[...] = dot_nt(grad_proj, wo_ref[...]).astype(BF16)


def vector_line(row):
    return lambda width: pl.BlockSpec((None, 1, width), lambda *_: (row, 0, 0))


def feed(tokens, mixed, cotangent, vectors, wo, wu, wd):
    count, width = tokens.shape
    hidden = wu.shape[1]
    block = 512
    chunk = width
    chunks = hidden // chunk
    rows = pl.BlockSpec((block, width), lambda i: (i, 0))
    anywhere = pl.BlockSpec(memory_space=pl.ANY)
    wide = pl.BlockSpec((block, hidden), lambda i: (i, 0))

    def low(columns):
        return jax.ShapeDtypeStruct((count, columns), BF16)

    return pl.pallas_call(
        functools.partial(feed_kernel, chunk),
        out_shape=[
            low(width),
            jax.ShapeDtypeStruct((count, width), F32),
            low(width),
            jax.ShapeDtypeStruct((3 + chunks, 1, width), F32),
            low(width),
            low(hidden),
            low(hidden),
            low(width),
        ],
        grid=(count // block,),
        in_specs=[
            rows,
            rows,
            rows,
            vector_line(GAIN2)(width),
            vector_line(SHIFT2)(width),
            pl.BlockSpec((chunks, 1, chunk), lambda i: (0, 0, 0)),
            vector_line(DOWN_BIAS)(width),
            anywhere,
            anywhere,
            anywhere,
        ],
        out_specs=[
            rows,
            rows,
            rows,
            pl.BlockSpec((3 + chunks, 1, width), lambda i: (0, 0, 0)),
            rows,
            wide,
            wide,
            rows,
        ],
        scratch_shapes=[
            pltpu.VMEM(wo.shape, BF16),
            pltpu.VMEM((chunks, width, chunk), BF16),
            pltpu.VMEM((chunks, chunk, width), BF16),
            pltpu.VMEM((block, width), F32),
            pltpu.VMEM((block, width), F32),
            pltpu.VMEM((block, width), F32),
            pltpu.SemaphoreType.DMA((1 + 2 * chunks,)),
        ],
        compiler_params=params("arbitrary"),
        name="feed",
    )(
        tokens,
        mixed,
        cotangent,
        vectors,
        vectors,
        vectors,
        vectors,
        wo,
        wu,
        wd,
    )


def input_kernel(
    count,
    copies,
    gmid_ref,
    gain_ref,
    shift_ref,
    x_hbm,
    gq_hbm,
    gk_hbm,
    gv_hbm,
    w_hbm,
    gx_ref,
    gw_ref,
    gsmall_ref,
    x_ref,
    n1_ref,
    g_ref,
    w_ref,
    small_ref,
    load_sem,
    *rest,
):
    step = pl.program_id(0)
    total, width = x_ref.shape
    block = gx_ref.shape[0]
    place = Place(count, copies)
    parts = []
    for which in range(3):

        def write(value, which=which):
            gw_ref[:, which * width : (which + 1) * width] = value

        parts.append(Scatter(place, rest[6 * which : 6 * which + 6], write))
    small = Reduce(place, rest[18:22], gsmall_ref)

    def load_x():
        return pltpu.make_async_copy(x_hbm, x_ref, load_sem.at[0])

    def load_grad(which):
        source = (gq_hbm, gk_hbm, gv_hbm)[which]
        return pltpu.make_async_copy(source, g_ref.at[which], load_sem.at[1 + which])

    def load_weight():
        return pltpu.make_async_copy(w_hbm, w_ref, load_sem.at[4])

    def begin():
        load_x().start()
        for which in range(3):
            load_grad(which).start()
        load_weight().start()
        place.meet(copies=True)
        small_ref[...] = jnp.zeros_like(small_ref)
        load_x().wait()

        def norm_rows(i, carry):
            at = pl.ds(pl.multiple_of(i * 256, 256), 256)
            normed, _ = normalize(x_ref[at, :].astype(F32))
            n1_ref[at, :] = (normed * gain_ref[...] + shift_ref[...]).astype(BF16)
            return carry

        lax.fori_loop(0, total // 256, norm_rows, 0)

    table = schedule(
        (0, begin),
        (1, parts[0].after_cores),
        (2, parts[1].after_cores),
        (3, parts[2].after_cores),
        (4, parts[0].after_columns),
        (5, parts[1].after_columns),
        (6, parts[2].after_columns),
        (6, parts[0].after_levels),
    )
    at_steps(step, table)

    @pl.when(step < 3)
    def _():
        for which in range(3):

            @pl.when(step == which)
            def _(which=which):
                load_grad(which).wait()

        grad = dot_tn(n1_ref[...], g_ref[step]).astype(BF16)
        for which in range(3):

            @pl.when(step == which)
            def _(which=which):
                rows = width // count
                for i in range(count):
                    parts[which].held[i] = grad[i * rows : (i + 1) * rows, :]
                parts[which].start()

    @pl.when(step == 3)
    def _():
        load_weight().wait()

    @pl.when(step >= 3)
    def _():
        at = pl.ds(pl.multiple_of((step - 3) * block, block), block)
        normed, inverse = normalize(x_ref[at, :].astype(F32))
        grad_normed = None
        for which in range(3):
            part = dot_nt(g_ref[which, at, :], w_ref[:, which * width : (which + 1) * width])
            grad_normed = part if grad_normed is None else grad_normed + part
        small_ref[0] += column_sum(grad_normed * normed)
        small_ref[1] += column_sum(grad_normed)
        gx_ref[...] = gmid_ref[...] + norm_back(grad_normed * gain_ref[...], normed, inverse)

    @pl.when(step == pl.num_programs(0) - 1)
    def _():
        small.start(small_ref[...])
        parts[1].after_levels()
        small.after_cores()
        parts[0].after_copies()
        small.after_columns()
        parts[2].after_levels()
        parts[1].after_copies()
        small.after_levels()
        parts[2].after_copies()
        small.after_copies()
        for part in parts + [small]:
            part.drain()


def input_back(tokens, grad_middle, grads, vectors, weight, devices, copies):
    count, width = tokens.shape
    block = 512
    shard = width // devices
    rows = pl.BlockSpec((block, width), lambda i: (jnp.maximum(i - 3, 0), 0))
    anywhere = pl.BlockSpec(memory_space=pl.ANY)
    scratch = [
        pltpu.VMEM((count, width), BF16),
        pltpu.VMEM((count, width), BF16),
        pltpu.VMEM((3, count, width), BF16),
        pltpu.VMEM(weight.shape, BF16),
        pltpu.VMEM((2, 1, width), F32),
        pltpu.SemaphoreType.DMA((5,)),
    ]
    for _ in range(3):
        scratch += scatter_scratch(devices, copies, shard, width)
    scratch += reduce_scratch(devices, copies, 2, width)
    return pl.pallas_call(
        functools.partial(input_kernel, devices, copies),
        out_shape=[
            jax.ShapeDtypeStruct((count, width), F32),
            jax.ShapeDtypeStruct((shard, 3 * width), F32),
            jax.ShapeDtypeStruct((2, 1, width), F32),
        ],
        grid=(3 + count // block,),
        in_specs=[rows, vector_line(GAIN1)(width), vector_line(SHIFT1)(width)]
        + [anywhere] * 5,
        out_specs=[
            rows,
            pl.BlockSpec((shard, 3 * width), lambda i: (0, 0)),
            pl.BlockSpec((2, 1, width), lambda i: (0, 0, 0)),
        ],
        scratch_shapes=scratch,
        compiler_params=comm_params(3, "arbitrary"),
        name="input_back",
    )(grad_middle, vectors, vectors, tokens, *grads, weight)


def local(
    tokens,
    piece_start,
    piece_length,
    query_key_value,
    output_weight,
    up_weight,
    down_weight,
    first_gain,
    first_shift,
    second_gain,
    second_shift,
    up_bias,
    down_bias,
    cotangent,
):
    width = tokens.shape[1]
    devices, copies = (lax.axis_size("fsdp"), lax.axis_size("rep"))
    index = lax.axis_index("fsdp")

    def placed(vector):
        flat = jnp.zeros((devices * vector.shape[0],), BF16)
        flat = lax.dynamic_update_slice(flat, vector, (index * vector.shape[0],))
        return flat.reshape(-1, width)

    own = [up_bias, first_gain, first_shift, second_gain, second_shift, down_bias]
    own = jnp.concatenate([placed(vector) for vector in own], axis=0)
    own = jnp.pad(own, ((0, LINES - own.shape[0]), (0, 0)))

    projected, wqkv, vectors = project(tokens, query_key_value, own, devices, copies)
    mixed, attention, (wo, wu, wd) = attend(
        projected,
        piece_start,
        piece_length,
        output_weight,
        up_weight,
        down_weight,
        devices,
        copies,
    )
    block_output, grad_middle, grad_mixed, small2, n2, hidden, grad_before, grad_proj = feed(
        tokens, mixed, cotangent, vectors, wo, wu, wd
    )
    *grads, gwo, gwu, gwd, small2 = attend_back(
        projected,
        piece_start,
        piece_length,
        grad_mixed,
        mixed,
        attention,
        (n2, grad_before, hidden, cotangent, grad_proj),
        small2,
        devices,
        copies,
    )
    grad_tokens, gwqkv, small1 = input_back(
        tokens, grad_middle, grads, vectors, wqkv, devices, copies
    )

    def mine(values):
        values = values.reshape(-1)
        size = values.shape[0] // devices
        return lax.dynamic_slice(values, (index * size,), (size,))

    return (
        block_output,
        grad_tokens,
        gwqkv,
        gwo,
        gwu,
        gwd,
        mine(small1[0]),
        mine(small1[1]),
        mine(small2[0]),
        mine(small2[1]),
        mine(small2[3:]),
        mine(small2[2]),
    )


def solution(mesh):
    rows = P(("fsdp", "rep"), None)
    matrix = P("fsdp", None)
    vector = P("fsdp")
    return jax.shard_map(
        local,
        mesh=mesh,
        in_specs=(rows,) * 3 + (matrix,) * 4 + (vector,) * 6 + (rows,),
        out_specs=(rows,) * 2 + (matrix,) * 4 + (vector,) * 6,
        check_vma=False,
    )
```

```python
import functools

import jax
import jax.numpy as jnp
from jax import lax
from jax.experimental import pallas as pl
from jax.experimental.pallas import tpu as pltpu
from jax.sharding import PartitionSpec as P

HEAD_DIM = 64
PAIR = 2 * HEAD_DIM
ROWS = 256
MASKED_VALUE = -1e30
EPSILON = 1e-05
SCALE = HEAD_DIM**-0.5
GAIN1, SHIFT1, GAIN2, SHIFT2, DOWN_BIAS = (4, 5, 6, 7, 8)
LINES = 16
GELU_IN = 0.7978845608028654
GELU_CUBE = 0.044715
VMEM_LIMIT = 60 * 1024 * 1024

F32 = jnp.float32
BF16 = jnp.bfloat16


def dot(left, right):
    return lax.dot_general(left, right, (((1,), (0,)), ((), ())), preferred_element_type=F32)


def dot_nt(left, right):
    return lax.dot_general(left, right, (((1,), (1,)), ((), ())), preferred_element_type=F32)


def dot_tn(left, right):
    return lax.dot_general(left, right, (((0,), (0,)), ((), ())), preferred_element_type=F32)


def row_mean(values):
    return jnp.mean(values, axis=-1, keepdims=True)


def normalize(values):
    center = values - row_mean(values)
    inverse = lax.rsqrt(row_mean(center * center) + EPSILON)
    return (center * inverse, inverse)


def norm_back(grad, normed, inverse):
    return (grad - row_mean(grad) - normed * row_mean(grad * normed)) * inverse


def column_sum(values):
    return jnp.sum(values, axis=0, keepdims=True)


def params(*semantics):
    return pltpu.CompilerParams(dimension_semantics=semantics, vmem_limit_bytes=VMEM_LIMIT)


def comm_params(number, *semantics):
    return pltpu.CompilerParams(
        dimension_semantics=semantics,
        vmem_limit_bytes=VMEM_LIMIT,
        collective_id=number,
        has_side_effects=True,
    )


MESH = pl.DeviceIdType.MESH
LEVELS = 4
CORES = 2


class Place:
    def __init__(self, count, copies):
        self.count, self.copies = (count, copies)
        self.columns = count // (LEVELS * CORES)
        self.index = lax.axis_index("fsdp")
        self.rep = lax.axis_index("rep")
        self.core = lax.rem(self.index, CORES)
        chip = lax.div(self.index, CORES)
        self.column = lax.rem(chip, self.columns)
        self.level = lax.div(chip, self.columns)
        self.half = lax.rem(self.rep, 2)

    def block(self, up=0, across=0, other=0):
        level = lax.rem(self.level + (up + LEVELS), LEVELS)
        column = lax.rem(self.column + (across + self.columns), self.columns)
        core = lax.rem(self.core + other, CORES)
        return (level * self.columns + column) * CORES + core

    def device(self, up=0, across=0, other=0, copy=0):
        return (self.block(up, across, other), lax.rem(self.rep + copy, self.copies))

    def twin(self):
        return (self.index, self.rep + 1 - 2 * self.half)

    def meet(self, twin=False, copies=False):
        others = [self.device(up=up) for up in range(1, LEVELS)]
        others += [self.device(across=across) for across in range(1, self.columns)]
        others += [self.device(other=1)]
        if twin:
            others += [self.twin()]
        if copies:
            others += [self.device(copy=copy) for copy in range(1, self.copies)]
        barrier = pltpu.get_barrier_semaphore()
        for other in others:
            pl.semaphore_signal(barrier, inc=1, device_id=other, device_id_type=MESH)
        pl.semaphore_wait(barrier, len(others))


def send(source, target, sems, slot, device):
    return pltpu.make_async_remote_copy(
        src_ref=source,
        dst_ref=target,
        send_sem=sems.at[2 * slot],
        recv_sem=sems.at[2 * slot + 1],
        device_id=device,
        device_id_type=MESH,
    )


def gather_sems(count):
    return 2 * (LEVELS - 1 + 3 * count // CORES) + 1


class Gather:
    def __init__(self, place, source, target, rows, shared, sems):
        self.place, self.source, self.target = (place, source, target)
        self.sems, self.shared = (sems, shared)
        if shared:
            third = rows // 3
            half = place.half
            self.part = pl.ds(pl.multiple_of(half * third, third), 2 * third)
            self.give = pl.ds(pl.multiple_of(half * (2 * third), third), third)
        else:
            self.part = pl.ds(0, rows)

    def held(self, up, across):
        if up == 0 and across == 0:
            return self.source
        return self.target(self.place.block(-up, -across))

    def slot(self, phase, up, across):
        area = self.place.count // CORES
        return LEVELS - 1 + phase * area + across * LEVELS + up

    def level_copies(self):
        target = self.target(self.place.block()).at[self.part, :]
        source = self.source.at[self.part, :]
        return [
            send(source, target, self.sems, up - 1, self.place.device(up=up))
            for up in range(1, LEVELS)
        ]

    def column_copies(self, ups):
        place = self.place
        return [
            send(
                self.held(up, 0).at[self.part, :],
                self.target(place.block(-up)).at[self.part, :],
                self.sems,
                self.slot(0, up, across),
                place.device(across=across),
            )
            for up in ups
            for across in range(1, place.columns)
        ]

    def twin_copies(self, acrosses):
        if not self.shared:
            return []
        place = self.place
        return [
            send(
                self.held(up, across).at[self.give, :],
                self.target(place.block(-up, -across)).at[self.give, :],
                self.sems,
                self.slot(1, up, across),
                place.twin(),
            )
            for across in acrosses
            for up in range(LEVELS)
            if up or across
        ]

    def core_copies(self, first):
        place = self.place
        return [
            send(
                self.held(up, across),
                self.target(place.block(-up, -across)),
                self.sems,
                self.slot(2, up, across),
                place.device(other=1),
            )
            for across in range(place.columns)
            for up in range(LEVELS)
            if (up == 0 and across == 0) == first
        ]

    def own(self):
        last = gather_sems(self.place.count) - 1
        return pltpu.make_async_copy(
            self.source, self.target(self.place.block()), self.sems.at[last]
        )

    def start(self):
        for copy in self.level_copies() + self.core_copies(True):
            copy.start()
        self.own().start()

    def after_levels(self):
        for copy in self.column_copies([0]):
            copy.start()
        for copy in self.level_copies():
            copy.wait_recv()
        for copy in self.column_copies(range(1, LEVELS)) + self.twin_copies([0]):
            copy.start()

    def after_columns(self):
        for copy in self.column_copies(range(LEVELS)):
            copy.wait_recv()
        for copy in self.twin_copies(range(1, self.place.columns)):
            copy.start()
        if not self.shared:
            self.to_cores()

    def after_twins(self):
        for copy in self.twin_copies(range(self.place.columns)):
            copy.wait_recv()
        if self.shared:
            self.to_cores()

    def to_cores(self):
        for copy in self.core_copies(False):
            copy.start()

    def finish(self):
        for copy in self.core_copies(True) + self.core_copies(False):
            copy.wait_recv()
        self.own().wait()

    def drain(self):
        columns = range(self.place.columns)
        copies = self.level_copies() + self.column_copies(range(LEVELS))
        copies += self.twin_copies(columns) + self.core_copies(True) + self.core_copies(False)
        for copy in copies:
            copy.wait_send()


def scatter_slots(count, copies):
    area = count // CORES
    return area + (area - LEVELS) + (LEVELS - 1) + (copies - 1)


def scatter_scratch(count, copies, rows, columns):
    across = count // (CORES * LEVELS)
    return [
        pltpu.VMEM((count, rows, columns), BF16),
        pltpu.VMEM((across, LEVELS, rows, columns), BF16),
        pltpu.VMEM((max(across - 1, 1), LEVELS, rows, columns), BF16),
        pltpu.VMEM((LEVELS - 1, rows, columns), BF16),
        pltpu.VMEM((copies, rows, columns), BF16),
        pltpu.SemaphoreType.DMA((2 * scatter_slots(count, copies),)),
    ]


def add_low(left, right):
    return (left.astype(F32) + right.astype(F32)).astype(BF16)


class Scatter:
    def __init__(self, place, refs, write):
        self.place, self.write = (place, write)
        self.held, self.from_core, self.from_column, self.from_level, self.parts, self.sems = refs
        self.area = place.count // CORES

    def core_copies(self):
        place = self.place
        return [
            send(
                self.held.at[place.block(up, across, 1)],
                self.from_core.at[across, up],
                self.sems,
                across * LEVELS + up,
                place.device(other=1),
            )
            for across in range(place.columns)
            for up in range(LEVELS)
        ]

    def column_copies(self):
        place = self.place
        return [
            send(
                self.held.at[place.block(up, across)],
                self.from_column.at[across - 1, up],
                self.sems,
                self.area + (across - 1) * LEVELS + up,
                place.device(across=across),
            )
            for across in range(1, place.columns)
            for up in range(LEVELS)
        ]

    def level_copies(self):
        place = self.place
        base = 2 * self.area - LEVELS
        return [
            send(
                self.held.at[place.block(up)],
                self.from_level.at[up - 1],
                self.sems,
                base + up - 1,
                place.device(up=up),
            )
            for up in range(1, LEVELS)
        ]

    def rep_copies(self):
        place = self.place
        base = 2 * self.area - 1
        mine = self.parts.at[place.rep]
        return [
            send(mine, mine, self.sems, base + copy - 1, place.device(copy=copy))
            for copy in range(1, place.copies)
        ]

    def start(self):
        for copy in self.core_copies():
            copy.start()

    def after_cores(self):
        place = self.place
        for copy in self.core_copies():
            copy.wait_recv()

        def add(i, carry):
            across, up = (lax.div(i, LEVELS), lax.rem(i, LEVELS))
            block = place.block(up, across)
            self.held[block] = add_low(self.held[block], self.from_core[across, up])
            return carry

        lax.fori_loop(0, self.area, add, 0)
        for copy in self.column_copies():
            copy.start()

    def after_columns(self):
        place = self.place
        for copy in self.column_copies():
            copy.wait_recv()

        def add(up, carry):
            block = place.block(up)
            total = self.held[block].astype(F32)
            for across in range(place.columns - 1):
                total = total + self.from_column[across, up].astype(F32)
            self.held[block] = total.astype(BF16)
            return carry

        lax.fori_loop(0, LEVELS, add, 0)
        for copy in self.level_copies():
            copy.start()

    def after_levels(self):
        for copy in self.level_copies():
            copy.wait_recv()
        total = self.held[self.place.block()].astype(F32)
        for level in range(LEVELS - 1):
            total = total + self.from_level[level].astype(F32)
        self.parts[self.place.rep] = total.astype(BF16)
        for copy in self.rep_copies():
            copy.start()

    def after_copies(self):
        for copy in self.rep_copies():
            copy.wait_recv()
        total = self.parts[0].astype(F32)
        for rep in range(1, self.place.copies):
            total = total + self.parts[rep].astype(F32)
        self.write(total)

    def drain(self):
        copies = self.core_copies() + self.column_copies() + self.level_copies()
        for copy in copies + self.rep_copies():
            copy.wait_send()


def reduce_scratch(count, copies, lines, width):
    across = count // (CORES * LEVELS)
    slots = 1 + (across - 1) + (LEVELS - 1) + (copies - 1)
    return [
        pltpu.VMEM((3, lines, 1, width), F32),
        pltpu.VMEM((1 + across - 1 + LEVELS - 1, lines, 1, width), F32),
        pltpu.VMEM((copies, lines, 1, width), F32),
        pltpu.SemaphoreType.DMA((2 * slots,)),
    ]


class Reduce:
    def __init__(self, place, refs, out):
        self.place, self.out = (place, out)
        self.sums, self.landed, self.parts, self.sems = refs

    def group(self, phase):
        place = self.place
        if phase == 0:
            targets = [place.device(other=1)]
            first = 0
        elif phase == 1:
            targets = [place.device(across=across) for across in range(1, place.columns)]
            first = 1
        else:
            targets = [place.device(up=up) for up in range(1, LEVELS)]
            first = place.columns
        return [
            send(self.sums.at[phase], self.landed.at[first + i], self.sems, first + i, target)
            for i, target in enumerate(targets)
        ]

    def rep_copies(self):
        place = self.place
        base = place.columns + LEVELS - 1
        mine = self.parts.at[place.rep]
        return [
            send(mine, mine, self.sems, base + copy - 1, place.device(copy=copy))
            for copy in range(1, place.copies)
        ]

    def start(self, value):
        self.sums[0] = value
        for copy in self.group(0):
            copy.start()

    def next(self, phase):
        copies = self.group(phase)
        for copy in copies:
            copy.wait_recv()
        first = (0, 1, self.place.columns)[phase]
        total = self.sums[phase]
        for i in range(len(copies)):
            total = total + self.landed[first + i]
        if phase < 2:
            self.sums[phase + 1] = total
            for copy in self.group(phase + 1):
                copy.start()
        else:
            self.parts[self.place.rep] = total
            for copy in self.rep_copies():
                copy.start()

    def after_cores(self):
        self.next(0)

    def after_columns(self):
        self.next(1)

    def after_levels(self):
        self.next(2)

    def after_copies(self):
        for copy in self.rep_copies():
            copy.wait_recv()
        total = self.parts[0]
        for rep in range(1, self.place.copies):
            total = total + self.parts[rep]
        self.out[...] = total

    def drain(self):
        for copy in self.group(0) + self.group(1) + self.group(2) + self.rep_copies():
            copy.wait_send()


def label_of(position, start_ref, length_ref, seq, pieces):
    label = jnp.zeros(position.shape, jnp.int32)
    for piece in range(pieces):
        start = start_ref[seq, piece]
        inside = (position >= start) & (position < start + length_ref[seq, piece])
        label = jnp.where(inside, piece + 1, label)
    return label


def key_count(first_row, slot):
    return (first_row // slot + 1) * slot


def block_masks(start_ref, length_ref, seq, pieces, first_row, keys):
    query_pos = first_row + lax.broadcasted_iota(jnp.int32, (ROWS, 1), 0)
    key_pos = lax.broadcasted_iota(jnp.int32, (1, keys), 1)
    query_label = label_of(query_pos, start_ref, length_ref, seq, pieces)
    key_label = label_of(key_pos, start_ref, length_ref, seq, pieces)
    query_label = jnp.where(query_label > 0, query_label, -1)
    allowed = (key_pos <= query_pos) | (query_label == key_label)
    chosen = allowed & (key_pos != 0) & (key_pos != query_pos)
    return (allowed, chosen)


def triangle_sum(triangle, values):
    upper = values.astype(BF16)
    rest = values - upper.astype(F32)
    middle = rest.astype(BF16)
    lower = (rest - middle.astype(F32)).astype(BF16)
    return dot(triangle, upper) + dot(triangle, middle) + dot(triangle, lower)


def head_mask(half):
    lane = lax.broadcasted_iota(jnp.int32, (1, PAIR), 1)
    return (lane >= HEAD_DIM) if half else (lane < HEAD_DIM)


def at_steps(step, table):
    for when in sorted(set(table)):
        @pl.when(step == when)
        def _(when=when):
            for action in table[when]:
                action()


def schedule(*entries):
    table = {}
    for when, action in entries:
        table.setdefault(when, []).append(action)
    return table


def pair_groups(pairs):
    groups, at = ([], 0)
    for size in [1, 1] + [2] * pairs:
        if at < pairs:
            groups.append(range(at, min(at + size, pairs)))
            at += size
    return groups


def front_kernel(
    slot,
    pieces,
    count,
    copies,
    pairs,
    start_ref,
    length_ref,
    x_hbm,
    wqkv_hbm,
    vec_hbm,
    wo_hbm,
    wu_hbm,
    wd_hbm,
    qkv_ref,
    o_ref,
    *rest,
):
    att_refs, rest = (rest[:pieces], rest[pieces:])
    n1_hbm, vec_ref, full_w, full_o, full_u, full_d = rest[:6]
    x_ref, n1_ref, all_ref, stage_ref, w_ref, bias_ref, prefix_ref = rest[6:13]
    stage_sems, load_sems, vec_sems, w_sems, rest_sems = rest[13:]
    pair, seq = (pl.program_id(0), pl.program_id(1))
    sequences = pl.num_programs(1)
    step = pair * sequences + seq
    length = qkv_ref.shape[0]
    width = x_ref.shape[1]
    sequence_count = x_ref.shape[0] // length
    lines = vec_hbm.shape[0]
    zero = jnp.zeros((), BF16)
    place = Place(count, copies)
    twins = copies % 2 == 0

    def whole(ref, rows, cut, i, columns):
        def target(block):
            first = pl.multiple_of(block * (rows * cut) + i * rows, rows)
            return ref.at[pl.ds(first, rows), columns]

        return target

    vec = Gather(place, vec_hbm, whole(all_ref, lines, 1, 0, pl.ds(0, width)), lines, False, vec_sems)
    groups = pair_groups(pairs)
    rows = wqkv_hbm.shape[0]
    gathers = []
    for i, group in enumerate(groups):
        columns = pl.ds(group[0] * 3 * PAIR, len(group) * 3 * PAIR)
        shared = twins and i > 2 and rows % 48 == 0
        gathers.append(
            Gather(
                place,
                stage_ref.at[:, columns],
                whole(full_w, rows, 1, 0, columns),
                rows,
                shared,
                w_sems.at[i],
            )
        )
    cuts = []
    for shard, full, cut_rows, cut_columns in (
        (wo_hbm, full_o, 1, 1),
        (wu_hbm, full_u, 1, 2),
        (wd_hbm, full_d, 2, 1),
    ):
        rows, columns = (shard.shape[0] // cut_rows, shard.shape[1] // cut_columns)
        for i in range(cut_rows):
            for j in range(cut_columns):
                across = pl.ds(j * columns, columns)
                source = shard.at[pl.ds(i * rows, rows), across]
                target = whole(full, rows, cut_rows, i, across)
                cuts.append(Gather(place, source, target, rows, twins, rest_sems.at[len(cuts)]))

    def stage_copies():
        found = []
        for p in range(pairs):
            for which in range(3):
                at = 3 * p + which
                found.append(
                    pltpu.make_async_copy(
                        wqkv_hbm.at[:, pl.ds(which * width + p * PAIR, PAIR)],
                        stage_ref.at[:, pl.ds(at * PAIR, PAIR)],
                        stage_sems.at[at],
                    )
                )
        return found

    def load_x():
        return pltpu.make_async_copy(x_hbm, x_ref, load_sems.at[0])

    def keep_n1():
        return pltpu.make_async_copy(n1_ref, n1_hbm, load_sems.at[1])

    def load_w(p):
        return pltpu.make_async_copy(
            full_w.at[:, pl.ds(p * 3 * PAIR, 3 * PAIR)], w_ref.at[p % 2], load_sems.at[2 + p % 2]
        )

    def norm_rows(which):
        gain, shift = (vec_ref[GAIN1], vec_ref[SHIFT1])

        def body(i, carry):
            at = pl.ds(pl.multiple_of(which * length + i * ROWS, ROWS), ROWS)
            normed, _ = normalize(x_ref[at, :].astype(F32))
            n1_ref[at, :] = (normed * gain + shift).astype(BF16)
            return carry

        lax.fori_loop(0, length // ROWS, body, 0)
        if which == sequence_count - 1:
            keep_n1().start()

    def begin():
        for copy in stage_copies():
            copy.start()
        load_x().start()
        place.meet(twin=twins)
        vec.start()
        for copy in stage_copies():
            copy.wait()
        for gather in gathers + cuts:
            gather.start()
        vec.after_levels()
        gathers[0].after_levels()
        vec.after_columns()
        gathers[0].after_columns()
        gathers[1].after_levels()
        vec.finish()
        vectors = all_ref[0:lines, :].astype(F32)
        for other in range(1, count):
            vectors = vectors + all_ref[other * lines : (other + 1) * lines, :].astype(F32)
        for line in range(lines):
            vec_ref[line] = vectors[line : line + 1, :]
        load_x().wait()
        gathers[0].finish()
        load_w(0).start()
        norm_rows(0)
        gathers[1].after_columns()
        load_w(0).wait()

    def ready(p):
        for group, gather in zip(groups, gathers):
            if p == group[0]:
                gather.finish()
        load_w(p).start()

    s = sequence_count
    entries = [(0, begin)]
    entries += [(which, functools.partial(norm_rows, which)) for which in range(1, s)]
    entries += [
        (1, gathers[2].after_levels),
        (2, gathers[2].after_columns),
    ]
    for i, gather in enumerate(gathers[3:]):
        need = groups[3 + i][0] * s - 1
        entries += [
            (need - 4, gather.after_levels),
            (need - 3, gather.after_columns),
            (need - 2, gather.after_twins),
        ]
    for p in range(1, pairs):
        entries.append((p * s - 1, functools.partial(ready, p)))
        entries.append((p * s, load_w(p).wait))
    for i, cut in enumerate(cuts):
        entries += [
            ((3, 4, 6, 7, 9)[i], cut.after_levels),
            ((5, 6, 8, 9, 10)[i], cut.after_columns),
            ((6, 8, 9, 10, 11)[i], cut.after_twins),
        ]
    at_steps(step, schedule(*entries))

    seq_rows = pl.ds(pl.multiple_of(seq * length, length), length)
    qkv_ref[...] = dot(n1_ref[seq_rows, :], w_ref[lax.rem(pair, 2)]).astype(BF16)

    @pl.when(pair == 0)
    def _():
        prefix_ref[...] = jnp.zeros_like(prefix_ref)
        row = lax.broadcasted_iota(jnp.int32, (ROWS, ROWS), 0)
        col = lax.broadcasted_iota(jnp.int32, (ROWS, ROWS), 1)
        triangle = (col < row).astype(BF16)
        for first_row in range(0, length, ROWS):
            keys = key_count(first_row, slot)
            at = pl.ds(first_row, ROWS)
            query = jnp.where(head_mask(0), qkv_ref[at, :PAIR], zero)
            scores = dot_nt(query, qkv_ref[:keys, PAIR : 2 * PAIR]) * SCALE
            allowed, chosen = block_masks(start_ref, length_ref, seq, pieces, first_row, keys)
            selected = jnp.where(chosen & (scores > 0), scores, 0.0)
            penalty = prefix_ref[:, :keys] + triangle_sum(triangle, selected)
            bias_ref[seq, at, :keys] = jnp.where(allowed, -penalty, MASKED_VALUE)
            prefix_ref[:, :keys] += column_sum(selected)

    for first_row in range(0, length, ROWS):
        keys = key_count(first_row, slot)
        at = pl.ds(first_row, ROWS)
        slot_rows = pl.ds(first_row % slot, ROWS)
        mixed = None
        for half in range(2):
            mask = head_mask(half)
            query = jnp.where(mask, qkv_ref[at, :PAIR], zero) * jnp.asarray(SCALE, BF16)
            logits = dot_nt(query, qkv_ref[:keys, PAIR : 2 * PAIR]) + bias_ref[seq, at, :keys]
            largest = jnp.max(logits, axis=-1, keepdims=True)
            raised = jnp.exp(logits - largest)
            inverse = 1.0 / jnp.sum(raised, axis=-1, keepdims=True)
            attention = (raised * inverse).astype(BF16)
            att_refs[first_row // slot][half, slot_rows, :] = attention
            value = jnp.where(mask, qkv_ref[:keys, 2 * PAIR :], zero)
            part = dot(attention, value)
            mixed = part if mixed is None else mixed + part
        o_ref[at, :] = mixed.astype(BF16)

    @pl.when(step == pairs * sequence_count - 1)
    def _():
        for cut in cuts:
            cut.finish()
        for gather in [vec] + gathers + cuts:
            gather.drain()
        keep_n1().wait()


def front(tokens, starts, lengths, wqkv, vectors, wo, wu, wd, devices, copies):
    sequences, pieces = starts.shape
    count, width = tokens.shape
    length = count // sequences
    slot = length // pieces
    pairs = width // PAIR
    lines = vectors.shape[0]
    anywhere = pl.BlockSpec(memory_space=pl.ANY)

    def low(*shape):
        return jax.ShapeDtypeStruct(shape, BF16)

    att_shapes = [low(sequences, 2 * pairs, slot, (i + 1) * slot) for i in range(pieces)]
    att_specs = [
        pl.BlockSpec((None, 2, slot, (i + 1) * slot), lambda p, s, a, b: (s, p, 0, 0))
        for i in range(pieces)
    ]
    weights = [low(devices * w.shape[0], w.shape[1]) for w in (wqkv, wo, wu, wd)]
    sems = gather_sems(devices)
    results = pl.pallas_call(
        functools.partial(front_kernel, slot, pieces, devices, copies, pairs),
        out_shape=[low(count, 3 * width), low(count, width)]
        + att_shapes
        + [low(count, width), jax.ShapeDtypeStruct((lines, 1, width), F32)]
        + weights,
        grid_spec=pltpu.PrefetchScalarGridSpec(
            num_scalar_prefetch=2,
            grid=(pairs, sequences),
            in_specs=[anywhere] * 6,
            out_specs=[
                pl.BlockSpec((length, 3 * PAIR), lambda p, s, a, b: (s, p)),
                pl.BlockSpec((length, PAIR), lambda p, s, a, b: (s, p)),
            ]
            + att_specs
            + [anywhere, pl.BlockSpec((lines, 1, width), lambda *_: (0, 0, 0))]
            + [anywhere] * 4,
            scratch_shapes=[
                pltpu.VMEM((count, width), BF16),
                pltpu.VMEM((count, width), BF16),
                pltpu.VMEM((devices * lines, width), BF16),
                pltpu.VMEM(wqkv.shape, BF16),
                pltpu.VMEM((2, width, 3 * PAIR), BF16),
                pltpu.VMEM((sequences, length, length), F32),
                pltpu.VMEM((1, length), F32),
                pltpu.SemaphoreType.DMA((3 * pairs,)),
                pltpu.SemaphoreType.DMA((4,)),
                pltpu.SemaphoreType.DMA((sems,)),
                pltpu.SemaphoreType.DMA((len(pair_groups(pairs)), sems)),
                pltpu.SemaphoreType.DMA((5, sems)),
            ],
        ),
        compiler_params=comm_params(1, "arbitrary", "arbitrary"),
        name="front",
    )(starts, lengths, tokens, wqkv, vectors, wo, wu, wd)
    return (results[:2], results[2 : 2 + pieces], results[2 + pieces :])


def attend_back_kernel(
    slot,
    pieces,
    chunks,
    count,
    copies,
    pairs,
    start_ref,
    length_ref,
    q_ref,
    k_ref,
    v_ref,
    gm_ref,
    o_ref,
    *rest,
):
    att_refs = rest[:pieces]
    rest = rest[pieces:]
    n2_hbm, gb_hbm, hid_hbm, cot_hbm, mixed_hbm, gproj_hbm, small_ref = rest[:7]
    g_ref, gwo_ref, gwu_ref, gwd_ref, gsmall_ref = rest[7:12]
    sum_ref, later_ref, dq_ref, dk_ref, dv_ref, left_ref, right_ref, load_sem = rest[12:20]
    rest = rest[20:]
    step = pl.program_id(0)
    first_step = 2 * chunks + 1
    turn = jnp.maximum(step - first_step, 0)
    seq = lax.div(turn, pairs)
    turn = lax.rem(turn, pairs)
    last = turn == pairs - 1
    width = left_ref.shape[2]

    place = Place(count, copies)
    parts = []
    for c in range(chunks):

        def write_up(value, c=c):
            gwu_ref[:, c * width : (c + 1) * width] = value

        parts.append(Scatter(place, rest[6 * c : 6 * c + 6], write_up))
    rest = rest[6 * chunks :]
    half_rows = gwd_ref.shape[0] // 2
    for h in range(2):

        def write_down(value, h=h):
            gwd_ref[h * half_rows : (h + 1) * half_rows, :] = value

        parts.append(Scatter(place, rest[6 * h : 6 * h + 6], write_down))
    rest = rest[12:]

    def write_out(value):
        gwo_ref[...] = value

    parts.append(Scatter(place, rest[:6], write_out))
    small = Reduce(place, rest[6:10], gsmall_ref)
    up_parts, (down0, down1, out_part) = (parts[:chunks], parts[chunks:])

    left_slot = [0] * chunks + [(c + 1) % 2 for c in range(chunks)] + [(chunks + 1) % 2]
    right_slot = [c % 2 for c in range(chunks)] + [chunks % 2] * chunks + [(chunks + 1) % 2]

    def chunk_of(ref, c):
        return ref.at[:, pl.ds(c * width, width)]

    left_loads = {0: n2_hbm, 2 * chunks: mixed_hbm}
    right_loads = {chunks: cot_hbm, 2 * chunks: gproj_hbm}
    for c in range(chunks):
        left_loads[chunks + c] = chunk_of(hid_hbm, c)
        right_loads[c] = chunk_of(gb_hbm, c)

    def loads(when):
        copies = []
        if when in left_loads:
            at = left_slot[when]
            copies.append(
                pltpu.make_async_copy(left_loads[when], left_ref.at[at], load_sem.at[at])
            )
        if when in right_loads:
            at = right_slot[when]
            copies.append(
                pltpu.make_async_copy(right_loads[when], right_ref.at[at], load_sem.at[2 + at])
            )
        return copies

    def begin():
        for copy in loads(0):
            copy.start()
        place.meet(copies=True)
        small.start(small_ref[...])

    entries = [(0, begin)]
    for c, part in enumerate(up_parts):
        entries += [
            (c + 2, part.after_cores),
            (2 * c + 5, part.after_columns),
            (2 * c + 8, part.after_levels),
            (2 * c + 10, part.after_copies),
        ]
    entries += [
        (3, small.after_cores),
        (6, small.after_columns),
        (10, small.after_levels),
        (13, small.after_copies),
        (first_step, down0.after_cores),
        (first_step + 1, down1.after_cores),
        (first_step + 1, out_part.after_cores),
        (first_step + 4, down0.after_columns),
        (first_step + 6, down1.after_columns),
        (first_step + 7, out_part.after_columns),
        (first_step + 7, down0.after_levels),
        (first_step + 9, down0.after_copies),
        (first_step + 9, down1.after_levels),
        (first_step + 10, out_part.after_levels),
        (first_step + 11, down1.after_copies),
    ]
    at_steps(step, schedule(*entries))

    @pl.when(step < first_step)
    def _():
        left_at = jnp.zeros((), jnp.int32)
        right_at = jnp.zeros((), jnp.int32)
        for when in range(first_step):

            @pl.when(step == when)
            def _(when=when):
                if when + 1 < first_step:
                    for copy in loads(when + 1):
                        copy.start()
                for copy in loads(when):
                    copy.wait()

            left_at = jnp.where(step == when, left_slot[when], left_at)
            right_at = jnp.where(step == when, right_slot[when], right_at)
        grad = dot_tn(left_ref[left_at], right_ref[right_at]).astype(BF16)
        for when in range(first_step):

            @pl.when(step == when)
            def _(when=when):
                if when < chunks or when == 2 * chunks:
                    part = out_part if when == 2 * chunks else up_parts[when]
                    rows = width // count
                    for block in range(count):
                        part.held[block] = grad[block * rows : (block + 1) * rows, :]
                    part.start()
                else:
                    blocks = count // chunks
                    for i in range(blocks):
                        block = (when - chunks) * blocks + i
                        for h, part in enumerate((down0, down1)):
                            at = (2 * i + h) * half_rows
                            part.held[block] = grad[at : at + half_rows, :]
                    if when == 2 * chunks - 1:
                        down0.start()
                        down1.start()

    @pl.when(step >= first_step)
    def _():
        attend_back_step(
            slot,
            pieces,
            seq,
            turn,
            last,
            start_ref,
            length_ref,
            (q_ref, k_ref, v_ref, gm_ref, o_ref),
            att_refs,
            g_ref,
            (sum_ref, later_ref, dq_ref, dk_ref, dv_ref),
        )

    @pl.when(step == pl.num_programs(0) - 1)
    def _():
        out_part.after_copies()
        for part in parts + [small]:
            part.drain()


def attend_back_step(
    slot, pieces, seq, turn, last, start_ref, length_ref, inputs, att_refs, g_ref, scratch
):
    q_ref, k_ref, v_ref, gm_ref, o_ref = inputs
    sum_ref, later_ref, dq_ref, dk_ref, dv_ref = scratch
    length = q_ref.shape[0]
    zero = jnp.zeros((), BF16)
    scale = jnp.asarray(SCALE, BF16)

    @pl.when(turn == 0)
    def _():
        sum_ref[...] = jnp.zeros_like(sum_ref)

    dk_ref[...] = jnp.zeros_like(dk_ref)
    dv_ref[...] = jnp.zeros_like(dv_ref)

    def head(half, first_head):
        mask = head_mask(half)
        if first_head:
            later_ref[...] = jnp.zeros_like(later_ref)
            row = lax.broadcasted_iota(jnp.int32, (ROWS, ROWS), 0)
            col = lax.broadcasted_iota(jnp.int32, (ROWS, ROWS), 1)
            triangle = (col > row).astype(BF16)
        for first_row in reversed(range(0, length, ROWS)):
            keys = key_count(first_row, slot)
            rows = pl.ds(first_row, ROWS)
            slot_rows = pl.ds(first_row % slot, ROWS)
            grad = jnp.where(mask, gm_ref[rows, :], zero)
            delta = jnp.sum(
                grad.astype(F32) * o_ref[rows, :].astype(F32), axis=-1, keepdims=True
            )
            attention = att_refs[first_row // slot][half, slot_rows, :]
            grad_attention = dot_nt(grad, v_ref[:keys, :])
            grad_logits = attention.astype(F32) * (grad_attention - delta)
            query = jnp.where(mask, q_ref[rows, :], zero) * scale
            if first_head:
                total = sum_ref[rows, :keys] + grad_logits
                grad_selected = -(later_ref[:, :keys] + triangle_sum(triangle, total))
                later_ref[:, :keys] += column_sum(total)
                _, chosen = block_masks(start_ref, length_ref, seq, pieces, first_row, keys)
                positive = dot_nt(query, k_ref[:keys, :]) > 0
                grad_logits = grad_logits + jnp.where(chosen & positive, grad_selected, 0.0)
            else:
                sum_ref[rows, :keys] += grad_logits
            grad_scores = grad_logits.astype(BF16)
            key = jnp.where(mask, k_ref[:keys, :], zero) * scale
            part = dot(grad_scores, key)
            if half == 1:
                dq_ref[rows, :] = part
            else:
                dq_ref[rows, :] += part
            dk_ref[:keys, :] += dot_tn(grad_scores, query)
            dv_ref[:keys, :] += dot_tn(attention, grad)

    head(1, False)

    @pl.when(jnp.logical_not(last))
    def _():
        head(0, False)

    @pl.when(last)
    def _():
        head(0, True)

    for which, ref in enumerate((dq_ref, dk_ref, dv_ref)):
        g_ref[:, which * PAIR : (which + 1) * PAIR] = ref[...].astype(BF16)


def attend_back(
    projected, starts, lengths, grad_mixed, mixed, attention, kept, small, devices, copies
):
    n2, grad_before, hidden, cotangent, grad_proj = kept
    sequences, pieces = starts.shape
    count, columns = projected.shape
    length = count // sequences
    slot = length // pieces
    width = columns // 3
    pairs = width // PAIR
    chunks = hidden.shape[1] // width
    first_step = 2 * chunks + 1
    rows = width // devices
    down_rows = hidden.shape[1] // devices
    lines = small.shape[0]

    def turn(step):
        at = jnp.maximum(step - first_step, 0)
        return (lax.div(at, pairs), pairs - 1 - lax.rem(at, pairs))

    def part(which, of=3, size=1):
        def index(step, a, b):
            seq, pair = turn(step)
            return (seq, of * pair + which)

        return pl.BlockSpec((length, size * PAIR), index)

    def att_index(step, a, b):
        seq, pair = turn(step)
        return (seq, pair, 0, 0)

    att_specs = [pl.BlockSpec((None, 2, slot, (i + 1) * slot), att_index) for i in range(pieces)]
    anywhere = pl.BlockSpec(memory_space=pl.ANY)

    def fixed(shape):
        return pl.BlockSpec(shape, lambda *_: (0,) * len(shape))

    results = [(rows, width), (rows, chunks * width), (down_rows, width), (lines, 1, width)]
    scratch = [
        pltpu.VMEM((length, length), F32),
        pltpu.VMEM((1, length), F32),
        pltpu.VMEM((length, PAIR), F32),
        pltpu.VMEM((length, PAIR), F32),
        pltpu.VMEM((length, PAIR), F32),
        pltpu.VMEM((2, count, width), BF16),
        pltpu.VMEM((2, count, width), BF16),
        pltpu.SemaphoreType.DMA((4,)),
    ]
    for piece_rows in [rows] * chunks + [down_rows // 2] * 2 + [rows]:
        scratch += scatter_scratch(devices, copies, piece_rows, width)
    scratch += reduce_scratch(devices, copies, lines, width)
    return pl.pallas_call(
        functools.partial(
            attend_back_kernel, slot, pieces, chunks, devices, copies, pairs
        ),
        out_shape=[jax.ShapeDtypeStruct((count, columns), BF16)]
        + [jax.ShapeDtypeStruct(shape, F32) for shape in results],
        grid_spec=pltpu.PrefetchScalarGridSpec(
            num_scalar_prefetch=2,
            grid=(first_step + sequences * pairs,),
            in_specs=[part(0), part(1), part(2), part(0, 1), part(0, 1)]
            + att_specs
            + [anywhere] * 6
            + [fixed((lines, 1, width))],
            out_specs=[part(0, 1, 3)] + [fixed(shape) for shape in results],
            scratch_shapes=scratch,
        ),
        compiler_params=comm_params(2, "arbitrary"),
        name="attend_back",
    )(
        starts,
        lengths,
        projected,
        projected,
        projected,
        grad_mixed,
        mixed,
        *attention,
        n2,
        grad_before,
        hidden,
        cotangent,
        mixed,
        grad_proj,
        small,
    )


def gelu_and_slope(values):
    square = values * values
    inner = GELU_IN * values * (1.0 + GELU_CUBE * square)
    bent = jnp.tanh(inner)
    half = 0.5 * (1.0 + bent)
    slope = half + 0.5 * values * (1.0 - bent * bent) * (
        GELU_IN * (1.0 + 3.0 * GELU_CUBE * square)
    )
    return (values * half, slope)


def feed_kernel(
    chunk,
    x_ref,
    mixed_ref,
    cot_ref,
    gain_ref,
    shift_ref,
    up_bias_ref,
    down_bias_ref,
    wo_hbm,
    wu_hbm,
    wd_hbm,
    out_ref,
    gmid_ref,
    gmix_ref,
    small_ref,
    n2_ref,
    hid_ref,
    gb_ref,
    gproj_ref,
    wo_ref,
    wu_ref,
    wd_ref,
    acc_ref,
    gnorm_ref,
    mid_ref,
    load_sem,
):
    step = pl.program_id(0)
    chunks = wu_ref.shape[0]

    def load_out():
        return pltpu.make_async_copy(wo_hbm, wo_ref, load_sem.at[0])

    def load_up(c):
        return pltpu.make_async_copy(
            wu_hbm.at[:, pl.ds(c * chunk, chunk)], wu_ref.at[c], load_sem.at[1 + 2 * c]
        )

    def load_down(c):
        return pltpu.make_async_copy(
            wd_hbm.at[pl.ds(c * chunk, chunk), :], wd_ref.at[c], load_sem.at[2 + 2 * c]
        )

    @pl.when(step == 0)
    def _():
        load_out().start()
        for c in range(chunks):
            load_up(c).start()
            load_down(c).start()
        small_ref[...] = jnp.zeros_like(small_ref)
        load_out().wait()

    mid_ref[...] = x_ref[...].astype(F32) + dot(mixed_ref[...], wo_ref[...])

    @pl.when(step == 0)
    def _():
        for c in range(chunks):
            load_up(c).wait()
            load_down(c).wait()

    normed, _ = normalize(mid_ref[...])
    n2_ref[...] = (normed * gain_ref[...] + shift_ref[...]).astype(BF16)
    acc_ref[...] = jnp.zeros_like(acc_ref)
    gnorm_ref[...] = jnp.zeros_like(gnorm_ref)

    def one_chunk(c, carry):
        columns = pl.ds(pl.multiple_of(c * chunk, chunk), chunk)
        before = dot(n2_ref[...], wu_ref[c]) + up_bias_ref[c]
        hidden, slope = gelu_and_slope(before)
        hidden = hidden.astype(BF16)
        hid_ref[:, columns] = hidden
        acc_ref[...] += dot(hidden, wd_ref[c])
        grad_hidden = dot_nt(cot_ref[...], wd_ref[c]).astype(BF16)
        grad_before = (grad_hidden.astype(F32) * slope).astype(BF16)
        gb_ref[:, columns] = grad_before
        small_ref[3 + c] += column_sum(grad_before.astype(F32))
        gnorm_ref[...] += dot_nt(grad_before, wu_ref[c])
        return carry

    lax.fori_loop(0, chunks, one_chunk, 0)

    out_ref[...] = (mid_ref[...] + (acc_ref[...] + down_bias_ref[...])).astype(BF16)
    grad_normed = gnorm_ref[...]
    normed, inverse = normalize(mid_ref[...])
    cot = cot_ref[...].astype(F32)
    small_ref[0] += column_sum(grad_normed * normed)
    small_ref[1] += column_sum(grad_normed)
    small_ref[2] += column_sum(cot)
    grad_middle = cot + norm_back(grad_normed * gain_ref[...], normed, inverse)
    gmid_ref[...] = grad_middle
    grad_proj = grad_middle.astype(BF16)
    gproj_ref[...] = grad_proj
    gmix_ref[...] = dot_nt(grad_proj, wo_ref[...]).astype(BF16)


def vector_line(row):
    return lambda width: pl.BlockSpec((None, 1, width), lambda *_: (row, 0, 0))


def feed(tokens, mixed, cotangent, vectors, wo, wu, wd):
    count, width = tokens.shape
    hidden = wu.shape[1]
    block = 512
    chunk = width
    chunks = hidden // chunk
    rows = pl.BlockSpec((block, width), lambda i: (i, 0))
    anywhere = pl.BlockSpec(memory_space=pl.ANY)
    wide = pl.BlockSpec((block, hidden), lambda i: (i, 0))

    def low(columns):
        return jax.ShapeDtypeStruct((count, columns), BF16)

    return pl.pallas_call(
        functools.partial(feed_kernel, chunk),
        out_shape=[
            low(width),
            jax.ShapeDtypeStruct((count, width), F32),
            low(width),
            jax.ShapeDtypeStruct((3 + chunks, 1, width), F32),
            low(width),
            low(hidden),
            low(hidden),
            low(width),
        ],
        grid=(count // block,),
        in_specs=[
            rows,
            rows,
            rows,
            vector_line(GAIN2)(width),
            vector_line(SHIFT2)(width),
            pl.BlockSpec((chunks, 1, chunk), lambda i: (0, 0, 0)),
            vector_line(DOWN_BIAS)(width),
            anywhere,
            anywhere,
            anywhere,
        ],
        out_specs=[
            rows,
            rows,
            rows,
            pl.BlockSpec((3 + chunks, 1, width), lambda i: (0, 0, 0)),
            rows,
            wide,
            wide,
            rows,
        ],
        scratch_shapes=[
            pltpu.VMEM(wo.shape, BF16),
            pltpu.VMEM((chunks, width, chunk), BF16),
            pltpu.VMEM((chunks, chunk, width), BF16),
            pltpu.VMEM((block, width), F32),
            pltpu.VMEM((block, width), F32),
            pltpu.VMEM((block, width), F32),
            pltpu.SemaphoreType.DMA((1 + 2 * chunks,)),
        ],
        compiler_params=params("arbitrary"),
        name="feed",
    )(
        tokens,
        mixed,
        cotangent,
        vectors,
        vectors,
        vectors,
        vectors,
        wo,
        wu,
        wd,
    )


def input_kernel(
    count,
    copies,
    gmid_ref,
    gain_ref,
    shift_ref,
    x_hbm,
    g_hbm,
    w_hbm,
    gx_ref,
    gw_ref,
    gsmall_ref,
    x_ref,
    n1_ref,
    g_ref,
    w_ref,
    small_ref,
    load_sem,
    *rest,
):
    step = pl.program_id(0)
    total, width = x_ref.shape
    block = gx_ref.shape[0]
    place = Place(count, copies)
    parts = []
    for which in range(3):

        def write(value, which=which):
            for i in range(width // PAIR):
                at = which * (width // PAIR) + i
                first = (at % 3) * width + (at // 3) * PAIR
                gw_ref[:, first : first + PAIR] = value[:, i * PAIR : (i + 1) * PAIR]

        parts.append(Scatter(place, rest[6 * which : 6 * which + 6], write))
    small = Reduce(place, rest[18:22], gsmall_ref)

    def load_x():
        return pltpu.make_async_copy(x_hbm, x_ref, load_sem.at[0])

    def load_grad(which):
        source = g_hbm.at[:, pl.ds(which * width, width)]
        return pltpu.make_async_copy(source, g_ref.at[which], load_sem.at[1 + which])

    def load_weight():
        return pltpu.make_async_copy(w_hbm, w_ref, load_sem.at[4])

    def begin():
        load_x().start()
        for which in range(3):
            load_grad(which).start()
        load_weight().start()
        place.meet(copies=True)
        small_ref[...] = jnp.zeros_like(small_ref)
        load_x().wait()

        def norm_rows(i, carry):
            at = pl.ds(pl.multiple_of(i * 256, 256), 256)
            normed, _ = normalize(x_ref[at, :].astype(F32))
            n1_ref[at, :] = (normed * gain_ref[...] + shift_ref[...]).astype(BF16)
            return carry

        lax.fori_loop(0, total // 256, norm_rows, 0)

    table = schedule(
        (0, begin),
        (1, parts[0].after_cores),
        (2, parts[1].after_cores),
        (3, parts[2].after_cores),
        (4, parts[0].after_columns),
        (5, parts[1].after_columns),
        (6, parts[2].after_columns),
        (6, parts[0].after_levels),
    )
    at_steps(step, table)

    @pl.when(step < 3)
    def _():
        for which in range(3):

            @pl.when(step == which)
            def _(which=which):
                load_grad(which).wait()

        grad = dot_tn(n1_ref[...], g_ref[step]).astype(BF16)
        for which in range(3):

            @pl.when(step == which)
            def _(which=which):
                rows = width // count
                for i in range(count):
                    parts[which].held[i] = grad[i * rows : (i + 1) * rows, :]
                parts[which].start()

    @pl.when(step == 3)
    def _():
        load_weight().wait()

    @pl.when(step >= 3)
    def _():
        at = pl.ds(pl.multiple_of((step - 3) * block, block), block)
        normed, inverse = normalize(x_ref[at, :].astype(F32))
        grad_normed = None
        for which in range(3):
            part = dot_nt(g_ref[which, at, :], w_ref[:, which * width : (which + 1) * width])
            grad_normed = part if grad_normed is None else grad_normed + part
        small_ref[0] += column_sum(grad_normed * normed)
        small_ref[1] += column_sum(grad_normed)
        gx_ref[...] = gmid_ref[...] + norm_back(grad_normed * gain_ref[...], normed, inverse)

    @pl.when(step == pl.num_programs(0) - 1)
    def _():
        small.start(small_ref[...])
        parts[1].after_levels()
        small.after_cores()
        parts[0].after_copies()
        small.after_columns()
        parts[2].after_levels()
        parts[1].after_copies()
        small.after_levels()
        parts[2].after_copies()
        small.after_copies()
        for part in parts + [small]:
            part.drain()


def input_back(tokens, grad_middle, grads, vectors, weight, devices, copies):
    count, width = tokens.shape
    block = 512
    shard = width // devices
    rows = pl.BlockSpec((block, width), lambda i: (jnp.maximum(i - 3, 0), 0))
    anywhere = pl.BlockSpec(memory_space=pl.ANY)
    scratch = [
        pltpu.VMEM((count, width), BF16),
        pltpu.VMEM((count, width), BF16),
        pltpu.VMEM((3, count, width), BF16),
        pltpu.VMEM(weight.shape, BF16),
        pltpu.VMEM((2, 1, width), F32),
        pltpu.SemaphoreType.DMA((5,)),
    ]
    for _ in range(3):
        scratch += scatter_scratch(devices, copies, shard, width)
    scratch += reduce_scratch(devices, copies, 2, width)
    return pl.pallas_call(
        functools.partial(input_kernel, devices, copies),
        out_shape=[
            jax.ShapeDtypeStruct((count, width), F32),
            jax.ShapeDtypeStruct((shard, 3 * width), F32),
            jax.ShapeDtypeStruct((2, 1, width), F32),
        ],
        grid=(3 + count // block,),
        in_specs=[rows, vector_line(GAIN1)(width), vector_line(SHIFT1)(width)]
        + [anywhere] * 3,
        out_specs=[
            rows,
            pl.BlockSpec((shard, 3 * width), lambda i: (0, 0)),
            pl.BlockSpec((2, 1, width), lambda i: (0, 0, 0)),
        ],
        scratch_shapes=scratch,
        compiler_params=comm_params(3, "arbitrary"),
        name="input_back",
    )(grad_middle, vectors, vectors, tokens, grads, weight)


def local(
    tokens,
    piece_start,
    piece_length,
    query_key_value,
    output_weight,
    up_weight,
    down_weight,
    first_gain,
    first_shift,
    second_gain,
    second_shift,
    up_bias,
    down_bias,
    cotangent,
):
    width = tokens.shape[1]
    devices, copies = (lax.axis_size("fsdp"), lax.axis_size("rep"))
    index = lax.axis_index("fsdp")

    def placed(vector):
        flat = jnp.zeros((devices * vector.shape[0],), BF16)
        flat = lax.dynamic_update_slice(flat, vector, (index * vector.shape[0],))
        return flat.reshape(-1, width)

    own = [up_bias, first_gain, first_shift, second_gain, second_shift, down_bias]
    own = jnp.concatenate([placed(vector) for vector in own], axis=0)
    own = jnp.pad(own, ((0, LINES - own.shape[0]), (0, 0)))

    (projected, mixed), attention, (n1, vectors, wqkv, wo, wu, wd) = front(
        tokens,
        piece_start,
        piece_length,
        query_key_value,
        own,
        output_weight,
        up_weight,
        down_weight,
        devices,
        copies,
    )
    block_output, grad_middle, grad_mixed, small2, n2, hidden, grad_before, grad_proj = feed(
        tokens, mixed, cotangent, vectors, wo, wu, wd
    )
    grads, gwo, gwu, gwd, small2 = attend_back(
        projected,
        piece_start,
        piece_length,
        grad_mixed,
        mixed,
        attention,
        (n2, grad_before, hidden, cotangent, grad_proj),
        small2,
        devices,
        copies,
    )
    grad_tokens, gwqkv, small1 = input_back(
        tokens, grad_middle, grads, vectors, wqkv, devices, copies
    )

    def mine(values):
        values = values.reshape(-1)
        size = values.shape[0] // devices
        return lax.dynamic_slice(values, (index * size,), (size,))

    return (
        block_output,
        grad_tokens,
        gwqkv,
        gwo,
        gwu,
        gwd,
        mine(small1[0]),
        mine(small1[1]),
        mine(small2[0]),
        mine(small2[1]),
        mine(small2[3:]),
        mine(small2[2]),
    )


def solution(mesh):
    rows = P(("fsdp", "rep"), None)
    matrix = P("fsdp", None)
    vector = P("fsdp")
    return jax.shard_map(
        local,
        mesh=mesh,
        in_specs=(rows,) * 3 + (matrix,) * 4 + (vector,) * 6 + (rows,),
        out_specs=(rows,) * 2 + (matrix,) * 4 + (vector,) * 6,
        check_vma=False,
    )
```

```python
import functools

import jax
import jax.numpy as jnp
from jax import lax
from jax.experimental import pallas as pl
from jax.experimental.pallas import tpu as pltpu
from jax.sharding import PartitionSpec as P

HEAD_DIM = 64
PAIR = 2 * HEAD_DIM
ROWS = 256
MASKED_VALUE = -1e30
EPSILON = 1e-05
SCALE = HEAD_DIM**-0.5
GAIN1, SHIFT1, GAIN2, SHIFT2, DOWN_BIAS = (4, 5, 6, 7, 8)
LINES = 16
FRONT_TABLE = ((2, 4, 5, 7, 8), (4, 6, 7, 9, 10), (6, 8, 9, 11, 11))
BACK_TABLE = ((0, 3, 6, 8), (0, 5, 8, 10), (1, 6, 9, 11), (3, 7, 10, 11), (5, 8, 10, 12), (7, 9, 11, 13), (9, 10, 12, 14))
GELU_IN = 0.7978845608028654
GELU_CUBE = 0.044715
VMEM_LIMIT = 67043328

F32 = jnp.float32
BF16 = jnp.bfloat16


def dot(left, right):
    return lax.dot_general(left, right, (((1,), (0,)), ((), ())), preferred_element_type=F32)


def dot_nt(left, right):
    return lax.dot_general(left, right, (((1,), (1,)), ((), ())), preferred_element_type=F32)


def dot_tn(left, right):
    return lax.dot_general(left, right, (((0,), (0,)), ((), ())), preferred_element_type=F32)


def row_mean(values):
    return jnp.mean(values, axis=-1, keepdims=True)


def normalize(values):
    center = values - row_mean(values)
    inverse = lax.rsqrt(row_mean(center * center) + EPSILON)
    return (center * inverse, inverse)


def norm_back(grad, normed, inverse):
    return (grad - row_mean(grad) - normed * row_mean(grad * normed)) * inverse


def column_sum(values):
    return jnp.sum(values, axis=0, keepdims=True)


def params(*semantics):
    return pltpu.CompilerParams(dimension_semantics=semantics, vmem_limit_bytes=VMEM_LIMIT)


def comm_params(number, *semantics):
    return pltpu.CompilerParams(
        dimension_semantics=semantics,
        vmem_limit_bytes=VMEM_LIMIT,
        collective_id=number,
        has_side_effects=True,
    )


MESH = pl.DeviceIdType.MESH
LEVELS = 4
CORES = 2


class Place:
    def __init__(self, count, copies):
        self.count, self.copies = (count, copies)
        self.columns = count // (LEVELS * CORES)
        self.index = lax.axis_index("fsdp")
        self.rep = lax.axis_index("rep")
        self.core = lax.rem(self.index, CORES)
        chip = lax.div(self.index, CORES)
        self.column = lax.rem(chip, self.columns)
        self.level = lax.div(chip, self.columns)
        self.half = lax.rem(self.rep, 2)

    def block(self, up=0, across=0, other=0):
        level = lax.rem(self.level + (up + LEVELS), LEVELS)
        column = lax.rem(self.column + (across + self.columns), self.columns)
        core = lax.rem(self.core + other, CORES)
        return (level * self.columns + column) * CORES + core

    def device(self, up=0, across=0, other=0, copy=0):
        return (self.block(up, across, other), lax.rem(self.rep + copy, self.copies))

    def twin(self):
        return (self.index, self.rep + 1 - 2 * self.half)

    def meet(self, twin=False, copies=False):
        others = [self.device(up=up) for up in range(1, LEVELS)]
        others += [self.device(across=across) for across in range(1, self.columns)]
        others += [self.device(other=1)]
        if twin:
            others += [self.twin()]
        if copies:
            others += [self.device(copy=copy) for copy in range(1, self.copies)]
        barrier = pltpu.get_barrier_semaphore()
        for other in others:
            pl.semaphore_signal(barrier, inc=1, device_id=other, device_id_type=MESH)
        pl.semaphore_wait(barrier, len(others))


def send(source, target, sems, slot, device):
    return pltpu.make_async_remote_copy(
        src_ref=source,
        dst_ref=target,
        send_sem=sems.at[2 * slot],
        recv_sem=sems.at[2 * slot + 1],
        device_id=device,
        device_id_type=MESH,
    )


def gather_sems(count):
    return 2 * (LEVELS - 1 + 3 * count // CORES) + 1


class Gather:
    def __init__(self, place, source, target, rows, shared, sems):
        self.place, self.source, self.target = (place, source, target)
        self.sems, self.shared = (sems, shared)
        if shared:
            third = rows // 3
            half = place.half
            self.part = pl.ds(pl.multiple_of(half * third, third), 2 * third)
            self.give = pl.ds(pl.multiple_of(half * (2 * third), third), third)
        else:
            self.part = pl.ds(0, rows)

    def held(self, up, across):
        if up == 0 and across == 0:
            return self.source
        return self.target(self.place.block(-up, -across))

    def slot(self, phase, up, across):
        area = self.place.count // CORES
        return LEVELS - 1 + phase * area + across * LEVELS + up

    def level_copies(self):
        target = self.target(self.place.block()).at[self.part, :]
        source = self.source.at[self.part, :]
        return [
            send(source, target, self.sems, up - 1, self.place.device(up=up))
            for up in range(1, LEVELS)
        ]

    def column_copies(self, ups):
        place = self.place
        return [
            send(
                self.held(up, 0).at[self.part, :],
                self.target(place.block(-up)).at[self.part, :],
                self.sems,
                self.slot(0, up, across),
                place.device(across=across),
            )
            for up in ups
            for across in range(1, place.columns)
        ]

    def twin_copies(self, acrosses):
        if not self.shared:
            return []
        place = self.place
        return [
            send(
                self.held(up, across).at[self.give, :],
                self.target(place.block(-up, -across)).at[self.give, :],
                self.sems,
                self.slot(1, up, across),
                place.twin(),
            )
            for across in acrosses
            for up in range(LEVELS)
            if up or across
        ]

    def core_copies(self, first):
        place = self.place
        return [
            send(
                self.held(up, across),
                self.target(place.block(-up, -across)),
                self.sems,
                self.slot(2, up, across),
                place.device(other=1),
            )
            for across in range(place.columns)
            for up in range(LEVELS)
            if (up == 0 and across == 0) == first
        ]

    def own(self):
        last = gather_sems(self.place.count) - 1
        return pltpu.make_async_copy(
            self.source, self.target(self.place.block()), self.sems.at[last]
        )

    def start(self):
        for copy in self.level_copies() + self.core_copies(True):
            copy.start()
        self.own().start()

    def after_levels(self):
        for copy in self.column_copies([0]):
            copy.start()
        for copy in self.level_copies():
            copy.wait_recv()
        for copy in self.column_copies(range(1, LEVELS)) + self.twin_copies([0]):
            copy.start()

    def after_columns(self):
        for copy in self.column_copies(range(LEVELS)):
            copy.wait_recv()
        for copy in self.twin_copies(range(1, self.place.columns)):
            copy.start()
        if not self.shared:
            self.to_cores()

    def after_twins(self):
        for copy in self.twin_copies(range(self.place.columns)):
            copy.wait_recv()
        if self.shared:
            self.to_cores()

    def to_cores(self):
        for copy in self.core_copies(False):
            copy.start()

    def finish(self):
        for copy in self.core_copies(True) + self.core_copies(False):
            copy.wait_recv()
        self.own().wait()

    def drain(self):
        columns = range(self.place.columns)
        copies = self.level_copies() + self.column_copies(range(LEVELS))
        copies += self.twin_copies(columns) + self.core_copies(True) + self.core_copies(False)
        for copy in copies:
            copy.wait_send()


def scatter_slots(count, copies):
    area = count // CORES
    return area + (area - LEVELS) + (LEVELS - 1) + (copies - 1)


def scatter_scratch(count, copies, rows, columns):
    across = count // (CORES * LEVELS)
    return [
        pltpu.VMEM((count, rows, columns), BF16),
        pltpu.VMEM((across, LEVELS, rows, columns), BF16),
        pltpu.VMEM((max(across - 1, 1), LEVELS, rows, columns), BF16),
        pltpu.VMEM((LEVELS - 1, rows, columns), BF16),
        pltpu.VMEM((copies, rows, columns), BF16),
        pltpu.SemaphoreType.DMA((2 * scatter_slots(count, copies),)),
    ]


def add_low(left, right):
    return (left.astype(F32) + right.astype(F32)).astype(BF16)


class Scatter:
    def __init__(self, place, refs, write):
        self.place, self.write = (place, write)
        self.held, self.from_core, self.from_column, self.from_level, self.parts, self.sems = refs
        self.area = place.count // CORES

    def core_copies(self):
        place = self.place
        return [
            send(
                self.held.at[place.block(up, across, 1)],
                self.from_core.at[across, up],
                self.sems,
                across * LEVELS + up,
                place.device(other=1),
            )
            for across in range(place.columns)
            for up in range(LEVELS)
        ]

    def column_copies(self):
        place = self.place
        return [
            send(
                self.held.at[place.block(up, across)],
                self.from_column.at[across - 1, up],
                self.sems,
                self.area + (across - 1) * LEVELS + up,
                place.device(across=across),
            )
            for across in range(1, place.columns)
            for up in range(LEVELS)
        ]

    def level_copies(self):
        place = self.place
        base = 2 * self.area - LEVELS
        return [
            send(
                self.held.at[place.block(up)],
                self.from_level.at[up - 1],
                self.sems,
                base + up - 1,
                place.device(up=up),
            )
            for up in range(1, LEVELS)
        ]

    def rep_copies(self):
        place = self.place
        base = 2 * self.area - 1
        mine = self.parts.at[place.rep]
        return [
            send(mine, mine, self.sems, base + copy - 1, place.device(copy=copy))
            for copy in range(1, place.copies)
        ]

    def start(self):
        for copy in self.core_copies():
            copy.start()

    def start_blocks(self, first, blocks):
        place = self.place
        for i in range(blocks):
            block = first + i
            core = lax.rem(block, CORES)
            chip = lax.div(block, CORES)
            across = lax.rem(
                lax.rem(chip, place.columns) - place.column + place.columns, place.columns
            )
            up = lax.rem(lax.div(chip, place.columns) - place.level + LEVELS, LEVELS)

            @pl.when(core != place.core)
            def _(block=block, across=across, up=up):
                send(
                    self.held.at[block],
                    self.from_core.at[across, up],
                    self.sems,
                    across * LEVELS + up,
                    place.device(other=1),
                ).start()

    def after_cores(self):
        place = self.place
        for copy in self.core_copies():
            copy.wait_recv()

        def add(i, carry):
            across, up = (lax.div(i, LEVELS), lax.rem(i, LEVELS))
            block = place.block(up, across)
            self.held[block] = add_low(self.held[block], self.from_core[across, up])
            return carry

        lax.fori_loop(0, self.area, add, 0)
        for copy in self.column_copies():
            copy.start()

    def after_columns(self):
        place = self.place
        for copy in self.column_copies():
            copy.wait_recv()

        def add(up, carry):
            block = place.block(up)
            total = self.held[block].astype(F32)
            for across in range(place.columns - 1):
                total = total + self.from_column[across, up].astype(F32)
            self.held[block] = total.astype(BF16)
            return carry

        lax.fori_loop(0, LEVELS, add, 0)
        for copy in self.level_copies():
            copy.start()

    def after_levels(self):
        for copy in self.level_copies():
            copy.wait_recv()
        total = self.held[self.place.block()].astype(F32)
        for level in range(LEVELS - 1):
            total = total + self.from_level[level].astype(F32)
        self.parts[self.place.rep] = total.astype(BF16)
        for copy in self.rep_copies():
            copy.start()

    def after_copies(self):
        for copy in self.rep_copies():
            copy.wait_recv()
        total = self.parts[0].astype(F32)
        for rep in range(1, self.place.copies):
            total = total + self.parts[rep].astype(F32)
        self.write(total)

    def drain(self):
        copies = self.core_copies() + self.column_copies() + self.level_copies()
        for copy in copies + self.rep_copies():
            copy.wait_send()


def reduce_scratch(count, copies, lines, width):
    across = count // (CORES * LEVELS)
    slots = 1 + (across - 1) + (LEVELS - 1) + (copies - 1)
    return [
        pltpu.VMEM((3, lines, 1, width), F32),
        pltpu.VMEM((1 + across - 1 + LEVELS - 1, lines, 1, width), F32),
        pltpu.VMEM((copies, lines, 1, width), F32),
        pltpu.SemaphoreType.DMA((2 * slots,)),
    ]


class Reduce:
    def __init__(self, place, refs, out):
        self.place, self.out = (place, out)
        self.sums, self.landed, self.parts, self.sems = refs

    def group(self, phase):
        place = self.place
        if phase == 0:
            targets = [place.device(other=1)]
            first = 0
        elif phase == 1:
            targets = [place.device(across=across) for across in range(1, place.columns)]
            first = 1
        else:
            targets = [place.device(up=up) for up in range(1, LEVELS)]
            first = place.columns
        return [
            send(self.sums.at[phase], self.landed.at[first + i], self.sems, first + i, target)
            for i, target in enumerate(targets)
        ]

    def rep_copies(self):
        place = self.place
        base = place.columns + LEVELS - 1
        mine = self.parts.at[place.rep]
        return [
            send(mine, mine, self.sems, base + copy - 1, place.device(copy=copy))
            for copy in range(1, place.copies)
        ]

    def start(self, value):
        self.sums[0] = value
        for copy in self.group(0):
            copy.start()

    def next(self, phase):
        copies = self.group(phase)
        for copy in copies:
            copy.wait_recv()
        first = (0, 1, self.place.columns)[phase]
        total = self.sums[phase]
        for i in range(len(copies)):
            total = total + self.landed[first + i]
        if phase < 2:
            self.sums[phase + 1] = total
            for copy in self.group(phase + 1):
                copy.start()
        else:
            self.parts[self.place.rep] = total
            for copy in self.rep_copies():
                copy.start()

    def after_cores(self):
        self.next(0)

    def after_columns(self):
        self.next(1)

    def after_levels(self):
        self.next(2)

    def after_copies(self):
        for copy in self.rep_copies():
            copy.wait_recv()
        total = self.parts[0]
        for rep in range(1, self.place.copies):
            total = total + self.parts[rep]
        self.out[...] = total

    def drain(self):
        for copy in self.group(0) + self.group(1) + self.group(2) + self.rep_copies():
            copy.wait_send()


def label_of(position, start_ref, length_ref, seq, pieces):
    label = jnp.zeros(position.shape, jnp.int32)
    for piece in range(pieces):
        start = start_ref[seq, piece]
        inside = (position >= start) & (position < start + length_ref[seq, piece])
        label = jnp.where(inside, piece + 1, label)
    return label


def key_count(first_row, slot):
    return (first_row // slot + 1) * slot


def block_masks(start_ref, length_ref, seq, pieces, first_row, keys):
    query_pos = first_row + lax.broadcasted_iota(jnp.int32, (ROWS, 1), 0)
    key_pos = lax.broadcasted_iota(jnp.int32, (1, keys), 1)
    query_label = label_of(query_pos, start_ref, length_ref, seq, pieces)
    key_label = label_of(key_pos, start_ref, length_ref, seq, pieces)
    query_label = jnp.where(query_label > 0, query_label, -1)
    allowed = (key_pos <= query_pos) | (query_label == key_label)
    chosen = allowed & (key_pos != 0) & (key_pos != query_pos)
    return (allowed, chosen)


def triangle_sum(triangle, values):
    upper = values.astype(BF16)
    rest = values - upper.astype(F32)
    middle = rest.astype(BF16)
    lower = (rest - middle.astype(F32)).astype(BF16)
    return dot(triangle, upper) + dot(triangle, middle) + dot(triangle, lower)


def head_mask(half):
    lane = lax.broadcasted_iota(jnp.int32, (1, PAIR), 1)
    return (lane >= HEAD_DIM) if half else (lane < HEAD_DIM)


def at_steps(step, table):
    for when in sorted(set(table)):
        @pl.when(step == when)
        def _(when=when):
            for action in table[when]:
                action()


def schedule(*entries):
    table = {}
    for when, action in entries:
        table.setdefault(when, []).append(action)
    return table


def pair_groups(pairs):
    groups, at = ([], 0)
    for size in [1, 1] + [2] * pairs:
        if at < pairs:
            groups.append(range(at, min(at + size, pairs)))
            at += size
    return groups


def front_kernel(
    slot,
    pieces,
    count,
    copies,
    pairs,
    start_ref,
    length_ref,
    x_hbm,
    wqkv_hbm,
    vec_hbm,
    wo_hbm,
    wu_hbm,
    wd_hbm,
    qkv_ref,
    o_ref,
    inv_ref,
    *rest,
):
    att_refs, rest = (rest[:pieces], rest[pieces:])
    n1_hbm, vec_ref, full_w, full_o, full_u, full_d = rest[:6]
    x_ref, n1_ref, all_ref, stage_ref, w_ref, bias_ref, prefix_ref = rest[6:13]
    stage_sems, load_sems, vec_sems, w_sems, rest_sems = rest[13:]
    pair, seq = (pl.program_id(0), pl.program_id(1))
    sequences = pl.num_programs(1)
    step = pair * sequences + seq
    length = qkv_ref.shape[0]
    width = x_ref.shape[1]
    sequence_count = x_ref.shape[0] // length
    lines = vec_hbm.shape[0]
    zero = jnp.zeros((), BF16)
    place = Place(count, copies)
    twins = copies % 2 == 0

    def whole(ref, rows, cut, i, columns):
        def target(block):
            first = pl.multiple_of(block * (rows * cut) + i * rows, rows)
            return ref.at[pl.ds(first, rows), columns]

        return target

    vec = Gather(place, vec_hbm, whole(all_ref, lines, 1, 0, pl.ds(0, width)), lines, False, vec_sems)
    groups = pair_groups(pairs)
    rows = wqkv_hbm.shape[0]
    gathers = []
    for i, group in enumerate(groups):
        columns = pl.ds(group[0] * 3 * PAIR, len(group) * 3 * PAIR)
        shared = twins and i > 2 and rows % 48 == 0
        gathers.append(
            Gather(
                place,
                stage_ref.at[:, columns],
                whole(full_w, rows, 1, 0, columns),
                rows,
                shared,
                w_sems.at[i],
            )
        )
    cuts = []
    for shard, full, cut_rows, cut_columns in (
        (wo_hbm, full_o, 1, 1),
        (wu_hbm, full_u, 1, 2),
        (wd_hbm, full_d, 2, 1),
    ):
        rows, columns = (shard.shape[0] // cut_rows, shard.shape[1] // cut_columns)
        for i in range(cut_rows):
            for j in range(cut_columns):
                across = pl.ds(j * columns, columns)
                source = shard.at[pl.ds(i * rows, rows), across]
                target = whole(full, rows, cut_rows, i, across)
                cuts.append(Gather(place, source, target, rows, twins, rest_sems.at[len(cuts)]))

    def stage_copies():
        found = []
        for p in range(pairs):
            for which in range(3):
                at = 3 * p + which
                found.append(
                    pltpu.make_async_copy(
                        wqkv_hbm.at[:, pl.ds(which * width + p * PAIR, PAIR)],
                        stage_ref.at[:, pl.ds(at * PAIR, PAIR)],
                        stage_sems.at[at],
                    )
                )
        return found

    def load_x():
        return pltpu.make_async_copy(x_hbm, x_ref, load_sems.at[0])

    def keep_n1():
        return pltpu.make_async_copy(n1_ref, n1_hbm, load_sems.at[1])

    def load_w(p):
        return pltpu.make_async_copy(
            full_w.at[:, pl.ds(p * 3 * PAIR, 3 * PAIR)], w_ref.at[p % 2], load_sems.at[2 + p % 2]
        )

    def norm_rows(which):
        gain, shift = (vec_ref[GAIN1], vec_ref[SHIFT1])

        def body(i, carry):
            at = pl.ds(pl.multiple_of(which * length + i * ROWS, ROWS), ROWS)
            normed, _ = normalize(x_ref[at, :].astype(F32))
            n1_ref[at, :] = (normed * gain + shift).astype(BF16)
            return carry

        lax.fori_loop(0, length // ROWS, body, 0)
        if which == sequence_count - 1:
            keep_n1().start()

    def begin():
        for copy in stage_copies():
            copy.start()
        load_x().start()
        place.meet(twin=twins)
        vec.start()
        for copy in stage_copies():
            copy.wait()
        for gather in gathers + cuts:
            gather.start()
        vec.after_levels()
        gathers[0].after_levels()
        vec.after_columns()
        gathers[0].after_columns()
        gathers[1].after_levels()
        vec.finish()
        vectors = all_ref[0:lines, :].astype(F32)
        for other in range(1, count):
            vectors = vectors + all_ref[other * lines : (other + 1) * lines, :].astype(F32)
        for line in range(lines):
            vec_ref[line] = vectors[line : line + 1, :]
        load_x().wait()
        gathers[0].finish()
        load_w(0).start()
        norm_rows(0)
        gathers[1].after_columns()
        load_w(0).wait()

    def ready(p):
        for group, gather in zip(groups, gathers):
            if p == group[0]:
                gather.finish()
        load_w(p).start()

    s = sequence_count
    entries = [(0, begin)]
    entries += [(which, functools.partial(norm_rows, which)) for which in range(1, s)]
    entries += [
        (1, gathers[2].after_levels),
        (2, gathers[2].after_columns),
    ]
    for i, gather in enumerate(gathers[3:]):
        need = groups[3 + i][0] * s - 1
        entries += [
            (need - 4, gather.after_levels),
            (need - 3, gather.after_columns),
            (need - 2, gather.after_twins),
        ]
    for p in range(1, pairs):
        entries.append((p * s - 1, functools.partial(ready, p)))
        entries.append((p * s, load_w(p).wait))
    for i, cut in enumerate(cuts):
        entries += [
            (FRONT_TABLE[0][i], cut.after_levels),
            (FRONT_TABLE[1][i], cut.after_columns),
            (FRONT_TABLE[2][i], cut.after_twins),
        ]
    at_steps(step, schedule(*entries))

    seq_rows = pl.ds(pl.multiple_of(seq * length, length), length)
    qkv_ref[...] = dot(n1_ref[seq_rows, :], w_ref[lax.rem(pair, 2)]).astype(BF16)

    @pl.when(pair == 0)
    def _():
        prefix_ref[...] = jnp.zeros_like(prefix_ref)
        row = lax.broadcasted_iota(jnp.int32, (ROWS, ROWS), 0)
        col = lax.broadcasted_iota(jnp.int32, (ROWS, ROWS), 1)
        triangle = (col < row).astype(BF16)
        for first_row in range(0, length, ROWS):
            keys = key_count(first_row, slot)
            at = pl.ds(first_row, ROWS)
            query = jnp.where(head_mask(0), qkv_ref[at, :PAIR], zero)
            scores = dot_nt(query, qkv_ref[:keys, PAIR : 2 * PAIR]) * SCALE
            allowed, chosen = block_masks(start_ref, length_ref, seq, pieces, first_row, keys)
            selected = jnp.where(chosen & (scores > 0), scores, 0.0)
            penalty = prefix_ref[:, :keys] + triangle_sum(triangle, selected)
            bias_ref[seq, at, :keys] = jnp.where(allowed, -penalty, MASKED_VALUE)
            prefix_ref[:, :keys] += column_sum(selected)

    def logits_of(first_row, half):
        keys = key_count(first_row, slot)
        at = pl.ds(first_row, ROWS)
        query = jnp.where(head_mask(half), qkv_ref[at, :PAIR], zero) * jnp.asarray(SCALE, BF16)
        return dot_nt(query, qkv_ref[:keys, PAIR : 2 * PAIR]) + bias_ref[seq, at, :keys]

    def raise_and_mix(first_row, half, logits):
        keys = key_count(first_row, slot)
        largest = jnp.max(logits, axis=-1, keepdims=True)
        raised = jnp.exp(logits - largest)
        inverse = 1.0 / jnp.sum(raised, axis=-1, keepdims=True)
        low = raised.astype(BF16)
        att_refs[first_row // slot][half, pl.ds(first_row % slot, ROWS), :] = low
        value = jnp.where(head_mask(half), qkv_ref[:keys, 2 * PAIR :], zero)
        return (dot(low, value), inverse)

    def finish_rows(first_row, halves):
        (mixed0, inverse0), (mixed1, inverse1) = halves
        at = pl.ds(first_row, ROWS)
        inverse = jnp.where(head_mask(0), inverse0, inverse1)
        inv_ref[at, :] = inverse
        o_ref[at, :] = ((mixed0 + mixed1) * inverse).astype(BF16)

    blocks = [(first_row, half) for first_row in range(0, length, ROWS) for half in range(2)]
    halves, ahead = ([], logits_of(*blocks[0]))
    for i, block in enumerate(blocks):
        logits = ahead
        if i + 1 < len(blocks):
            ahead = logits_of(*blocks[i + 1])
        halves.append(raise_and_mix(*block, logits))
        if len(halves) == 2:
            finish_rows(block[0], halves)
            halves = []

    @pl.when(step == pairs * sequence_count - 1)
    def _():
        for cut in cuts:
            cut.finish()
        for gather in [vec] + gathers + cuts:
            gather.drain()
        keep_n1().wait()


def front(tokens, starts, lengths, wqkv, vectors, wo, wu, wd, devices, copies):
    sequences, pieces = starts.shape
    count, width = tokens.shape
    length = count // sequences
    slot = length // pieces
    pairs = width // PAIR
    lines = vectors.shape[0]
    anywhere = pl.BlockSpec(memory_space=pl.ANY)

    def low(*shape):
        return jax.ShapeDtypeStruct(shape, BF16)

    att_shapes = [low(sequences, 2 * pairs, slot, (i + 1) * slot) for i in range(pieces)]
    att_specs = [
        pl.BlockSpec((None, 2, slot, (i + 1) * slot), lambda p, s, a, b: (s, p, 0, 0))
        for i in range(pieces)
    ]
    weights = [low(devices * w.shape[0], w.shape[1]) for w in (wqkv, wo, wu, wd)]
    sems = gather_sems(devices)
    results = pl.pallas_call(
        functools.partial(front_kernel, slot, pieces, devices, copies, pairs),
        out_shape=[
            low(count, 3 * width),
            low(count, width),
            jax.ShapeDtypeStruct((count, width), F32),
        ]
        + att_shapes
        + [low(count, width), jax.ShapeDtypeStruct((lines, 1, width), F32)]
        + weights,
        grid_spec=pltpu.PrefetchScalarGridSpec(
            num_scalar_prefetch=2,
            grid=(pairs, sequences),
            in_specs=[anywhere] * 6,
            out_specs=[
                pl.BlockSpec((length, 3 * PAIR), lambda p, s, a, b: (s, p)),
                pl.BlockSpec((length, PAIR), lambda p, s, a, b: (s, p)),
                pl.BlockSpec((length, PAIR), lambda p, s, a, b: (s, p)),
            ]
            + att_specs
            + [anywhere, pl.BlockSpec((lines, 1, width), lambda *_: (0, 0, 0))]
            + [anywhere] * 4,
            scratch_shapes=[
                pltpu.VMEM((count, width), BF16),
                pltpu.VMEM((count, width), BF16),
                pltpu.VMEM((devices * lines, width), BF16),
                pltpu.VMEM(wqkv.shape, BF16),
                pltpu.VMEM((2, width, 3 * PAIR), BF16),
                pltpu.VMEM((sequences, length, length), F32),
                pltpu.VMEM((1, length), F32),
                pltpu.SemaphoreType.DMA((3 * pairs,)),
                pltpu.SemaphoreType.DMA((4,)),
                pltpu.SemaphoreType.DMA((sems,)),
                pltpu.SemaphoreType.DMA((len(pair_groups(pairs)), sems)),
                pltpu.SemaphoreType.DMA((5, sems)),
            ],
        ),
        compiler_params=comm_params(1, "arbitrary", "arbitrary"),
        name="front",
    )(starts, lengths, tokens, wqkv, vectors, wo, wu, wd)
    return (results[:3], results[3 : 3 + pieces], results[3 + pieces :])


TAIL = 2


def attend_back_kernel(
    slot,
    pieces,
    chunks,
    count,
    copies,
    pairs,
    start_ref,
    length_ref,
    qkv_ref,
    gm_ref,
    o_ref,
    inv_ref,
    *rest,
):
    att_hbms, rest = (rest[:pieces], rest[pieces:])
    n1_hbm, n2_hbm, gb_hbm, hid_hbm, cot_hbm, mixed_hbm, gproj_hbm, small_ref = rest[:8]
    g_ref, gqkv_ref, gwo_ref, gwu_ref, gwd_ref, gsmall_ref = rest[8:14]
    later_ref, dq_ref, dk_ref, dv_ref, left_ref, right_ref = rest[14:20]
    load_sem, att_sem = rest[20:22]
    rest = rest[22:]
    sum_refs, att_refs, ds_refs = (rest[i * pieces : (i + 1) * pieces] for i in range(3))
    rest = rest[3 * pieces :]
    step = pl.program_id(0)
    first_step = 2 * chunks + 1
    length = qkv_ref.shape[0]
    width = left_ref.shape[2]
    sequences = left_ref.shape[1] // length
    turns = pairs * sequences
    turn = jnp.maximum(step - first_step, 0)

    place = Place(count, copies)
    parts = []

    def add_part(write):
        at = 6 * len(parts)
        parts.append(Scatter(place, rest[at : at + 6], write))

    for c in range(chunks):

        def write_up(value, c=c):
            gwu_ref[:, c * width : (c + 1) * width] = value

        add_part(write_up)
    half_rows = gwd_ref.shape[0] // 2
    for h in range(2):

        def write_down(value, h=h):
            gwd_ref[h * half_rows : (h + 1) * half_rows, :] = value

        add_part(write_down)

    def write_out(value):
        gwo_ref[...] = value

    add_part(write_out)
    for pair in range(pairs - 1, TAIL - 1, -1):

        def write_pair(value, pair=pair):
            for which in range(3):
                first = which * width + pair * PAIR
                gqkv_ref[:, first : first + PAIR] = value[:, which * PAIR : (which + 1) * PAIR]

        add_part(write_pair)
    small = Reduce(place, rest[6 * len(parts) : 6 * len(parts) + 4], gsmall_ref)
    up_parts, (down0, down1, out_part) = (parts[:chunks], parts[chunks : chunks + 3])
    pair_parts = parts[chunks + 3 :]

    left_slot = [0] * chunks + [(c + 1) % 2 for c in range(chunks)] + [(chunks + 1) % 2]
    right_slot = [c % 2 for c in range(chunks)] + [chunks % 2] * chunks + [(chunks + 1) % 2]

    def chunk_of(ref, c):
        return ref.at[:, pl.ds(c * width, width)]

    left_loads = {0: n2_hbm, 2 * chunks: mixed_hbm}
    right_loads = {chunks: cot_hbm, 2 * chunks: gproj_hbm}
    for c in range(chunks):
        left_loads[chunks + c] = chunk_of(hid_hbm, c)
        right_loads[c] = chunk_of(gb_hbm, c)

    def loads(when):
        found = []
        if when in left_loads:
            at = left_slot[when]
            found.append(
                pltpu.make_async_copy(left_loads[when], left_ref.at[at], load_sem.at[at])
            )
        if when in right_loads:
            at = right_slot[when]
            found.append(
                pltpu.make_async_copy(right_loads[when], right_ref.at[at], load_sem.at[2 + at])
            )
        return found

    n1_slot = chunks % 2

    def load_n1():
        return pltpu.make_async_copy(n1_hbm, left_ref.at[n1_slot], load_sem.at[4])

    def load_att(at, half):
        seq = lax.rem(at, sequences)
        head = 2 * (pairs - 1 - lax.div(at, sequences)) + half
        return [
            pltpu.make_async_copy(
                att_hbms[i].at[seq, head], att_refs[i].at[half], att_sem.at[half * pieces + i]
            )
            for i in range(pieces)
        ]

    def begin():
        for copy in loads(0):
            copy.start()
        place.meet(copies=True)
        small.start(small_ref[...])

    def before_attention():
        load_n1().start()
        for half in range(2):
            for copy in load_att(0, half):
                copy.start()

    entries = [(0, begin), (first_step - 1, before_attention)]
    for c, part in enumerate(up_parts):
        entries += [
            (c + 2, part.after_cores),
            (2 * c + 5, part.after_columns),
            (2 * c + 8, part.after_levels),
            (2 * c + 10, part.after_copies),
        ]
    f = first_step
    late = BACK_TABLE
    names = (down0, down1, out_part) + tuple(pair_parts)
    entries += [
        (3, small.after_cores),
        (6, small.after_columns),
        (10, small.after_levels),
        (13, small.after_copies),
        (f + sequences - 1, load_n1().wait),
    ]
    left_over = []
    for part, whens in zip(names, late):
        actions = (part.after_cores, part.after_columns, part.after_levels, part.after_copies)
        for phase, (when, action) in enumerate(zip(whens, actions)):
            if when < sequences * pairs:
                entries.append((f + when, action))
            else:
                left_over.append((when, phase, action))
    at_steps(step, schedule(*entries))

    @pl.when(step < first_step)
    def _():
        left_at = jnp.zeros((), jnp.int32)
        right_at = jnp.zeros((), jnp.int32)
        for when in range(first_step):

            @pl.when(step == when)
            def _(when=when):
                if when + 1 < first_step:
                    for copy in loads(when + 1):
                        copy.start()
                for copy in loads(when):
                    copy.wait()

            left_at = jnp.where(step == when, left_slot[when], left_at)
            right_at = jnp.where(step == when, right_slot[when], right_at)
        grad = dot_tn(left_ref[left_at], right_ref[right_at]).astype(BF16)
        for when in range(first_step):

            @pl.when(step == when)
            def _(when=when):
                if when < chunks or when == 2 * chunks:
                    part = out_part if when == 2 * chunks else up_parts[when]
                    rows = width // count
                    for block in range(count):
                        part.held[block] = grad[block * rows : (block + 1) * rows, :]
                    part.start()
                else:
                    blocks = count // chunks
                    for i in range(blocks):
                        block = (when - chunks) * blocks + i
                        for h, part in enumerate((down0, down1)):
                            at = (2 * i + h) * half_rows
                            part.held[block] = grad[at : at + half_rows, :]
                    for part in (down0, down1):
                        part.start_blocks((when - chunks) * blocks, blocks)

    @pl.when(step >= first_step)
    def _():
        seq = lax.rem(turn, sequences)
        inputs = (qkv_ref, gm_ref, o_ref, inv_ref)
        masks = (slot, pieces, start_ref, length_ref)
        scratch = (sum_refs, att_refs, ds_refs, later_ref, dq_ref, dk_ref, dv_ref)

        @pl.when(turn < sequences)
        def _():
            for ref in sum_refs:
                ref[seq] = jnp.zeros(ref.shape[1:], F32)

        def wait_att(half):
            for copy in load_att(turn, half):
                copy.wait()

        def next_att(half):
            @pl.when(turn < turns - 1)
            def _():
                for copy in load_att(turn + 1, half):
                    copy.start()

        wait_att(1)
        head_back(1, False, seq, masks, inputs, scratch)
        next_att(1)
        wait_att(0)

        @pl.when(turn < turns - sequences)
        def _():
            head_back(0, False, seq, masks, inputs, scratch)

        @pl.when(turn >= turns - sequences)
        def _():
            head_back(0, True, seq, masks, inputs, scratch)

        next_att(0)
        grads = (dq_ref[...], jnp.transpose(dk_ref[...]), jnp.transpose(dv_ref[...]))
        keep = pl.ds(pl.multiple_of(seq * length, length), length)
        for which, grad in enumerate(grads):
            columns = slice(which * PAIR, (which + 1) * PAIR)
            low = grad.astype(BF16)
            g_ref[:, columns] = low
            right_ref[0, keep, columns] = low

    @pl.when((step >= first_step) & (lax.rem(turn, sequences) == sequences - 1))
    def _():
        @pl.when(turn < (pairs - TAIL) * sequences)
        def _():
            grad = dot_tn(left_ref[n1_slot], right_ref[0, :, : 3 * PAIR]).astype(BF16)
            rows = width // count
            for i, part in enumerate(pair_parts):

                @pl.when(turn == (i + 1) * sequences - 1)
                def _(part=part):
                    for block in range(count):
                        part.held[block] = grad[block * rows : (block + 1) * rows, :]
                    part.start()

    @pl.when(step == pl.num_programs(0) - 1)
    def _():
        for _, _, action in sorted(left_over, key=lambda item: item[:2]):
            action()
        for part in parts + [small]:
            part.drain()


def head_back(half, first_head, seq, masks, inputs, scratch):
    slot, pieces, start_ref, length_ref = masks
    qkv_ref, gm_ref, o_ref, inv_ref = inputs
    sum_refs, att_refs, ds_refs, later_ref, dq_ref, dk_ref, dv_ref = scratch
    zero = jnp.zeros((), BF16)
    scale = jnp.asarray(SCALE, BF16)
    mask = head_mask(half)

    def scaled_grad(rows):
        return jnp.where(mask, gm_ref[rows, :].astype(F32) * inv_ref[rows, :], 0.0)

    def query_of(rows):
        return jnp.where(mask, qkv_ref[rows, :PAIR], zero) * scale

    if first_head:
        later_ref[...] = jnp.zeros_like(later_ref)
        row = lax.broadcasted_iota(jnp.int32, (ROWS, ROWS), 0)
        col = lax.broadcasted_iota(jnp.int32, (ROWS, ROWS), 1)
        triangle = (col > row).astype(BF16)
    for i in reversed(range(pieces)):
        keys = (i + 1) * slot
        for first in reversed(range(0, slot, ROWS)):
            rows = pl.ds(i * slot + first, ROWS)
            at = pl.ds(first, ROWS)
            scaled = scaled_grad(rows)
            delta = jnp.sum(scaled * o_ref[rows, :].astype(F32), axis=-1, keepdims=True)
            grad_attention = dot_nt(scaled.astype(BF16), qkv_ref[:keys, 2 * PAIR :])
            grad_logits = att_refs[i][half, at, :].astype(F32) * (grad_attention - delta)
            if first_head:
                total = sum_refs[i][seq, at, :] + grad_logits
                grad_selected = -(later_ref[:, :keys] + triangle_sum(triangle, total))
                later_ref[:, :keys] += column_sum(total)
                _, chosen = block_masks(
                    start_ref, length_ref, seq, pieces, i * slot + first, keys
                )
                positive = dot_nt(query_of(rows), qkv_ref[:keys, PAIR : 2 * PAIR]) > 0
                grad_logits = grad_logits + jnp.where(chosen & positive, grad_selected, 0.0)
            else:
                sum_refs[i][seq, at, :] += grad_logits
            ds_refs[i][at, :] = grad_logits.astype(BF16)
        rows = pl.ds(i * slot, slot)
        key = jnp.where(mask, qkv_ref[:keys, PAIR : 2 * PAIR], zero) * scale
        query_part = dot(ds_refs[i][...], key)
        key_part = dot_tn(query_of(rows), ds_refs[i][...])
        value_part = dot_tn(scaled_grad(rows).astype(BF16), att_refs[i][half])
        if half == 1:
            dq_ref[rows, :] = query_part
        else:
            dq_ref[rows, :] += query_part
        if half == 1 and i == pieces - 1:
            dk_ref[...] = key_part
            dv_ref[...] = value_part
        else:
            dk_ref[:, :keys] += key_part
            dv_ref[:, :keys] += value_part


def attend_back(
    projected, starts, lengths, grad_mixed, mixed, inverse, attention, kept, small, devices, copies
):
    n1, n2, grad_before, hidden, cotangent, grad_proj = kept
    sequences, pieces = starts.shape
    count, columns = projected.shape
    length = count // sequences
    slot = length // pieces
    width = columns // 3
    pairs = width // PAIR
    chunks = hidden.shape[1] // width
    first_step = 2 * chunks + 1
    rows = width // devices
    down_rows = hidden.shape[1] // devices
    lines = small.shape[0]

    def part(size):
        def index(step, a, b):
            at = jnp.maximum(step - first_step, 0)
            return (lax.rem(at, sequences), pairs - 1 - lax.div(at, sequences))

        return pl.BlockSpec((length, size * PAIR), index)

    anywhere = pl.BlockSpec(memory_space=pl.ANY)

    def fixed(shape):
        return pl.BlockSpec(shape, lambda *_: (0,) * len(shape))

    results = [
        (rows, columns),
        (rows, width),
        (rows, chunks * width),
        (down_rows, width),
        (lines, 1, width),
    ]
    slots = [(slot, (i + 1) * slot) for i in range(pieces)]
    scratch = [
        pltpu.VMEM((1, length), F32),
        pltpu.VMEM((length, PAIR), F32),
        pltpu.VMEM((PAIR, length), F32),
        pltpu.VMEM((PAIR, length), F32),
        pltpu.VMEM((2, count, width), BF16),
        pltpu.VMEM((2, count, width), BF16),
        pltpu.SemaphoreType.DMA((5,)),
        pltpu.SemaphoreType.DMA((2 * pieces,)),
    ]
    scratch += [pltpu.VMEM((sequences,) + shape, F32) for shape in slots]
    scratch += [pltpu.VMEM((2,) + shape, BF16) for shape in slots]
    scratch += [pltpu.VMEM(shape, BF16) for shape in slots]
    for piece_rows in [rows] * chunks + [down_rows // 2] * 2 + [rows]:
        scratch += scatter_scratch(devices, copies, piece_rows, width)
    for _ in range(pairs - TAIL):
        scratch += scatter_scratch(devices, copies, rows, 3 * PAIR)
    scratch += reduce_scratch(devices, copies, lines, width)
    return pl.pallas_call(
        functools.partial(
            attend_back_kernel, slot, pieces, chunks, devices, copies, pairs
        ),
        out_shape=[jax.ShapeDtypeStruct((count, columns), BF16)]
        + [jax.ShapeDtypeStruct(shape, F32) for shape in results],
        grid_spec=pltpu.PrefetchScalarGridSpec(
            num_scalar_prefetch=2,
            grid=(first_step + sequences * pairs,),
            in_specs=[part(3)]
            + [part(1)] * 3
            + [anywhere] * (pieces + 7)
            + [fixed((lines, 1, width))],
            out_specs=[part(3)] + [fixed(shape) for shape in results],
            scratch_shapes=scratch,
        ),
        compiler_params=comm_params(2, "arbitrary"),
        name="attend_back",
    )(
        starts,
        lengths,
        projected,
        grad_mixed,
        mixed,
        inverse,
        *attention,
        n1,
        n2,
        grad_before,
        hidden,
        cotangent,
        mixed,
        grad_proj,
        small,
    )


def gelu_and_slope(values):
    square = values * values
    inner = GELU_IN * values * (1.0 + GELU_CUBE * square)
    bent = jnp.tanh(inner)
    half = 0.5 * (1.0 + bent)
    slope = half + 0.5 * values * (1.0 - bent * bent) * (
        GELU_IN * (1.0 + 3.0 * GELU_CUBE * square)
    )
    return (values * half, slope)


def feed_kernel(
    chunk,
    x_ref,
    mixed_ref,
    cot_ref,
    gain_ref,
    shift_ref,
    up_bias_ref,
    down_bias_ref,
    wo_hbm,
    wu_hbm,
    wd_hbm,
    out_ref,
    gmid_ref,
    gmix_ref,
    small_ref,
    n2_ref,
    hid_ref,
    gb_ref,
    gproj_ref,
    wo_ref,
    wu_ref,
    wd_ref,
    acc_ref,
    gnorm_ref,
    mid_ref,
    load_sem,
):
    step = pl.program_id(0)
    chunks = wu_ref.shape[0]

    def load_out():
        return pltpu.make_async_copy(wo_hbm, wo_ref, load_sem.at[0])

    def load_up(c):
        return pltpu.make_async_copy(
            wu_hbm.at[:, pl.ds(c * chunk, chunk)], wu_ref.at[c], load_sem.at[1 + 2 * c]
        )

    def load_down(c):
        return pltpu.make_async_copy(
            wd_hbm.at[pl.ds(c * chunk, chunk), :], wd_ref.at[c], load_sem.at[2 + 2 * c]
        )

    @pl.when(step == 0)
    def _():
        load_out().start()
        for c in range(chunks):
            load_up(c).start()
            load_down(c).start()
        small_ref[...] = jnp.zeros_like(small_ref)
        load_out().wait()

    mid_ref[...] = x_ref[...].astype(F32) + dot(mixed_ref[...], wo_ref[...])

    @pl.when(step == 0)
    def _():
        for c in range(chunks):
            load_up(c).wait()
            load_down(c).wait()

    normed, _ = normalize(mid_ref[...])
    n2_ref[...] = (normed * gain_ref[...] + shift_ref[...]).astype(BF16)
    acc_ref[...] = jnp.zeros_like(acc_ref)
    gnorm_ref[...] = jnp.zeros_like(gnorm_ref)

    def one_chunk(c, carry):
        columns = pl.ds(pl.multiple_of(c * chunk, chunk), chunk)
        before = dot(n2_ref[...], wu_ref[c]) + up_bias_ref[c]
        hidden, slope = gelu_and_slope(before)
        hidden = hidden.astype(BF16)
        hid_ref[:, columns] = hidden
        acc_ref[...] += dot(hidden, wd_ref[c])
        grad_hidden = dot_nt(cot_ref[...], wd_ref[c]).astype(BF16)
        grad_before = (grad_hidden.astype(F32) * slope).astype(BF16)
        gb_ref[:, columns] = grad_before
        small_ref[3 + c] += column_sum(grad_before.astype(F32))
        gnorm_ref[...] += dot_nt(grad_before, wu_ref[c])
        return carry

    lax.fori_loop(0, chunks, one_chunk, 0, unroll=True)

    out_ref[...] = (mid_ref[...] + (acc_ref[...] + down_bias_ref[...])).astype(BF16)
    grad_normed = gnorm_ref[...]
    normed, inverse = normalize(mid_ref[...])
    cot = cot_ref[...].astype(F32)
    small_ref[0] += column_sum(grad_normed * normed)
    small_ref[1] += column_sum(grad_normed)
    small_ref[2] += column_sum(cot)
    grad_middle = cot + norm_back(grad_normed * gain_ref[...], normed, inverse)
    gmid_ref[...] = grad_middle
    grad_proj = grad_middle.astype(BF16)
    gproj_ref[...] = grad_proj
    gmix_ref[...] = dot_nt(grad_proj, wo_ref[...]).astype(BF16)


def vector_line(row):
    return lambda width: pl.BlockSpec((None, 1, width), lambda *_: (row, 0, 0))


def feed(tokens, mixed, cotangent, vectors, wo, wu, wd):
    count, width = tokens.shape
    hidden = wu.shape[1]
    block = 512
    chunk = width
    chunks = hidden // chunk
    rows = pl.BlockSpec((block, width), lambda i: (i, 0))
    anywhere = pl.BlockSpec(memory_space=pl.ANY)
    wide = pl.BlockSpec((block, hidden), lambda i: (i, 0))

    def low(columns):
        return jax.ShapeDtypeStruct((count, columns), BF16)

    return pl.pallas_call(
        functools.partial(feed_kernel, chunk),
        out_shape=[
            low(width),
            jax.ShapeDtypeStruct((count, width), F32),
            low(width),
            jax.ShapeDtypeStruct((3 + chunks, 1, width), F32),
            low(width),
            low(hidden),
            low(hidden),
            low(width),
        ],
        grid=(count // block,),
        in_specs=[
            rows,
            rows,
            rows,
            vector_line(GAIN2)(width),
            vector_line(SHIFT2)(width),
            pl.BlockSpec((chunks, 1, chunk), lambda i: (0, 0, 0)),
            vector_line(DOWN_BIAS)(width),
            anywhere,
            anywhere,
            anywhere,
        ],
        out_specs=[
            rows,
            rows,
            rows,
            pl.BlockSpec((3 + chunks, 1, width), lambda i: (0, 0, 0)),
            rows,
            wide,
            wide,
            rows,
        ],
        scratch_shapes=[
            pltpu.VMEM(wo.shape, BF16),
            pltpu.VMEM((chunks, width, chunk), BF16),
            pltpu.VMEM((chunks, chunk, width), BF16),
            pltpu.VMEM((block, width), F32),
            pltpu.VMEM((block, width), F32),
            pltpu.VMEM((block, width), F32),
            pltpu.SemaphoreType.DMA((1 + 2 * chunks,)),
        ],
        compiler_params=params("arbitrary"),
        name="feed",
    )(
        tokens,
        mixed,
        cotangent,
        vectors,
        vectors,
        vectors,
        vectors,
        wo,
        wu,
        wd,
    )


def input_kernel(
    count,
    copies,
    gmid_ref,
    gain_ref,
    shift_ref,
    rest_ref,
    x_hbm,
    n1_hbm,
    g_hbm,
    w_hbm,
    gx_ref,
    gw_ref,
    gsmall_ref,
    x_ref,
    n1_ref,
    g_ref,
    w_ref,
    small_ref,
    load_sem,
    *rest,
):
    step = pl.program_id(0)
    total, width = x_ref.shape
    columns = w_ref.shape[1]
    block = gx_ref.shape[0]
    first = TAIL * 3 * PAIR
    place = Place(count, copies)

    def write(value):
        gw_ref[...] = rest_ref[...]
        for at in range(3 * TAIL):
            to = (at % 3) * width + (at // 3) * PAIR
            gw_ref[:, to : to + PAIR] = value[:, at * PAIR : (at + 1) * PAIR]

    part = Scatter(place, rest[:6], write)
    small = Reduce(place, rest[6:10], gsmall_ref)

    def loads():
        near, far = (pl.ds(0, first), pl.ds(first, columns - first))
        pairs = [
            (n1_hbm, n1_ref),
            (g_hbm.at[:, near], g_ref.at[:, near]),
            (x_hbm, x_ref),
            (g_hbm.at[:, far], g_ref.at[:, far]),
            (w_hbm, w_ref),
        ]
        return [
            pltpu.make_async_copy(source, target, load_sem.at[i])
            for i, (source, target) in enumerate(pairs)
        ]

    def begin():
        for copy in loads():
            copy.start()
        place.meet(copies=True)
        small_ref[...] = jnp.zeros_like(small_ref)
        for copy in loads()[:2]:
            copy.wait()
        grad = dot_tn(n1_ref[...], g_ref[:, :first]).astype(BF16)
        rows = width // count
        for i in range(count):
            part.held[i] = grad[i * rows : (i + 1) * rows, :]
        part.start()
        for copy in loads()[2:]:
            copy.wait()

    steps = total // block
    table = schedule(
        (0, begin),
        (1, part.after_cores),
        (min(3, steps - 1), part.after_columns),
    )
    at_steps(step, table)

    normed, inverse = normalize(
        x_ref[pl.ds(pl.multiple_of(step * block, block), block), :].astype(F32)
    )
    grads = g_ref[pl.ds(pl.multiple_of(step * block, block), block), :]
    grad_normed = dot_nt(grads, w_ref[...])
    small_ref[0] += column_sum(grad_normed * normed)
    small_ref[1] += column_sum(grad_normed)
    gx_ref[...] = gmid_ref[...] + norm_back(grad_normed * gain_ref[...], normed, inverse)

    @pl.when(step == steps - 1)
    def _():
        small.start(small_ref[...])
        small.after_cores()
        part.after_levels()
        small.after_columns()
        part.after_copies()
        small.after_levels()
        small.after_copies()
        part.drain()
        small.drain()


def input_back(tokens, n1, grad_middle, grads, grad_rest, vectors, weight, devices, copies):
    count, width = tokens.shape
    block = 512
    shard = width // devices
    rows = pl.BlockSpec((block, width), lambda i: (i, 0))
    own = pl.BlockSpec((shard, 3 * width), lambda i: (0, 0))
    anywhere = pl.BlockSpec(memory_space=pl.ANY)
    scratch = [
        pltpu.VMEM((count, width), BF16),
        pltpu.VMEM((count, width), BF16),
        pltpu.VMEM((count, 3 * width), BF16),
        pltpu.VMEM(weight.shape, BF16),
        pltpu.VMEM((2, 1, width), F32),
        pltpu.SemaphoreType.DMA((5,)),
    ]
    scratch += scatter_scratch(devices, copies, shard, TAIL * 3 * PAIR)
    scratch += reduce_scratch(devices, copies, 2, width)
    return pl.pallas_call(
        functools.partial(input_kernel, devices, copies),
        out_shape=[
            jax.ShapeDtypeStruct((count, width), F32),
            jax.ShapeDtypeStruct((shard, 3 * width), F32),
            jax.ShapeDtypeStruct((2, 1, width), F32),
        ],
        grid=(count // block,),
        in_specs=[rows, vector_line(GAIN1)(width), vector_line(SHIFT1)(width), own]
        + [anywhere] * 4,
        out_specs=[
            rows,
            own,
            pl.BlockSpec((2, 1, width), lambda i: (0, 0, 0)),
        ],
        scratch_shapes=scratch,
        compiler_params=comm_params(3, "arbitrary"),
        name="input_back",
    )(grad_middle, vectors, vectors, grad_rest, tokens, n1, grads, weight)


def local(
    tokens,
    piece_start,
    piece_length,
    query_key_value,
    output_weight,
    up_weight,
    down_weight,
    first_gain,
    first_shift,
    second_gain,
    second_shift,
    up_bias,
    down_bias,
    cotangent,
):
    width = tokens.shape[1]
    devices, copies = (lax.axis_size("fsdp"), lax.axis_size("rep"))
    index = lax.axis_index("fsdp")

    def placed(vector):
        flat = jnp.zeros((devices * vector.shape[0],), BF16)
        flat = lax.dynamic_update_slice(flat, vector, (index * vector.shape[0],))
        return flat.reshape(-1, width)

    own = [up_bias, first_gain, first_shift, second_gain, second_shift, down_bias]
    own = jnp.concatenate([placed(vector) for vector in own], axis=0)
    own = jnp.pad(own, ((0, LINES - own.shape[0]), (0, 0)))

    (projected, mixed, inverse), attention, (n1, vectors, wqkv, wo, wu, wd) = front(
        tokens,
        piece_start,
        piece_length,
        query_key_value,
        own,
        output_weight,
        up_weight,
        down_weight,
        devices,
        copies,
    )
    block_output, grad_middle, grad_mixed, small2, n2, hidden, grad_before, grad_proj = feed(
        tokens, mixed, cotangent, vectors, wo, wu, wd
    )
    grads, grad_rest, gwo, gwu, gwd, small2 = attend_back(
        projected,
        piece_start,
        piece_length,
        grad_mixed,
        mixed,
        inverse,
        attention,
        (n1, n2, grad_before, hidden, cotangent, grad_proj),
        small2,
        devices,
        copies,
    )
    grad_tokens, gwqkv, small1 = input_back(
        tokens, n1, grad_middle, grads, grad_rest, vectors, wqkv, devices, copies
    )

    def mine(values):
        values = values.reshape(-1)
        size = values.shape[0] // devices
        return lax.dynamic_slice(values, (index * size,), (size,))

    return (
        block_output,
        grad_tokens,
        gwqkv,
        gwo,
        gwu,
        gwd,
        mine(small1[0]),
        mine(small1[1]),
        mine(small2[0]),
        mine(small2[1]),
        mine(small2[3:]),
        mine(small2[2]),
    )


def solution(mesh):
    rows = P(("fsdp", "rep"), None)
    matrix = P("fsdp", None)
    vector = P("fsdp")
    return jax.shard_map(
        local,
        mesh=mesh,
        in_specs=(rows,) * 3 + (matrix,) * 4 + (vector,) * 6 + (rows,),
        out_specs=(rows,) * 2 + (matrix,) * 4 + (vector,) * 6,
        check_vma=False,
    )
```

```python
import functools

import jax
import jax.numpy as jnp
from jax import lax
from jax.experimental import pallas as pl
from jax.experimental.pallas import tpu as pltpu
from jax.sharding import PartitionSpec as P

HEAD_DIM = 64
PAIR = 2 * HEAD_DIM
ROWS = 256
MASKED_VALUE = -1e30
EPSILON = 1e-05
SCALE = HEAD_DIM**-0.5
GAIN1, SHIFT1, GAIN2, SHIFT2, DOWN_BIAS = (4, 5, 6, 7, 8)
LINES = 16
FRONT_TABLE = ((2, 4, 5, 7, 8), (4, 6, 7, 9, 10), (6, 8, 9, 11, 11))
BACK_TABLE = ((0, 3, 6, 8), (0, 5, 8, 10), (1, 6, 9, 11), (3, 7, 10, 11), (5, 8, 10, 12), (7, 9, 11, 13), (9, 10, 12, 14))
GELU_IN = 0.7978845608028654
GELU_CUBE = 0.044715
VMEM_LIMIT = 67043328

F32 = jnp.float32
BF16 = jnp.bfloat16


def dot(left, right):
    return lax.dot_general(left, right, (((1,), (0,)), ((), ())), preferred_element_type=F32)


def dot_nt(left, right):
    return lax.dot_general(left, right, (((1,), (1,)), ((), ())), preferred_element_type=F32)


def dot_tn(left, right):
    return lax.dot_general(left, right, (((0,), (0,)), ((), ())), preferred_element_type=F32)


def row_mean(values):
    return jnp.mean(values, axis=-1, keepdims=True)


def normalize(values):
    center = values - row_mean(values)
    inverse = lax.rsqrt(row_mean(center * center) + EPSILON)
    return (center * inverse, inverse)


def norm_back(grad, normed, inverse):
    return (grad - row_mean(grad) - normed * row_mean(grad * normed)) * inverse


def column_sum(values):
    return jnp.sum(values, axis=0, keepdims=True)


def params(*semantics):
    return pltpu.CompilerParams(dimension_semantics=semantics, vmem_limit_bytes=VMEM_LIMIT)


def comm_params(number, *semantics):
    return pltpu.CompilerParams(
        dimension_semantics=semantics,
        vmem_limit_bytes=VMEM_LIMIT,
        collective_id=number,
        has_side_effects=True,
    )


MESH = pl.DeviceIdType.MESH
LEVELS = 4
CORES = 2


class Place:
    def __init__(self, count, copies):
        self.count, self.copies = (count, copies)
        self.columns = count // (LEVELS * CORES)
        self.index = lax.axis_index("fsdp")
        self.rep = lax.axis_index("rep")
        self.core = lax.rem(self.index, CORES)
        chip = lax.div(self.index, CORES)
        self.column = lax.rem(chip, self.columns)
        self.level = lax.div(chip, self.columns)
        self.half = lax.rem(self.rep, 2)

    def block(self, up=0, across=0, other=0):
        level = lax.rem(self.level + (up + LEVELS), LEVELS)
        column = lax.rem(self.column + (across + self.columns), self.columns)
        core = lax.rem(self.core + other, CORES)
        return (level * self.columns + column) * CORES + core

    def device(self, up=0, across=0, other=0, copy=0):
        return (self.block(up, across, other), lax.rem(self.rep + copy, self.copies))

    def twin(self):
        return (self.index, self.rep + 1 - 2 * self.half)

    def meet(self, twin=False, copies=False):
        others = [self.device(up=up) for up in range(1, LEVELS)]
        others += [self.device(across=across) for across in range(1, self.columns)]
        others += [self.device(other=1)]
        if twin:
            others += [self.twin()]
        if copies:
            others += [self.device(copy=copy) for copy in range(1, self.copies)]
        barrier = pltpu.get_barrier_semaphore()
        for other in others:
            pl.semaphore_signal(barrier, inc=1, device_id=other, device_id_type=MESH)
        pl.semaphore_wait(barrier, len(others))


def send(source, target, sems, slot, device):
    return pltpu.make_async_remote_copy(
        src_ref=source,
        dst_ref=target,
        send_sem=sems.at[2 * slot],
        recv_sem=sems.at[2 * slot + 1],
        device_id=device,
        device_id_type=MESH,
    )


def gather_sems(count):
    across = count // (LEVELS * CORES) - 1
    return 2 * (2 * (LEVELS - 1) + 2 * across + 1) + 1


class Gather:
    def __init__(self, place, source, target, first, columns, shared, sems):
        self.place, self.source, self.target = (place, source, target)
        self.sems, self.shared, self.across = (sems, shared, columns)
        rows = source.shape[0]
        base = place.core * (target.shape[2] // CORES) + first
        third = rows // 3
        half = place.half
        self.whole = pl.ds(pl.multiple_of(base, rows), rows)
        if shared:
            self.near = pl.ds(pl.multiple_of(half * third, third), 2 * third)
            self.part = pl.ds(pl.multiple_of(base + half * third, third), 2 * third)
            self.give = pl.ds(pl.multiple_of(base + half * (2 * third), third), third)
        else:
            self.near, self.part = (pl.ds(0, rows), self.whole)

    def held(self, level, column, rows):
        return self.target.at[level, column, rows, self.across]

    def send(self, ref, slot, device):
        return send(ref, ref, self.sems, slot, device)

    def level_copies(self):
        place = self.place
        return [
            send(
                self.source.at[self.near, :],
                self.held(place.level, place.column, self.part),
                self.sems,
                up - 1,
                place.device(up=up),
            )
            for up in range(1, LEVELS)
        ]

    def column_copies(self):
        place = self.place
        ref = self.held(slice(None), place.column, self.part)
        return [
            self.send(ref, LEVELS - 2 + across, place.device(across=across))
            for across in range(1, place.columns)
        ]

    def twin_copies(self, near):
        if not self.shared:
            return []
        place = self.place
        base = LEVELS - 1 + place.columns - 1
        if near:
            return [
                self.send(
                    self.held(
                        lax.rem(place.level + (LEVELS - up), LEVELS), place.column, self.give
                    ),
                    base + up - 1,
                    place.twin(),
                )
                for up in range(1, LEVELS)
            ]
        return [
            self.send(
                self.held(
                    slice(None),
                    lax.rem(place.column + (place.columns - across), place.columns),
                    self.give,
                ),
                base + LEVELS - 2 + across,
                place.twin(),
            )
            for across in range(1, place.columns)
        ]

    def core_copy(self):
        slot = 2 * (LEVELS - 1) + 2 * (self.place.columns - 1)
        ref = self.held(slice(None), slice(None), self.whole)
        return self.send(ref, slot, self.place.device(other=1))

    def own(self):
        place = self.place
        last = gather_sems(place.count) - 1
        return pltpu.make_async_copy(
            self.source, self.held(place.level, place.column, self.whole), self.sems.at[last]
        )

    def start(self):
        for copy in self.level_copies():
            copy.start()
        self.own().start()

    def after_levels(self):
        self.own().wait()
        for copy in self.level_copies():
            copy.wait_recv()
        for copy in self.column_copies() + self.twin_copies(True):
            copy.start()

    def after_columns(self):
        for copy in self.column_copies():
            copy.wait_recv()
        for copy in self.twin_copies(False):
            copy.start()
        if not self.shared:
            self.core_copy().start()

    def after_twins(self):
        if self.shared:
            for copy in self.twin_copies(True) + self.twin_copies(False):
                copy.wait_recv()
            self.core_copy().start()

    def finish(self):
        self.core_copy().wait_recv()

    def drain(self):
        copies = self.level_copies() + self.column_copies()
        for copy in copies + self.twin_copies(True) + self.twin_copies(False):
            copy.wait_send()
        self.core_copy().wait_send()


def scatter_slots(count, copies):
    across = count // (CORES * LEVELS) - 1
    return LEVELS + across + (LEVELS - 1) + (copies - 1)


def scatter_scratch(count, copies, rows, columns):
    across = count // (CORES * LEVELS)
    return [
        pltpu.VMEM((LEVELS, across, CORES, rows, columns), BF16),
        pltpu.VMEM((LEVELS, across, rows, columns), BF16),
        pltpu.VMEM((max(across - 1, 1), LEVELS, rows, columns), BF16),
        pltpu.VMEM((LEVELS - 1, rows, columns), BF16),
        pltpu.VMEM((copies, rows, columns), BF16),
        pltpu.SemaphoreType.DMA((2 * scatter_slots(count, copies),)),
    ]


def add_low(left, right):
    return (left.astype(F32) + right.astype(F32)).astype(BF16)


class Scatter:
    def __init__(self, place, refs, write, by_level=False):
        self.place, self.write, self.by_level = (place, write, by_level)
        self.held, self.from_core, self.from_column, self.from_level, self.parts, self.sems = refs

    def put(self, block, value):
        chip = block // CORES
        self.held[chip // self.place.columns, chip % self.place.columns, block % CORES] = value

    def core_copies(self):
        place = self.place
        other = 1 - place.core
        if not self.by_level:
            source = self.held.at[:, :, other]
            return [send(source, self.from_core, self.sems, 0, place.device(other=1))]
        return [
            send(
                self.held.at[level, :, other],
                self.from_core.at[level],
                self.sems,
                level,
                place.device(other=1),
            )
            for level in range(LEVELS)
        ]

    def column_copies(self):
        place = self.place
        return [
            send(
                self.held.at[:, lax.rem(place.column + across, place.columns), place.core],
                self.from_column.at[across - 1],
                self.sems,
                LEVELS + across - 1,
                place.device(across=across),
            )
            for across in range(1, place.columns)
        ]

    def level_copies(self):
        place = self.place
        base = LEVELS + place.columns - 1
        return [
            send(
                self.held.at[lax.rem(place.level + up, LEVELS), place.column, place.core],
                self.from_level.at[up - 1],
                self.sems,
                base + up - 1,
                place.device(up=up),
            )
            for up in range(1, LEVELS)
        ]

    def rep_copies(self):
        place = self.place
        base = 2 * LEVELS + place.columns - 2
        mine = self.parts.at[place.rep]
        return [
            send(mine, mine, self.sems, base + copy - 1, place.device(copy=copy))
            for copy in range(1, place.copies)
        ]

    def start(self):
        for copy in self.core_copies():
            copy.start()

    def after_cores(self):
        place = self.place
        for copy in self.core_copies():
            copy.wait_recv()

        def add(i, carry):
            level, column = (lax.div(i, place.columns), lax.rem(i, place.columns))
            self.held[level, column, place.core] = add_low(
                self.held[level, column, place.core], self.from_core[level, column]
            )
            return carry

        lax.fori_loop(0, LEVELS * place.columns, add, 0)
        for copy in self.column_copies():
            copy.start()

    def after_columns(self):
        place = self.place
        for copy in self.column_copies():
            copy.wait_recv()

        def add(level, carry):
            total = self.held[level, place.column, place.core].astype(F32)
            for across in range(place.columns - 1):
                total = total + self.from_column[across, level].astype(F32)
            self.held[level, place.column, place.core] = total.astype(BF16)
            return carry

        lax.fori_loop(0, LEVELS, add, 0)
        for copy in self.level_copies():
            copy.start()

    def after_levels(self):
        place = self.place
        for copy in self.level_copies():
            copy.wait_recv()
        total = self.held[place.level, place.column, place.core].astype(F32)
        for level in range(LEVELS - 1):
            total = total + self.from_level[level].astype(F32)
        self.parts[place.rep] = total.astype(BF16)
        for copy in self.rep_copies():
            copy.start()

    def after_copies(self):
        for copy in self.rep_copies():
            copy.wait_recv()
        total = self.parts[0].astype(F32)
        for rep in range(1, self.place.copies):
            total = total + self.parts[rep].astype(F32)
        self.write(total)

    def drain(self):
        copies = self.core_copies() + self.column_copies() + self.level_copies()
        for copy in copies + self.rep_copies():
            copy.wait_send()


def reduce_scratch(count, copies, lines, width):
    across = count // (CORES * LEVELS)
    slots = 1 + (across - 1) + (LEVELS - 1) + (copies - 1)
    return [
        pltpu.VMEM((3, lines, 1, width), F32),
        pltpu.VMEM((1 + across - 1 + LEVELS - 1, lines, 1, width), F32),
        pltpu.VMEM((copies, lines, 1, width), F32),
        pltpu.SemaphoreType.DMA((2 * slots,)),
    ]


class Reduce:
    def __init__(self, place, refs, out):
        self.place, self.out = (place, out)
        self.sums, self.landed, self.parts, self.sems = refs

    def group(self, phase):
        place = self.place
        if phase == 0:
            targets = [place.device(other=1)]
            first = 0
        elif phase == 1:
            targets = [place.device(across=across) for across in range(1, place.columns)]
            first = 1
        else:
            targets = [place.device(up=up) for up in range(1, LEVELS)]
            first = place.columns
        return [
            send(self.sums.at[phase], self.landed.at[first + i], self.sems, first + i, target)
            for i, target in enumerate(targets)
        ]

    def rep_copies(self):
        place = self.place
        base = place.columns + LEVELS - 1
        mine = self.parts.at[place.rep]
        return [
            send(mine, mine, self.sems, base + copy - 1, place.device(copy=copy))
            for copy in range(1, place.copies)
        ]

    def start(self, value):
        self.sums[0] = value
        for copy in self.group(0):
            copy.start()

    def next(self, phase):
        copies = self.group(phase)
        for copy in copies:
            copy.wait_recv()
        first = (0, 1, self.place.columns)[phase]
        total = self.sums[phase]
        for i in range(len(copies)):
            total = total + self.landed[first + i]
        if phase < 2:
            self.sums[phase + 1] = total
            for copy in self.group(phase + 1):
                copy.start()
        else:
            self.parts[self.place.rep] = total
            for copy in self.rep_copies():
                copy.start()

    def after_cores(self):
        self.next(0)

    def after_columns(self):
        self.next(1)

    def after_levels(self):
        self.next(2)

    def after_copies(self):
        for copy in self.rep_copies():
            copy.wait_recv()
        total = self.parts[0]
        for rep in range(1, self.place.copies):
            total = total + self.parts[rep]
        self.out[...] = total

    def drain(self):
        for copy in self.group(0) + self.group(1) + self.group(2) + self.rep_copies():
            copy.wait_send()


def label_of(position, start_ref, length_ref, seq, pieces):
    label = jnp.zeros(position.shape, jnp.int32)
    for piece in range(pieces):
        start = start_ref[seq, piece]
        inside = (position >= start) & (position < start + length_ref[seq, piece])
        label = jnp.where(inside, piece + 1, label)
    return label


def key_count(first_row, slot):
    return (first_row // slot + 1) * slot


def block_masks(start_ref, length_ref, seq, pieces, first_row, keys):
    query_pos = first_row + lax.broadcasted_iota(jnp.int32, (ROWS, 1), 0)
    key_pos = lax.broadcasted_iota(jnp.int32, (1, keys), 1)
    query_label = label_of(query_pos, start_ref, length_ref, seq, pieces)
    key_label = label_of(key_pos, start_ref, length_ref, seq, pieces)
    query_label = jnp.where(query_label > 0, query_label, -1)
    allowed = (key_pos <= query_pos) | (query_label == key_label)
    chosen = allowed & (key_pos != 0) & (key_pos != query_pos)
    return (allowed, chosen)


def triangle_sum(triangle, values):
    upper = values.astype(BF16)
    rest = values - upper.astype(F32)
    middle = rest.astype(BF16)
    lower = (rest - middle.astype(F32)).astype(BF16)
    return dot(triangle, upper) + dot(triangle, middle) + dot(triangle, lower)


def head_mask(half):
    lane = lax.broadcasted_iota(jnp.int32, (1, PAIR), 1)
    first = half * HEAD_DIM
    return (lane >= first) & (lane < first + HEAD_DIM)


def at_steps(step, table):
    for when in sorted(set(table)):
        @pl.when(step == when)
        def _(when=when):
            for action in table[when]:
                action()


def schedule(*entries):
    table = {}
    for when, action in entries:
        table.setdefault(when, []).append(action)
    return table


def pair_groups(pairs):
    groups, at = ([], 0)
    for size in [1, 1] + [2] * pairs:
        if at < pairs:
            groups.append(range(at, min(at + size, pairs)))
            at += size
    return groups


def front_kernel(
    slot,
    pieces,
    count,
    copies,
    pairs,
    start_ref,
    length_ref,
    x_hbm,
    wqkv_hbm,
    vec_hbm,
    wo_hbm,
    wu_hbm,
    wd_hbm,
    qkv_ref,
    o_ref,
    inv_ref,
    *rest,
):
    att_refs, rest = (rest[:pieces], rest[pieces:])
    n1_hbm, vec_ref, full_w, full_o, full_u, full_d = rest[:6]
    x_ref, n1_ref, all_ref, stage_ref, w_ref, bias_ref, prefix_ref = rest[6:13]
    stage_sems, load_sems, vec_sems, w_sems, rest_sems = rest[13:]
    pair, seq = (pl.program_id(0), pl.program_id(1))
    sequences = pl.num_programs(1)
    step = pair * sequences + seq
    length = qkv_ref.shape[0]
    width = x_ref.shape[1]
    sequence_count = x_ref.shape[0] // length
    lines = vec_hbm.shape[0]
    zero = jnp.zeros((), BF16)
    place = Place(count, copies)
    twins = copies % 2 == 0

    vec = Gather(place, vec_hbm, all_ref, 0, pl.ds(0, width), False, vec_sems)
    groups = pair_groups(pairs)
    gathers = []
    for i, group in enumerate(groups):
        columns = pl.ds(group[0] * 3 * PAIR, len(group) * 3 * PAIR)
        shared = twins and i > 2 and wqkv_hbm.shape[0] % 48 == 0
        source = stage_ref.at[:, columns]
        gathers.append(Gather(place, source, full_w, 0, columns, shared, w_sems.at[i]))
    cuts = []
    for shard, full, cut_rows, cut_columns in (
        (wo_hbm, full_o, 1, 1),
        (wu_hbm, full_u, 1, 2),
        (wd_hbm, full_d, 2, 1),
    ):
        rows, columns = (shard.shape[0] // cut_rows, shard.shape[1] // cut_columns)
        for i in range(cut_rows):
            for j in range(cut_columns):
                across = pl.ds(j * columns, columns)
                source = shard.at[pl.ds(i * rows, rows), across]
                cuts.append(
                    Gather(place, source, full, i * rows, across, twins, rest_sems.at[len(cuts)])
                )

    def stage_copies():
        found = []
        for p in range(pairs):
            for which in range(3):
                at = 3 * p + which
                found.append(
                    pltpu.make_async_copy(
                        wqkv_hbm.at[:, pl.ds(which * width + p * PAIR, PAIR)],
                        stage_ref.at[:, pl.ds(at * PAIR, PAIR)],
                        stage_sems.at[at],
                    )
                )
        return found

    def load_x():
        return pltpu.make_async_copy(x_hbm, x_ref, load_sems.at[0])

    def keep_n1():
        return pltpu.make_async_copy(n1_ref, n1_hbm, load_sems.at[1])

    def load_w(p):
        return pltpu.make_async_copy(
            full_w.at[:, :, :, pl.ds(p * 3 * PAIR, 3 * PAIR)],
            w_ref.at[p % 2],
            load_sems.at[2 + p % 2],
        )

    def norm_rows(which):
        gain, shift = (vec_ref[GAIN1], vec_ref[SHIFT1])

        def body(i, carry):
            at = pl.ds(pl.multiple_of(which * length + i * ROWS, ROWS), ROWS)
            normed, _ = normalize(x_ref[at, :].astype(F32))
            n1_ref[at, :] = (normed * gain + shift).astype(BF16)
            return carry

        lax.fori_loop(0, length // ROWS, body, 0)
        if which == sequence_count - 1:
            keep_n1().start()

    def begin():
        for copy in stage_copies():
            copy.start()
        load_x().start()
        place.meet(twin=twins)
        vec.start()
        for copy in stage_copies():
            copy.wait()
        for gather in gathers + cuts:
            gather.start()
        vec.after_levels()
        gathers[0].after_levels()
        vec.after_columns()
        gathers[0].after_columns()
        gathers[1].after_levels()
        vec.finish()
        vectors = jnp.zeros((lines, width), F32)
        for chip in range(count // CORES):
            both = all_ref[chip // place.columns, chip % place.columns].astype(F32)
            vectors = vectors + both[:lines] + both[lines:]
        for line in range(lines):
            vec_ref[line] = vectors[line : line + 1, :]
        load_x().wait()
        gathers[0].finish()
        load_w(0).start()
        norm_rows(0)
        gathers[1].after_columns()
        load_w(0).wait()

    def ready(p):
        for group, gather in zip(groups, gathers):
            if p == group[0]:
                gather.finish()
        load_w(p).start()

    s = sequence_count
    entries = [(0, begin)]
    entries += [(which, functools.partial(norm_rows, which)) for which in range(1, s)]
    entries += [
        (1, gathers[2].after_levels),
        (2, gathers[2].after_columns),
    ]
    for i, gather in enumerate(gathers[3:]):
        need = groups[3 + i][0] * s - 1
        entries += [
            (need - 4, gather.after_levels),
            (need - 3, gather.after_columns),
            (need - 2, gather.after_twins),
        ]
    for p in range(1, pairs):
        entries.append((p * s - 1, functools.partial(ready, p)))
        entries.append((p * s, load_w(p).wait))
    for i, cut in enumerate(cuts):
        entries += [
            (FRONT_TABLE[0][i], cut.after_levels),
            (FRONT_TABLE[1][i], cut.after_columns),
            (FRONT_TABLE[2][i], cut.after_twins),
        ]
    at_steps(step, schedule(*entries))

    seq_rows = pl.ds(pl.multiple_of(seq * length, length), length)
    weight = w_ref[lax.rem(pair, 2)].reshape(width, 3 * PAIR)
    qkv_ref[...] = dot(n1_ref[seq_rows, :], weight).astype(BF16)

    @pl.when(pair == 0)
    def _():
        prefix_ref[...] = jnp.zeros_like(prefix_ref)
        row = lax.broadcasted_iota(jnp.int32, (ROWS, ROWS), 0)
        col = lax.broadcasted_iota(jnp.int32, (ROWS, ROWS), 1)
        triangle = (col < row).astype(BF16)
        for first_row in range(0, length, ROWS):
            keys = key_count(first_row, slot)
            at = pl.ds(first_row, ROWS)
            query = jnp.where(head_mask(0), qkv_ref[at, :PAIR], zero)
            scores = dot_nt(query, qkv_ref[:keys, PAIR : 2 * PAIR]) * SCALE
            allowed, chosen = block_masks(start_ref, length_ref, seq, pieces, first_row, keys)
            selected = jnp.where(chosen & (scores > 0), scores, 0.0)
            penalty = prefix_ref[:, :keys] + triangle_sum(triangle, selected)
            bias_ref[seq, at, :keys] = jnp.where(allowed, -penalty, MASKED_VALUE)
            prefix_ref[:, :keys] += column_sum(selected)

    def logits_of(first_row, half):
        keys = key_count(first_row, slot)
        at = pl.ds(first_row, ROWS)
        query = jnp.where(head_mask(half), qkv_ref[at, :PAIR], zero) * jnp.asarray(SCALE, BF16)
        return dot_nt(query, qkv_ref[:keys, PAIR : 2 * PAIR]) + bias_ref[seq, at, :keys]

    def raise_and_mix(first_row, half, logits):
        keys = key_count(first_row, slot)
        largest = jnp.max(logits, axis=-1, keepdims=True)
        raised = jnp.exp(logits - largest)
        inverse = 1.0 / jnp.sum(raised, axis=-1, keepdims=True)
        low = raised.astype(BF16)
        att_refs[first_row // slot][half, pl.ds(first_row % slot, ROWS), :] = low
        value = jnp.where(head_mask(half), qkv_ref[:keys, 2 * PAIR :], zero)
        return (dot(low, value), inverse)

    def finish_rows(first_row, halves):
        (mixed0, inverse0), (mixed1, inverse1) = halves
        at = pl.ds(first_row, ROWS)
        inverse = jnp.where(head_mask(0), inverse0, inverse1)
        inv_ref[at, :] = inverse
        o_ref[at, :] = ((mixed0 + mixed1) * inverse).astype(BF16)

    blocks = [(first_row, half) for first_row in range(0, length, ROWS) for half in range(2)]
    halves, ahead = ([], logits_of(*blocks[0]))
    for i, block in enumerate(blocks):
        logits = ahead
        if i + 1 < len(blocks):
            ahead = logits_of(*blocks[i + 1])
        halves.append(raise_and_mix(*block, logits))
        if len(halves) == 2:
            finish_rows(block[0], halves)
            halves = []

    @pl.when(step == pairs * sequence_count - 1)
    def _():
        for cut in cuts:
            cut.finish()
        for gather in [vec] + gathers + cuts:
            gather.drain()
        keep_n1().wait()


def front(tokens, starts, lengths, wqkv, vectors, wo, wu, wd, devices, copies):
    sequences, pieces = starts.shape
    count, width = tokens.shape
    length = count // sequences
    slot = length // pieces
    pairs = width // PAIR
    lines = vectors.shape[0]
    anywhere = pl.BlockSpec(memory_space=pl.ANY)

    def low(*shape):
        return jax.ShapeDtypeStruct(shape, BF16)

    att_shapes = [low(sequences, 2 * pairs, slot, (i + 1) * slot) for i in range(pieces)]
    att_specs = [
        pl.BlockSpec((None, 2, slot, (i + 1) * slot), lambda p, s, a, b: (s, p, 0, 0))
        for i in range(pieces)
    ]
    across = devices // (LEVELS * CORES)

    def spread(array):
        return (LEVELS, across, CORES * array.shape[0], array.shape[1])

    weights = [low(*spread(w)) for w in (wqkv, wo, wu, wd)]
    sems = gather_sems(devices)
    results = pl.pallas_call(
        functools.partial(front_kernel, slot, pieces, devices, copies, pairs),
        out_shape=[
            low(count, 3 * width),
            low(count, width),
            jax.ShapeDtypeStruct((count, width), F32),
        ]
        + att_shapes
        + [low(count, width), jax.ShapeDtypeStruct((lines, 1, width), F32)]
        + weights,
        grid_spec=pltpu.PrefetchScalarGridSpec(
            num_scalar_prefetch=2,
            grid=(pairs, sequences),
            in_specs=[anywhere] * 6,
            out_specs=[
                pl.BlockSpec((length, 3 * PAIR), lambda p, s, a, b: (s, p)),
                pl.BlockSpec((length, PAIR), lambda p, s, a, b: (s, p)),
                pl.BlockSpec((length, PAIR), lambda p, s, a, b: (s, p)),
            ]
            + att_specs
            + [anywhere, pl.BlockSpec((lines, 1, width), lambda *_: (0, 0, 0))]
            + [anywhere] * 4,
            scratch_shapes=[
                pltpu.VMEM((count, width), BF16),
                pltpu.VMEM((count, width), BF16),
                pltpu.VMEM(spread(vectors), BF16),
                pltpu.VMEM(wqkv.shape, BF16),
                pltpu.VMEM((2,) + spread(wqkv)[:3] + (3 * PAIR,), BF16),
                pltpu.VMEM((sequences, length, length), F32),
                pltpu.VMEM((1, length), F32),
                pltpu.SemaphoreType.DMA((3 * pairs,)),
                pltpu.SemaphoreType.DMA((4,)),
                pltpu.SemaphoreType.DMA((sems,)),
                pltpu.SemaphoreType.DMA((len(pair_groups(pairs)), sems)),
                pltpu.SemaphoreType.DMA((5, sems)),
            ],
        ),
        compiler_params=comm_params(1, "arbitrary", "arbitrary"),
        name="front",
    )(starts, lengths, tokens, wqkv, vectors, wo, wu, wd)
    n1, lines, *weights = results[3 + pieces :]
    weights = [w.reshape(-1, w.shape[-1]) for w in weights]
    return (results[:3], results[3 : 3 + pieces], [n1, lines] + weights)


TAIL = 2


def attend_back_kernel(
    slot,
    pieces,
    chunks,
    count,
    copies,
    pairs,
    start_ref,
    length_ref,
    qkv_ref,
    gm_ref,
    o_ref,
    inv_ref,
    *rest,
):
    att_hbms, rest = (rest[:pieces], rest[pieces:])
    n1_hbm, n2_hbm, gb_hbm, hid_hbm, cot_hbm, mixed_hbm, gproj_hbm, small_ref = rest[:8]
    g_ref, gqkv_ref, gwo_ref, gwu_ref, gwd_ref, gsmall_ref = rest[8:14]
    later_ref, dq_ref, dk_ref, dv_ref, left_ref, right_ref = rest[14:20]
    load_sem, att_sem = rest[20:22]
    rest = rest[22:]
    sum_refs, att_refs, ds_refs = (rest[i * pieces : (i + 1) * pieces] for i in range(3))
    rest = rest[3 * pieces :]
    step = pl.program_id(0)
    first_step = 2 * chunks + 1
    length = qkv_ref.shape[0]
    width = left_ref.shape[2]
    sequences = left_ref.shape[1] // length
    turns = pairs * sequences
    turn = jnp.maximum(step - first_step, 0)

    place = Place(count, copies)
    parts = []

    def add_part(write, by_level=False):
        at = 6 * len(parts)
        parts.append(Scatter(place, rest[at : at + 6], write, by_level))

    for c in range(chunks):

        def write_up(value, c=c):
            gwu_ref[:, c * width : (c + 1) * width] = value

        add_part(write_up)
    half_rows = gwd_ref.shape[0] // 2
    for h in range(2):

        def write_down(value, h=h):
            gwd_ref[h * half_rows : (h + 1) * half_rows, :] = value

        add_part(write_down, chunks == LEVELS)

    def write_out(value):
        gwo_ref[...] = value

    add_part(write_out)
    for pair in range(pairs - 1, TAIL - 1, -1):

        def write_pair(value, pair=pair):
            for which in range(3):
                first = which * width + pair * PAIR
                gqkv_ref[:, first : first + PAIR] = value[:, which * PAIR : (which + 1) * PAIR]

        add_part(write_pair)
    small = Reduce(place, rest[6 * len(parts) : 6 * len(parts) + 4], gsmall_ref)
    up_parts, (down0, down1, out_part) = (parts[:chunks], parts[chunks : chunks + 3])
    pair_parts = parts[chunks + 3 :]

    left_slot = [0] * chunks + [(c + 1) % 2 for c in range(chunks)] + [(chunks + 1) % 2]
    right_slot = [c % 2 for c in range(chunks)] + [chunks % 2] * chunks + [(chunks + 1) % 2]

    def chunk_of(ref, c):
        return ref.at[:, pl.ds(c * width, width)]

    left_loads = {0: n2_hbm, 2 * chunks: mixed_hbm}
    right_loads = {chunks: cot_hbm, 2 * chunks: gproj_hbm}
    for c in range(chunks):
        left_loads[chunks + c] = chunk_of(hid_hbm, c)
        right_loads[c] = chunk_of(gb_hbm, c)

    def loads(when):
        found = []
        if when in left_loads:
            at = left_slot[when]
            found.append(
                pltpu.make_async_copy(left_loads[when], left_ref.at[at], load_sem.at[at])
            )
        if when in right_loads:
            at = right_slot[when]
            found.append(
                pltpu.make_async_copy(right_loads[when], right_ref.at[at], load_sem.at[2 + at])
            )
        return found

    n1_slot = chunks % 2

    def load_n1():
        return pltpu.make_async_copy(n1_hbm, left_ref.at[n1_slot], load_sem.at[4])

    def load_att(at, half):
        seq = lax.rem(at, sequences)
        head = 2 * (pairs - 1 - lax.div(at, sequences)) + half
        return [
            pltpu.make_async_copy(
                att_hbms[i].at[seq, head], att_refs[i].at[half], att_sem.at[half * pieces + i]
            )
            for i in range(pieces)
        ]

    def begin():
        for copy in loads(0):
            copy.start()
        place.meet(copies=True)
        small.start(small_ref[...])

    def before_attention():
        load_n1().start()
        for half in range(2):
            for copy in load_att(0, half):
                copy.start()

    entries = [(0, begin), (first_step - 1, before_attention)]
    for c, part in enumerate(up_parts):
        entries += [
            (c + 2, part.after_cores),
            (2 * c + 5, part.after_columns),
            (2 * c + 8, part.after_levels),
            (2 * c + 10, part.after_copies),
        ]
    f = first_step
    late = BACK_TABLE
    names = (down0, down1, out_part) + tuple(pair_parts)
    entries += [
        (3, small.after_cores),
        (6, small.after_columns),
        (10, small.after_levels),
        (13, small.after_copies),
        (f + sequences - 1, load_n1().wait),
    ]
    left_over = []
    for part, whens in zip(names, late):
        actions = (part.after_cores, part.after_columns, part.after_levels, part.after_copies)
        for phase, (when, action) in enumerate(zip(whens, actions)):
            if when < sequences * pairs:
                entries.append((f + when, action))
            else:
                left_over.append((when, phase, action))
    at_steps(step, schedule(*entries))

    @pl.when(step < first_step)
    def _():
        left_at = jnp.zeros((), jnp.int32)
        right_at = jnp.zeros((), jnp.int32)
        for when in range(first_step):

            @pl.when(step == when)
            def _(when=when):
                if when + 1 < first_step:
                    for copy in loads(when + 1):
                        copy.start()
                for copy in loads(when):
                    copy.wait()

            left_at = jnp.where(step == when, left_slot[when], left_at)
            right_at = jnp.where(step == when, right_slot[when], right_at)
        grad = dot_tn(left_ref[left_at], right_ref[right_at]).astype(BF16)
        for when in range(first_step):

            @pl.when(step == when)
            def _(when=when):
                if when < chunks or when == 2 * chunks:
                    part = out_part if when == 2 * chunks else up_parts[when]
                    rows = width // count
                    for block in range(count):
                        part.put(block, grad[block * rows : (block + 1) * rows, :])
                    part.start()
                else:
                    blocks = count // chunks
                    for i in range(blocks):
                        block = (when - chunks) * blocks + i
                        for h, part in enumerate((down0, down1)):
                            at = (2 * i + h) * half_rows
                            part.put(block, grad[at : at + half_rows, :])
                    for part in (down0, down1):
                        if part.by_level:
                            part.core_copies()[when - chunks].start()
                        elif when == 2 * chunks - 1:
                            part.start()

    @pl.when(step >= first_step)
    def _():
        seq = lax.rem(turn, sequences)
        inputs = (qkv_ref, gm_ref, o_ref, inv_ref)
        masks = (slot, pieces, start_ref, length_ref)
        scratch = (sum_refs, att_refs, ds_refs, later_ref, dq_ref, dk_ref, dv_ref)

        @pl.when(turn < sequences)
        def _():
            for ref in sum_refs:
                ref[seq] = jnp.zeros(ref.shape[1:], F32)

        def wait_att(half):
            for copy in load_att(turn, half):
                copy.wait()

        def next_att(half):
            @pl.when(turn < turns - 1)
            def _():
                for copy in load_att(turn + 1, half):
                    copy.start()

        for ref in (dq_ref, dk_ref, dv_ref):
            ref[...] = jnp.zeros_like(ref)
        special = turn >= turns - sequences

        def plain(i, carry):
            half = 1 - i
            wait_att(half)
            head_back(half, False, seq, masks, inputs, scratch)
            next_att(half)
            return carry

        lax.fori_loop(0, jnp.where(special, 1, 2), plain, 0)

        @pl.when(special)
        def _():
            wait_att(0)
            head_back(0, True, seq, masks, inputs, scratch)
            next_att(0)

        grads = (dq_ref[...], jnp.transpose(dk_ref[...]), jnp.transpose(dv_ref[...]))
        keep = pl.ds(pl.multiple_of(seq * length, length), length)
        for which, grad in enumerate(grads):
            columns = slice(which * PAIR, (which + 1) * PAIR)
            low = grad.astype(BF16)
            g_ref[:, columns] = low
            right_ref[0, keep, columns] = low

    @pl.when((step >= first_step) & (lax.rem(turn, sequences) == sequences - 1))
    def _():
        @pl.when(turn < (pairs - TAIL) * sequences)
        def _():
            grad = dot_tn(left_ref[n1_slot], right_ref[0, :, : 3 * PAIR]).astype(BF16)
            rows = width // count
            for i, part in enumerate(pair_parts):

                @pl.when(turn == (i + 1) * sequences - 1)
                def _(part=part):
                    for block in range(count):
                        part.put(block, grad[block * rows : (block + 1) * rows, :])
                    part.start()

    @pl.when(step == pl.num_programs(0) - 1)
    def _():
        for _, _, action in sorted(left_over, key=lambda item: item[:2]):
            action()
        for part in parts + [small]:
            part.drain()


def head_back(half, first_head, seq, masks, inputs, scratch):
    slot, pieces, start_ref, length_ref = masks
    qkv_ref, gm_ref, o_ref, inv_ref = inputs
    sum_refs, att_refs, ds_refs, later_ref, dq_ref, dk_ref, dv_ref = scratch
    zero = jnp.zeros((), BF16)
    scale = jnp.asarray(SCALE, BF16)
    mask = head_mask(half)

    def scaled_grad(rows):
        return jnp.where(mask, gm_ref[rows, :].astype(F32) * inv_ref[rows, :], 0.0)

    def query_of(rows):
        return jnp.where(mask, qkv_ref[rows, :PAIR], zero) * scale

    if first_head:
        later_ref[...] = jnp.zeros_like(later_ref)
        row = lax.broadcasted_iota(jnp.int32, (ROWS, ROWS), 0)
        col = lax.broadcasted_iota(jnp.int32, (ROWS, ROWS), 1)
        triangle = (col > row).astype(BF16)
    for i in reversed(range(pieces)):
        keys = (i + 1) * slot
        for first in reversed(range(0, slot, ROWS)):
            rows = pl.ds(i * slot + first, ROWS)
            at = pl.ds(first, ROWS)
            scaled = scaled_grad(rows)
            delta = jnp.sum(scaled * o_ref[rows, :].astype(F32), axis=-1, keepdims=True)
            grad_attention = dot_nt(scaled.astype(BF16), qkv_ref[:keys, 2 * PAIR :])
            grad_logits = att_refs[i][half, at, :].astype(F32) * (grad_attention - delta)
            if first_head:
                total = sum_refs[i][seq, at, :] + grad_logits
                grad_selected = -(later_ref[:, :keys] + triangle_sum(triangle, total))
                later_ref[:, :keys] += column_sum(total)
                _, chosen = block_masks(
                    start_ref, length_ref, seq, pieces, i * slot + first, keys
                )
                positive = dot_nt(query_of(rows), qkv_ref[:keys, PAIR : 2 * PAIR]) > 0
                grad_logits = grad_logits + jnp.where(chosen & positive, grad_selected, 0.0)
            else:
                sum_refs[i][seq, at, :] += grad_logits
            ds_refs[i][at, :] = grad_logits.astype(BF16)
        rows = pl.ds(i * slot, slot)
        key = jnp.where(mask, qkv_ref[:keys, PAIR : 2 * PAIR], zero) * scale
        query_part = dot(ds_refs[i][...], key)
        key_part = dot_tn(query_of(rows), ds_refs[i][...])
        value_part = dot_tn(scaled_grad(rows).astype(BF16), att_refs[i][half])
        dq_ref[rows, :] += query_part
        dk_ref[:, :keys] += key_part
        dv_ref[:, :keys] += value_part


def attend_back(
    projected, starts, lengths, grad_mixed, mixed, inverse, attention, kept, small, devices, copies
):
    n1, n2, grad_before, hidden, cotangent, grad_proj = kept
    sequences, pieces = starts.shape
    count, columns = projected.shape
    length = count // sequences
    slot = length // pieces
    width = columns // 3
    pairs = width // PAIR
    chunks = hidden.shape[1] // width
    first_step = 2 * chunks + 1
    rows = width // devices
    down_rows = hidden.shape[1] // devices
    lines = small.shape[0]

    def part(size):
        def index(step, a, b):
            at = jnp.maximum(step - first_step, 0)
            return (lax.rem(at, sequences), pairs - 1 - lax.div(at, sequences))

        return pl.BlockSpec((length, size * PAIR), index)

    anywhere = pl.BlockSpec(memory_space=pl.ANY)

    def fixed(shape):
        return pl.BlockSpec(shape, lambda *_: (0,) * len(shape))

    results = [
        (rows, columns),
        (rows, width),
        (rows, chunks * width),
        (down_rows, width),
        (lines, 1, width),
    ]
    slots = [(slot, (i + 1) * slot) for i in range(pieces)]
    scratch = [
        pltpu.VMEM((1, length), F32),
        pltpu.VMEM((length, PAIR), F32),
        pltpu.VMEM((PAIR, length), F32),
        pltpu.VMEM((PAIR, length), F32),
        pltpu.VMEM((2, count, width), BF16),
        pltpu.VMEM((2, count, width), BF16),
        pltpu.SemaphoreType.DMA((5,)),
        pltpu.SemaphoreType.DMA((2 * pieces,)),
    ]
    scratch += [pltpu.VMEM((sequences,) + shape, F32) for shape in slots]
    scratch += [pltpu.VMEM((2,) + shape, BF16) for shape in slots]
    scratch += [pltpu.VMEM(shape, BF16) for shape in slots]
    for piece_rows in [rows] * chunks + [down_rows // 2] * 2 + [rows]:
        scratch += scatter_scratch(devices, copies, piece_rows, width)
    for _ in range(pairs - TAIL):
        scratch += scatter_scratch(devices, copies, rows, 3 * PAIR)
    scratch += reduce_scratch(devices, copies, lines, width)
    return pl.pallas_call(
        functools.partial(
            attend_back_kernel, slot, pieces, chunks, devices, copies, pairs
        ),
        out_shape=[jax.ShapeDtypeStruct((count, columns), BF16)]
        + [jax.ShapeDtypeStruct(shape, F32) for shape in results],
        grid_spec=pltpu.PrefetchScalarGridSpec(
            num_scalar_prefetch=2,
            grid=(first_step + sequences * pairs,),
            in_specs=[part(3)]
            + [part(1)] * 3
            + [anywhere] * (pieces + 7)
            + [fixed((lines, 1, width))],
            out_specs=[part(3)] + [fixed(shape) for shape in results],
            scratch_shapes=scratch,
        ),
        compiler_params=comm_params(2, "arbitrary"),
        name="attend_back",
    )(
        starts,
        lengths,
        projected,
        grad_mixed,
        mixed,
        inverse,
        *attention,
        n1,
        n2,
        grad_before,
        hidden,
        cotangent,
        mixed,
        grad_proj,
        small,
    )


def gelu_and_slope(values):
    square = values * values
    inner = GELU_IN * values * (1.0 + GELU_CUBE * square)
    bent = jnp.tanh(inner)
    half = 0.5 * (1.0 + bent)
    slope = half + 0.5 * values * (1.0 - bent * bent) * (
        GELU_IN * (1.0 + 3.0 * GELU_CUBE * square)
    )
    return (values * half, slope)


def feed_kernel(
    chunk,
    x_ref,
    mixed_ref,
    cot_ref,
    gain_ref,
    shift_ref,
    up_bias_ref,
    down_bias_ref,
    wo_hbm,
    wu_hbm,
    wd_hbm,
    out_ref,
    gmid_ref,
    gmix_ref,
    small_ref,
    n2_ref,
    hid_ref,
    gb_ref,
    gproj_ref,
    wo_ref,
    wu_ref,
    wd_ref,
    acc_ref,
    gnorm_ref,
    mid_ref,
    load_sem,
):
    step = pl.program_id(0)
    chunks = wu_ref.shape[0]

    def load_out():
        return pltpu.make_async_copy(wo_hbm, wo_ref, load_sem.at[0])

    def load_up(c):
        return pltpu.make_async_copy(
            wu_hbm.at[:, pl.ds(c * chunk, chunk)], wu_ref.at[c], load_sem.at[1 + 2 * c]
        )

    def load_down(c):
        return pltpu.make_async_copy(
            wd_hbm.at[pl.ds(c * chunk, chunk), :], wd_ref.at[c], load_sem.at[2 + 2 * c]
        )

    @pl.when(step == 0)
    def _():
        load_out().start()
        for c in range(chunks):
            load_up(c).start()
            load_down(c).start()
        small_ref[...] = jnp.zeros_like(small_ref)
        load_out().wait()

    mid_ref[...] = x_ref[...].astype(F32) + dot(mixed_ref[...], wo_ref[...])

    @pl.when(step == 0)
    def _():
        for c in range(chunks):
            load_up(c).wait()
            load_down(c).wait()

    normed, _ = normalize(mid_ref[...])
    n2_ref[...] = (normed * gain_ref[...] + shift_ref[...]).astype(BF16)
    def open_chunk(c):
        before = dot(n2_ref[...], wu_ref[c]) + up_bias_ref[c]
        grad_hidden = dot_nt(cot_ref[...], wd_ref[c]).astype(BF16)
        return (before, grad_hidden)

    ahead = open_chunk(0)
    for c in range(chunks):
        before, grad_hidden = ahead
        if c + 1 < chunks:
            ahead = open_chunk(c + 1)
        columns = slice(c * chunk, (c + 1) * chunk)
        hidden, slope = gelu_and_slope(before)
        hidden = hidden.astype(BF16)
        hid_ref[:, columns] = hidden
        grad_before = (grad_hidden.astype(F32) * slope).astype(BF16)
        gb_ref[:, columns] = grad_before
        small_ref[3 + c] += column_sum(grad_before.astype(F32))
        down = dot(hidden, wd_ref[c])
        back = dot_nt(grad_before, wu_ref[c])
        if c == 0:
            acc_ref[...] = down
            gnorm_ref[...] = back
        else:
            acc_ref[...] += down
            gnorm_ref[...] += back

    out_ref[...] = (mid_ref[...] + (acc_ref[...] + down_bias_ref[...])).astype(BF16)
    grad_normed = gnorm_ref[...]
    normed, inverse = normalize(mid_ref[...])
    cot = cot_ref[...].astype(F32)
    small_ref[0] += column_sum(grad_normed * normed)
    small_ref[1] += column_sum(grad_normed)
    small_ref[2] += column_sum(cot)
    grad_middle = cot + norm_back(grad_normed * gain_ref[...], normed, inverse)
    gmid_ref[...] = grad_middle
    grad_proj = grad_middle.astype(BF16)
    gproj_ref[...] = grad_proj
    gmix_ref[...] = dot_nt(grad_proj, wo_ref[...]).astype(BF16)


def vector_line(row):
    return lambda width: pl.BlockSpec((None, 1, width), lambda *_: (row, 0, 0))


def feed(tokens, mixed, cotangent, vectors, wo, wu, wd):
    count, width = tokens.shape
    hidden = wu.shape[1]
    block = 512
    chunk = width
    chunks = hidden // chunk
    rows = pl.BlockSpec((block, width), lambda i: (i, 0))
    anywhere = pl.BlockSpec(memory_space=pl.ANY)
    wide = pl.BlockSpec((block, hidden), lambda i: (i, 0))

    def low(columns):
        return jax.ShapeDtypeStruct((count, columns), BF16)

    return pl.pallas_call(
        functools.partial(feed_kernel, chunk),
        out_shape=[
            low(width),
            jax.ShapeDtypeStruct((count, width), F32),
            low(width),
            jax.ShapeDtypeStruct((3 + chunks, 1, width), F32),
            low(width),
            low(hidden),
            low(hidden),
            low(width),
        ],
        grid=(count // block,),
        in_specs=[
            rows,
            rows,
            rows,
            vector_line(GAIN2)(width),
            vector_line(SHIFT2)(width),
            pl.BlockSpec((chunks, 1, chunk), lambda i: (0, 0, 0)),
            vector_line(DOWN_BIAS)(width),
            anywhere,
            anywhere,
            anywhere,
        ],
        out_specs=[
            rows,
            rows,
            rows,
            pl.BlockSpec((3 + chunks, 1, width), lambda i: (0, 0, 0)),
            rows,
            wide,
            wide,
            rows,
        ],
        scratch_shapes=[
            pltpu.VMEM(wo.shape, BF16),
            pltpu.VMEM((chunks, width, chunk), BF16),
            pltpu.VMEM((chunks, chunk, width), BF16),
            pltpu.VMEM((block, width), F32),
            pltpu.VMEM((block, width), F32),
            pltpu.VMEM((block, width), F32),
            pltpu.SemaphoreType.DMA((1 + 2 * chunks,)),
        ],
        compiler_params=params("arbitrary"),
        name="feed",
    )(
        tokens,
        mixed,
        cotangent,
        vectors,
        vectors,
        vectors,
        vectors,
        wo,
        wu,
        wd,
    )


def input_kernel(
    count,
    copies,
    gmid_ref,
    gain_ref,
    shift_ref,
    rest_ref,
    x_hbm,
    n1_hbm,
    g_hbm,
    w_hbm,
    gx_ref,
    gw_ref,
    gsmall_ref,
    x_ref,
    n1_ref,
    g_ref,
    w_ref,
    small_ref,
    load_sem,
    *rest,
):
    step = pl.program_id(0)
    total, width = x_ref.shape
    columns = w_ref.shape[1]
    block = gx_ref.shape[0]
    first = TAIL * 3 * PAIR
    place = Place(count, copies)

    def write(value):
        gw_ref[...] = rest_ref[...]
        for at in range(3 * TAIL):
            to = (at % 3) * width + (at // 3) * PAIR
            gw_ref[:, to : to + PAIR] = value[:, at * PAIR : (at + 1) * PAIR]

    part = Scatter(place, rest[:6], write)
    small = Reduce(place, rest[6:10], gsmall_ref)

    def loads():
        near, far = (pl.ds(0, first), pl.ds(first, columns - first))
        pairs = [
            (n1_hbm, n1_ref),
            (g_hbm.at[:, near], g_ref.at[:, near]),
            (x_hbm, x_ref),
            (g_hbm.at[:, far], g_ref.at[:, far]),
            (w_hbm, w_ref),
        ]
        return [
            pltpu.make_async_copy(source, target, load_sem.at[i])
            for i, (source, target) in enumerate(pairs)
        ]

    def begin():
        for copy in loads():
            copy.start()
        place.meet(copies=True)
        small_ref[...] = jnp.zeros_like(small_ref)
        for copy in loads()[:2]:
            copy.wait()
        grad = dot_tn(n1_ref[...], g_ref[:, :first]).astype(BF16)
        rows = width // count
        for i in range(count):
            part.put(i, grad[i * rows : (i + 1) * rows, :])
        part.start()
        for copy in loads()[2:]:
            copy.wait()

    steps = total // block
    table = schedule(
        (0, begin),
        (1, part.after_cores),
        (min(3, steps - 1), part.after_columns),
    )
    at_steps(step, table)

    normed, inverse = normalize(
        x_ref[pl.ds(pl.multiple_of(step * block, block), block), :].astype(F32)
    )
    grads = g_ref[pl.ds(pl.multiple_of(step * block, block), block), :]
    grad_normed = dot_nt(grads, w_ref[...])
    small_ref[0] += column_sum(grad_normed * normed)
    small_ref[1] += column_sum(grad_normed)
    gx_ref[...] = gmid_ref[...] + norm_back(grad_normed * gain_ref[...], normed, inverse)

    @pl.when(step == steps - 1)
    def _():
        small.start(small_ref[...])
        small.after_cores()
        part.after_levels()
        small.after_columns()
        part.after_copies()
        small.after_levels()
        small.after_copies()
        part.drain()
        small.drain()


def input_back(tokens, n1, grad_middle, grads, grad_rest, vectors, weight, devices, copies):
    count, width = tokens.shape
    block = 512
    shard = width // devices
    rows = pl.BlockSpec((block, width), lambda i: (i, 0))
    own = pl.BlockSpec((shard, 3 * width), lambda i: (0, 0))
    anywhere = pl.BlockSpec(memory_space=pl.ANY)
    scratch = [
        pltpu.VMEM((count, width), BF16),
        pltpu.VMEM((count, width), BF16),
        pltpu.VMEM((count, 3 * width), BF16),
        pltpu.VMEM(weight.shape, BF16),
        pltpu.VMEM((2, 1, width), F32),
        pltpu.SemaphoreType.DMA((5,)),
    ]
    scratch += scatter_scratch(devices, copies, shard, TAIL * 3 * PAIR)
    scratch += reduce_scratch(devices, copies, 2, width)
    return pl.pallas_call(
        functools.partial(input_kernel, devices, copies),
        out_shape=[
            jax.ShapeDtypeStruct((count, width), F32),
            jax.ShapeDtypeStruct((shard, 3 * width), F32),
            jax.ShapeDtypeStruct((2, 1, width), F32),
        ],
        grid=(count // block,),
        in_specs=[rows, vector_line(GAIN1)(width), vector_line(SHIFT1)(width), own]
        + [anywhere] * 4,
        out_specs=[
            rows,
            own,
            pl.BlockSpec((2, 1, width), lambda i: (0, 0, 0)),
        ],
        scratch_shapes=scratch,
        compiler_params=comm_params(3, "arbitrary"),
        name="input_back",
    )(grad_middle, vectors, vectors, grad_rest, tokens, n1, grads, weight)


def local(
    tokens,
    piece_start,
    piece_length,
    query_key_value,
    output_weight,
    up_weight,
    down_weight,
    first_gain,
    first_shift,
    second_gain,
    second_shift,
    up_bias,
    down_bias,
    cotangent,
):
    width = tokens.shape[1]
    devices, copies = (lax.axis_size("fsdp"), lax.axis_size("rep"))
    index = lax.axis_index("fsdp")

    lines = jnp.stack([first_gain, first_shift, second_gain, second_shift, down_bias])
    own = lax.dynamic_update_slice(
        jnp.zeros((LINES - up_bias.shape[0] * devices // width, width), BF16),
        lines,
        (0, index * lines.shape[1]),
    )
    wide = lax.dynamic_update_slice(
        jnp.zeros((devices * up_bias.shape[0],), BF16), up_bias, (index * up_bias.shape[0],)
    )
    own = jnp.concatenate([wide.reshape(-1, width), own], axis=0)

    (projected, mixed, inverse), attention, (n1, vectors, wqkv, wo, wu, wd) = front(
        tokens,
        piece_start,
        piece_length,
        query_key_value,
        own,
        output_weight,
        up_weight,
        down_weight,
        devices,
        copies,
    )
    block_output, grad_middle, grad_mixed, small2, n2, hidden, grad_before, grad_proj = feed(
        tokens, mixed, cotangent, vectors, wo, wu, wd
    )
    grads, grad_rest, gwo, gwu, gwd, small2 = attend_back(
        projected,
        piece_start,
        piece_length,
        grad_mixed,
        mixed,
        inverse,
        attention,
        (n1, n2, grad_before, hidden, cotangent, grad_proj),
        small2,
        devices,
        copies,
    )
    grad_tokens, gwqkv, small1 = input_back(
        tokens, n1, grad_middle, grads, grad_rest, vectors, wqkv, devices, copies
    )

    def mine(values):
        values = values.reshape(-1)
        size = values.shape[0] // devices
        return lax.dynamic_slice(values, (index * size,), (size,))

    return (
        block_output,
        grad_tokens,
        gwqkv,
        gwo,
        gwu,
        gwd,
        mine(small1[0]),
        mine(small1[1]),
        mine(small2[0]),
        mine(small2[1]),
        mine(small2[3:]),
        mine(small2[2]),
    )


def solution(mesh):
    rows = P(("fsdp", "rep"), None)
    matrix = P("fsdp", None)
    vector = P("fsdp")
    return jax.shard_map(
        local,
        mesh=mesh,
        in_specs=(rows,) * 3 + (matrix,) * 4 + (vector,) * 6 + (rows,),
        out_specs=(rows,) * 2 + (matrix,) * 4 + (vector,) * 6,
        check_vma=False,
    )
```

```python
import functools

import jax
import jax.numpy as jnp
from jax import lax
from jax.experimental import pallas as pl
from jax.experimental.pallas import tpu as pltpu
from jax.sharding import PartitionSpec as P

HEAD_DIM = 64
PAIR = 2 * HEAD_DIM
ROWS = 256
MASKED_VALUE = -1e30
EPSILON = 1e-05
SCALE = HEAD_DIM**-0.5
GAIN1, SHIFT1, GAIN2, SHIFT2, DOWN_BIAS = (4, 5, 6, 7, 8)
LINES = 16
FRONT_TABLE = ((2, 4, 5, 7, 8), (4, 6, 7, 9, 10), (6, 8, 9, 11, 11))
BACK_TABLE = ((0, 3, 7, 9), (0, 5, 9, 11), (1, 6, 10, 11), (5, 8, 11, 12), (9, 11, 12, 13))
GELU_IN = 0.7978845608028654
GELU_CUBE = 0.044715
VMEM_LIMIT = 67043328

F32 = jnp.float32
BF16 = jnp.bfloat16


def dot(left, right):
    return lax.dot_general(left, right, (((1,), (0,)), ((), ())), preferred_element_type=F32)


def dot_nt(left, right):
    return lax.dot_general(left, right, (((1,), (1,)), ((), ())), preferred_element_type=F32)


def dot_tn(left, right):
    return lax.dot_general(left, right, (((0,), (0,)), ((), ())), preferred_element_type=F32)


def row_mean(values):
    return jnp.mean(values, axis=-1, keepdims=True)


def normalize(values):
    center = values - row_mean(values)
    inverse = lax.rsqrt(row_mean(center * center) + EPSILON)
    return (center * inverse, inverse)


def norm_back(grad, normed, inverse):
    return (grad - row_mean(grad) - normed * row_mean(grad * normed)) * inverse


def column_sum(values):
    return jnp.sum(values, axis=0, keepdims=True)


def params(*semantics):
    return pltpu.CompilerParams(dimension_semantics=semantics, vmem_limit_bytes=VMEM_LIMIT)


def comm_params(number, *semantics):
    return pltpu.CompilerParams(
        dimension_semantics=semantics,
        vmem_limit_bytes=VMEM_LIMIT,
        collective_id=number,
        has_side_effects=True,
    )


MESH = pl.DeviceIdType.MESH
LEVELS = 4
CORES = 2


class Place:
    def __init__(self, count, copies):
        self.count, self.copies = (count, copies)
        self.columns = count // (LEVELS * CORES)
        self.index = lax.axis_index("fsdp")
        self.rep = lax.axis_index("rep")
        self.core = lax.rem(self.index, CORES)
        chip = lax.div(self.index, CORES)
        self.column = lax.rem(chip, self.columns)
        self.level = lax.div(chip, self.columns)
        self.half = lax.rem(self.rep, 2)

    def block(self, up=0, across=0, other=0):
        level = lax.rem(self.level + (up + LEVELS), LEVELS)
        column = lax.rem(self.column + (across + self.columns), self.columns)
        core = lax.rem(self.core + other, CORES)
        return (level * self.columns + column) * CORES + core

    def device(self, up=0, across=0, other=0, copy=0):
        return (self.block(up, across, other), lax.rem(self.rep + copy, self.copies))

    def twin(self):
        return (self.index, self.rep + 1 - 2 * self.half)

    def meet(self, twin=False, copies=False):
        others = [self.device(up=up) for up in range(1, LEVELS)]
        others += [self.device(across=across) for across in range(1, self.columns)]
        others += [self.device(other=1)]
        if twin:
            others += [self.twin()]
        if copies:
            others += [self.device(copy=copy) for copy in range(1, self.copies)]
        barrier = pltpu.get_barrier_semaphore()
        for other in others:
            pl.semaphore_signal(barrier, inc=1, device_id=other, device_id_type=MESH)
        pl.semaphore_wait(barrier, len(others))


def send(source, target, sems, slot, device):
    return pltpu.make_async_remote_copy(
        src_ref=source,
        dst_ref=target,
        send_sem=sems.at[2 * slot],
        recv_sem=sems.at[2 * slot + 1],
        device_id=device,
        device_id_type=MESH,
    )


def gather_sems(count):
    across = count // (LEVELS * CORES) - 1
    return 2 * (2 * (LEVELS - 1) + 2 * across + 1) + 1


class Gather:
    def __init__(self, place, source, target, first, columns, shared, sems):
        self.place, self.source, self.target = (place, source, target)
        self.sems, self.shared, self.across = (sems, shared, columns)
        rows = source.shape[0]
        base = place.core * (target.shape[2] // CORES) + first
        third = rows // 3
        half = place.half
        self.whole = pl.ds(pl.multiple_of(base, rows), rows)
        if shared:
            self.near = pl.ds(pl.multiple_of(half * third, third), 2 * third)
            self.part = pl.ds(pl.multiple_of(base + half * third, third), 2 * third)
            self.give = pl.ds(pl.multiple_of(base + half * (2 * third), third), third)
        else:
            self.near, self.part = (pl.ds(0, rows), self.whole)

    def held(self, level, column, rows):
        return self.target.at[level, column, rows, self.across]

    def send(self, ref, slot, device):
        return send(ref, ref, self.sems, slot, device)

    def level_copies(self):
        place = self.place
        return [
            send(
                self.source.at[self.near, :],
                self.held(place.level, place.column, self.part),
                self.sems,
                up - 1,
                place.device(up=up),
            )
            for up in range(1, LEVELS)
        ]

    def column_copies(self):
        place = self.place
        ref = self.held(slice(None), place.column, self.part)
        return [
            self.send(ref, LEVELS - 2 + across, place.device(across=across))
            for across in range(1, place.columns)
        ]

    def twin_copies(self, near):
        if not self.shared:
            return []
        place = self.place
        base = LEVELS - 1 + place.columns - 1
        if near:
            return [
                self.send(
                    self.held(
                        lax.rem(place.level + (LEVELS - up), LEVELS), place.column, self.give
                    ),
                    base + up - 1,
                    place.twin(),
                )
                for up in range(1, LEVELS)
            ]
        return [
            self.send(
                self.held(
                    slice(None),
                    lax.rem(place.column + (place.columns - across), place.columns),
                    self.give,
                ),
                base + LEVELS - 2 + across,
                place.twin(),
            )
            for across in range(1, place.columns)
        ]

    def core_copy(self):
        slot = 2 * (LEVELS - 1) + 2 * (self.place.columns - 1)
        ref = self.held(slice(None), slice(None), self.whole)
        return self.send(ref, slot, self.place.device(other=1))

    def own(self):
        place = self.place
        last = gather_sems(place.count) - 1
        return pltpu.make_async_copy(
            self.source, self.held(place.level, place.column, self.whole), self.sems.at[last]
        )

    def start(self):
        for copy in self.level_copies():
            copy.start()
        self.own().start()

    def after_levels(self):
        self.own().wait()
        for copy in self.level_copies():
            copy.wait_recv()
        for copy in self.column_copies() + self.twin_copies(True):
            copy.start()

    def after_columns(self):
        for copy in self.column_copies():
            copy.wait_recv()
        for copy in self.twin_copies(False):
            copy.start()
        if not self.shared:
            self.core_copy().start()

    def after_twins(self):
        if self.shared:
            for copy in self.twin_copies(True) + self.twin_copies(False):
                copy.wait_recv()
            self.core_copy().start()

    def finish(self):
        self.core_copy().wait_recv()

    def drain(self):
        copies = self.level_copies() + self.column_copies()
        for copy in copies + self.twin_copies(True) + self.twin_copies(False):
            copy.wait_send()
        self.core_copy().wait_send()


def scatter_slots(count, copies):
    across = count // (CORES * LEVELS) - 1
    return LEVELS + across + (LEVELS - 1) + (copies - 1)


def scatter_scratch(count, copies, rows, columns):
    across = count // (CORES * LEVELS)
    return [
        pltpu.VMEM((LEVELS, across, CORES, rows, columns), BF16),
        pltpu.VMEM((LEVELS, across, rows, columns), BF16),
        pltpu.VMEM((max(across - 1, 1), LEVELS, rows, columns), BF16),
        pltpu.VMEM((LEVELS - 1, rows, columns), BF16),
        pltpu.VMEM((copies, rows, columns), BF16),
        pltpu.SemaphoreType.DMA((2 * scatter_slots(count, copies),)),
    ]


def add_low(left, right):
    return (left.astype(F32) + right.astype(F32)).astype(BF16)


class Scatter:
    def __init__(self, place, refs, write, by_level=False):
        self.place, self.write, self.by_level = (place, write, by_level)
        self.held, self.from_core, self.from_column, self.from_level, self.parts, self.sems = refs

    def put(self, block, value):
        chip = block // CORES
        self.held[chip // self.place.columns, chip % self.place.columns, block % CORES] = value

    def core_copies(self):
        place = self.place
        other = 1 - place.core
        if not self.by_level:
            source = self.held.at[:, :, other]
            return [send(source, self.from_core, self.sems, 0, place.device(other=1))]
        return [
            send(
                self.held.at[level, :, other],
                self.from_core.at[level],
                self.sems,
                level,
                place.device(other=1),
            )
            for level in range(LEVELS)
        ]

    def column_copies(self):
        place = self.place
        return [
            send(
                self.held.at[:, lax.rem(place.column + across, place.columns), place.core],
                self.from_column.at[across - 1],
                self.sems,
                LEVELS + across - 1,
                place.device(across=across),
            )
            for across in range(1, place.columns)
        ]

    def level_copies(self):
        place = self.place
        base = LEVELS + place.columns - 1
        return [
            send(
                self.held.at[lax.rem(place.level + up, LEVELS), place.column, place.core],
                self.from_level.at[up - 1],
                self.sems,
                base + up - 1,
                place.device(up=up),
            )
            for up in range(1, LEVELS)
        ]

    def rep_copies(self):
        place = self.place
        base = 2 * LEVELS + place.columns - 2
        mine = self.parts.at[place.rep]
        return [
            send(mine, mine, self.sems, base + copy - 1, place.device(copy=copy))
            for copy in range(1, place.copies)
        ]

    def start(self):
        for copy in self.core_copies():
            copy.start()

    def after_cores(self):
        place = self.place
        for copy in self.core_copies():
            copy.wait_recv()

        def add(i, carry):
            level, column = (lax.div(i, place.columns), lax.rem(i, place.columns))
            self.held[level, column, place.core] = add_low(
                self.held[level, column, place.core], self.from_core[level, column]
            )
            return carry

        lax.fori_loop(0, LEVELS * place.columns, add, 0)
        for copy in self.column_copies():
            copy.start()

    def after_columns(self):
        place = self.place
        for copy in self.column_copies():
            copy.wait_recv()

        def add(level, carry):
            total = self.held[level, place.column, place.core].astype(F32)
            for across in range(place.columns - 1):
                total = total + self.from_column[across, level].astype(F32)
            self.held[level, place.column, place.core] = total.astype(BF16)
            return carry

        lax.fori_loop(0, LEVELS, add, 0)
        for copy in self.level_copies():
            copy.start()

    def after_levels(self):
        place = self.place
        for copy in self.level_copies():
            copy.wait_recv()
        total = self.held[place.level, place.column, place.core].astype(F32)
        for level in range(LEVELS - 1):
            total = total + self.from_level[level].astype(F32)
        self.parts[place.rep] = total.astype(BF16)
        for copy in self.rep_copies():
            copy.start()

    def after_copies(self):
        for copy in self.rep_copies():
            copy.wait_recv()
        total = self.parts[0].astype(F32)
        for rep in range(1, self.place.copies):
            total = total + self.parts[rep].astype(F32)
        self.write(total)

    def drain(self):
        copies = self.core_copies() + self.column_copies() + self.level_copies()
        for copy in copies + self.rep_copies():
            copy.wait_send()


def reduce_scratch(count, copies, lines, width):
    across = count // (CORES * LEVELS)
    slots = 1 + (across - 1) + (LEVELS - 1) + (copies - 1)
    return [
        pltpu.VMEM((3, lines, 1, width), F32),
        pltpu.VMEM((1 + across - 1 + LEVELS - 1, lines, 1, width), F32),
        pltpu.VMEM((copies, lines, 1, width), F32),
        pltpu.SemaphoreType.DMA((2 * slots,)),
    ]


class Reduce:
    def __init__(self, place, refs, out):
        self.place, self.out = (place, out)
        self.sums, self.landed, self.parts, self.sems = refs

    def group(self, phase):
        place = self.place
        if phase == 0:
            targets = [place.device(other=1)]
            first = 0
        elif phase == 1:
            targets = [place.device(across=across) for across in range(1, place.columns)]
            first = 1
        else:
            targets = [place.device(up=up) for up in range(1, LEVELS)]
            first = place.columns
        return [
            send(self.sums.at[phase], self.landed.at[first + i], self.sems, first + i, target)
            for i, target in enumerate(targets)
        ]

    def rep_copies(self):
        place = self.place
        base = place.columns + LEVELS - 1
        mine = self.parts.at[place.rep]
        return [
            send(mine, mine, self.sems, base + copy - 1, place.device(copy=copy))
            for copy in range(1, place.copies)
        ]

    def start(self, value):
        self.sums[0] = value
        for copy in self.group(0):
            copy.start()

    def next(self, phase):
        copies = self.group(phase)
        for copy in copies:
            copy.wait_recv()
        first = (0, 1, self.place.columns)[phase]
        total = self.sums[phase]
        for i in range(len(copies)):
            total = total + self.landed[first + i]
        if phase < 2:
            self.sums[phase + 1] = total
            for copy in self.group(phase + 1):
                copy.start()
        else:
            self.parts[self.place.rep] = total
            for copy in self.rep_copies():
                copy.start()

    def after_cores(self):
        self.next(0)

    def after_columns(self):
        self.next(1)

    def after_levels(self):
        self.next(2)

    def after_copies(self):
        for copy in self.rep_copies():
            copy.wait_recv()
        total = self.parts[0]
        for rep in range(1, self.place.copies):
            total = total + self.parts[rep]
        self.out[...] = total

    def drain(self):
        for copy in self.group(0) + self.group(1) + self.group(2) + self.rep_copies():
            copy.wait_send()


def label_of(position, start_ref, length_ref, seq, pieces):
    label = jnp.zeros(position.shape, jnp.int32)
    for piece in range(pieces):
        start = start_ref[seq, piece]
        inside = (position >= start) & (position < start + length_ref[seq, piece])
        label = jnp.where(inside, piece + 1, label)
    return label


def key_count(first_row, slot):
    return (first_row // slot + 1) * slot


def block_masks(start_ref, length_ref, seq, pieces, first_row, keys):
    query_pos = first_row + lax.broadcasted_iota(jnp.int32, (ROWS, 1), 0)
    key_pos = lax.broadcasted_iota(jnp.int32, (1, keys), 1)
    query_label = label_of(query_pos, start_ref, length_ref, seq, pieces)
    key_label = label_of(key_pos, start_ref, length_ref, seq, pieces)
    query_label = jnp.where(query_label > 0, query_label, -1)
    allowed = (key_pos <= query_pos) | (query_label == key_label)
    chosen = allowed & (key_pos != 0) & (key_pos != query_pos)
    return (allowed, chosen)


def triangle_sum(triangle, values):
    upper = values.astype(BF16)
    rest = values - upper.astype(F32)
    middle = rest.astype(BF16)
    lower = (rest - middle.astype(F32)).astype(BF16)
    return dot(triangle, upper) + dot(triangle, middle) + dot(triangle, lower)


def head_mask(half):
    lane = lax.broadcasted_iota(jnp.int32, (1, PAIR), 1)
    first = half * HEAD_DIM
    return (lane >= first) & (lane < first + HEAD_DIM)


def at_steps(step, table):
    for when in sorted(set(table)):
        @pl.when(step == when)
        def _(when=when):
            for action in table[when]:
                action()


def schedule(*entries):
    table = {}
    for when, action in entries:
        table.setdefault(when, []).append(action)
    return table


def pair_groups(pairs):
    groups, at = ([], 0)
    for size in [1, 1] + [2] * pairs:
        if at < pairs:
            groups.append(range(at, min(at + size, pairs)))
            at += size
    return groups


def front_kernel(
    slot,
    pieces,
    count,
    copies,
    pairs,
    start_ref,
    length_ref,
    x_hbm,
    wqkv_hbm,
    vec_hbm,
    wo_hbm,
    wu_hbm,
    wd_hbm,
    qkv_ref,
    o_ref,
    inv_ref,
    *rest,
):
    att_refs, rest = (rest[:pieces], rest[pieces:])
    n1_hbm, vec_ref, full_w, full_o, full_u, full_d = rest[:6]
    x_ref, n1_ref, all_ref, stage_ref, w_ref, bias_ref, prefix_ref = rest[6:13]
    stage_sems, load_sems, vec_sems, w_sems, rest_sems = rest[13:]
    pair, seq = (pl.program_id(0), pl.program_id(1))
    sequences = pl.num_programs(1)
    step = pair * sequences + seq
    length = qkv_ref.shape[0]
    width = x_ref.shape[1]
    sequence_count = x_ref.shape[0] // length
    lines = vec_hbm.shape[0]
    zero = jnp.zeros((), BF16)
    place = Place(count, copies)
    twins = copies % 2 == 0

    vec = Gather(place, vec_hbm, all_ref, 0, pl.ds(0, width), False, vec_sems)
    groups = pair_groups(pairs)
    gathers = []
    for i, group in enumerate(groups):
        columns = pl.ds(group[0] * 3 * PAIR, len(group) * 3 * PAIR)
        shared = twins and i > 2 and wqkv_hbm.shape[0] % 48 == 0
        source = stage_ref.at[:, columns]
        gathers.append(Gather(place, source, full_w, 0, columns, shared, w_sems.at[i]))
    cuts = []
    for shard, full, cut_rows, cut_columns in (
        (wo_hbm, full_o, 1, 1),
        (wu_hbm, full_u, 1, 2),
        (wd_hbm, full_d, 2, 1),
    ):
        rows, columns = (shard.shape[0] // cut_rows, shard.shape[1] // cut_columns)
        for i in range(cut_rows):
            for j in range(cut_columns):
                across = pl.ds(j * columns, columns)
                source = shard.at[pl.ds(i * rows, rows), across]
                cuts.append(
                    Gather(place, source, full, i * rows, across, twins, rest_sems.at[len(cuts)])
                )

    def stage_copies():
        found = []
        for p in range(pairs):
            for which in range(3):
                at = 3 * p + which
                found.append(
                    pltpu.make_async_copy(
                        wqkv_hbm.at[:, pl.ds(which * width + p * PAIR, PAIR)],
                        stage_ref.at[:, pl.ds(at * PAIR, PAIR)],
                        stage_sems.at[at],
                    )
                )
        return found

    def load_x():
        return pltpu.make_async_copy(x_hbm, x_ref, load_sems.at[0])

    def keep_n1():
        return pltpu.make_async_copy(n1_ref, n1_hbm, load_sems.at[1])

    def load_w(p):
        return pltpu.make_async_copy(
            full_w.at[:, :, :, pl.ds(p * 3 * PAIR, 3 * PAIR)],
            w_ref.at[p % 2],
            load_sems.at[2 + p % 2],
        )

    def norm_rows(which):
        gain, shift = (vec_ref[GAIN1], vec_ref[SHIFT1])

        def body(i, carry):
            at = pl.ds(pl.multiple_of(which * length + i * ROWS, ROWS), ROWS)
            normed, _ = normalize(x_ref[at, :].astype(F32))
            n1_ref[at, :] = (normed * gain + shift).astype(BF16)
            return carry

        lax.fori_loop(0, length // ROWS, body, 0)
        if which == sequence_count - 1:
            keep_n1().start()

    def begin():
        for copy in stage_copies():
            copy.start()
        load_x().start()
        place.meet(twin=twins)
        vec.start()
        for copy in stage_copies():
            copy.wait()
        for gather in gathers + cuts:
            gather.start()
        vec.after_levels()
        gathers[0].after_levels()
        vec.after_columns()
        gathers[0].after_columns()
        gathers[1].after_levels()
        vec.finish()
        vectors = jnp.zeros((lines, width), F32)
        for chip in range(count // CORES):
            both = all_ref[chip // place.columns, chip % place.columns].astype(F32)
            vectors = vectors + both[:lines] + both[lines:]
        for line in range(lines):
            vec_ref[line] = vectors[line : line + 1, :]
        load_x().wait()
        gathers[0].finish()
        load_w(0).start()
        norm_rows(0)
        gathers[1].after_columns()
        load_w(0).wait()

    def ready(p):
        for group, gather in zip(groups, gathers):
            if p == group[0]:
                gather.finish()
        load_w(p).start()

    s = sequence_count
    entries = [(0, begin)]
    entries += [(which, functools.partial(norm_rows, which)) for which in range(1, s)]
    entries += [
        (1, gathers[2].after_levels),
        (2, gathers[2].after_columns),
    ]
    for i, gather in enumerate(gathers[3:]):
        need = groups[3 + i][0] * s - 1
        entries += [
            (need - 4, gather.after_levels),
            (need - 3, gather.after_columns),
            (need - 2, gather.after_twins),
        ]
    for p in range(1, pairs):
        entries.append((p * s - 1, functools.partial(ready, p)))
        entries.append((p * s, load_w(p).wait))
    for i, cut in enumerate(cuts):
        entries += [
            (FRONT_TABLE[0][i], cut.after_levels),
            (FRONT_TABLE[1][i], cut.after_columns),
            (FRONT_TABLE[2][i], cut.after_twins),
        ]
    at_steps(step, schedule(*entries))

    seq_rows = pl.ds(pl.multiple_of(seq * length, length), length)
    weight = w_ref[lax.rem(pair, 2)].reshape(width, 3 * PAIR)
    qkv_ref[...] = dot(n1_ref[seq_rows, :], weight).astype(BF16)

    @pl.when(pair == 0)
    def _():
        prefix_ref[...] = jnp.zeros_like(prefix_ref)
        row = lax.broadcasted_iota(jnp.int32, (ROWS, ROWS), 0)
        col = lax.broadcasted_iota(jnp.int32, (ROWS, ROWS), 1)
        triangle = (col < row).astype(BF16)
        for first_row in range(0, length, ROWS):
            keys = key_count(first_row, slot)
            at = pl.ds(first_row, ROWS)
            query = jnp.where(head_mask(0), qkv_ref[at, :PAIR], zero)
            scores = dot_nt(query, qkv_ref[:keys, PAIR : 2 * PAIR]) * SCALE
            allowed, chosen = block_masks(start_ref, length_ref, seq, pieces, first_row, keys)
            selected = jnp.where(chosen & (scores > 0), scores, 0.0)
            penalty = prefix_ref[:, :keys] + triangle_sum(triangle, selected)
            bias_ref[seq, at, :keys] = jnp.where(allowed, -penalty, MASKED_VALUE)
            prefix_ref[:, :keys] += column_sum(selected)

    def logits_of(first_row, half):
        keys = key_count(first_row, slot)
        at = pl.ds(first_row, ROWS)
        query = jnp.where(head_mask(half), qkv_ref[at, :PAIR], zero) * jnp.asarray(SCALE, BF16)
        return dot_nt(query, qkv_ref[:keys, PAIR : 2 * PAIR]) + bias_ref[seq, at, :keys]

    def raise_and_mix(first_row, half, logits):
        keys = key_count(first_row, slot)
        largest = jnp.max(logits, axis=-1, keepdims=True)
        raised = jnp.exp(logits - largest)
        inverse = 1.0 / jnp.sum(raised, axis=-1, keepdims=True)
        low = raised.astype(BF16)
        att_refs[first_row // slot][half, pl.ds(first_row % slot, ROWS), :] = low
        value = jnp.where(head_mask(half), qkv_ref[:keys, 2 * PAIR :], zero)
        return (dot(low, value), inverse)

    def finish_rows(first_row, halves):
        (mixed0, inverse0), (mixed1, inverse1) = halves
        at = pl.ds(first_row, ROWS)
        inverse = jnp.where(head_mask(0), inverse0, inverse1)
        inv_ref[at, :] = inverse
        o_ref[at, :] = ((mixed0 + mixed1) * inverse).astype(BF16)

    blocks = [(first_row, half) for first_row in range(0, length, ROWS) for half in range(2)]
    halves, ahead = ([], logits_of(*blocks[0]))
    for i, block in enumerate(blocks):
        logits = ahead
        if i + 1 < len(blocks):
            ahead = logits_of(*blocks[i + 1])
        halves.append(raise_and_mix(*block, logits))
        if len(halves) == 2:
            finish_rows(block[0], halves)
            halves = []

    @pl.when(step == pairs * sequence_count - 1)
    def _():
        for cut in cuts:
            cut.finish()
        for gather in [vec] + gathers + cuts:
            gather.drain()
        keep_n1().wait()


def front(tokens, starts, lengths, wqkv, vectors, wo, wu, wd, devices, copies):
    sequences, pieces = starts.shape
    count, width = tokens.shape
    length = count // sequences
    slot = length // pieces
    pairs = width // PAIR
    lines = vectors.shape[0]
    anywhere = pl.BlockSpec(memory_space=pl.ANY)

    def low(*shape):
        return jax.ShapeDtypeStruct(shape, BF16)

    att_shapes = [low(sequences, 2 * pairs, slot, (i + 1) * slot) for i in range(pieces)]
    att_specs = [
        pl.BlockSpec((None, 2, slot, (i + 1) * slot), lambda p, s, a, b: (s, p, 0, 0))
        for i in range(pieces)
    ]
    across = devices // (LEVELS * CORES)

    def spread(array):
        return (LEVELS, across, CORES * array.shape[0], array.shape[1])

    weights = [low(*spread(w)) for w in (wqkv, wo, wu, wd)]
    sems = gather_sems(devices)
    results = pl.pallas_call(
        functools.partial(front_kernel, slot, pieces, devices, copies, pairs),
        out_shape=[
            low(count, 3 * width),
            low(count, width),
            jax.ShapeDtypeStruct((count, width), F32),
        ]
        + att_shapes
        + [low(count, width), jax.ShapeDtypeStruct((lines, 1, width), F32)]
        + weights,
        grid_spec=pltpu.PrefetchScalarGridSpec(
            num_scalar_prefetch=2,
            grid=(pairs, sequences),
            in_specs=[anywhere] * 6,
            out_specs=[
                pl.BlockSpec((length, 3 * PAIR), lambda p, s, a, b: (s, p)),
                pl.BlockSpec((length, PAIR), lambda p, s, a, b: (s, p)),
                pl.BlockSpec((length, PAIR), lambda p, s, a, b: (s, p)),
            ]
            + att_specs
            + [anywhere, pl.BlockSpec((lines, 1, width), lambda *_: (0, 0, 0))]
            + [anywhere] * 4,
            scratch_shapes=[
                pltpu.VMEM((count, width), BF16),
                pltpu.VMEM((count, width), BF16),
                pltpu.VMEM(spread(vectors), BF16),
                pltpu.VMEM(wqkv.shape, BF16),
                pltpu.VMEM((2,) + spread(wqkv)[:3] + (3 * PAIR,), BF16),
                pltpu.VMEM((sequences, length, length), F32),
                pltpu.VMEM((1, length), F32),
                pltpu.SemaphoreType.DMA((3 * pairs,)),
                pltpu.SemaphoreType.DMA((4,)),
                pltpu.SemaphoreType.DMA((sems,)),
                pltpu.SemaphoreType.DMA((len(pair_groups(pairs)), sems)),
                pltpu.SemaphoreType.DMA((5, sems)),
            ],
        ),
        compiler_params=comm_params(1, "arbitrary", "arbitrary"),
        name="front",
    )(starts, lengths, tokens, wqkv, vectors, wo, wu, wd)
    n1, lines, *weights = results[3 + pieces :]
    weights = [w.reshape(-1, w.shape[-1]) for w in weights]
    return (results[:3], results[3 : 3 + pieces], [n1, lines] + weights)


TAIL = 2
TOGETHER = 2


def attend_back_kernel(
    slot,
    pieces,
    chunks,
    count,
    copies,
    pairs,
    start_ref,
    length_ref,
    qkv_ref,
    gm_ref,
    o_ref,
    inv_ref,
    *rest,
):
    att_hbms, rest = (rest[:pieces], rest[pieces:])
    n1_hbm, n2_hbm, gb_hbm, hid_hbm, cot_hbm, mixed_hbm, gproj_hbm, small_ref = rest[:8]
    g_ref, gqkv_ref, gwo_ref, gwu_ref, gwd_ref, gsmall_ref = rest[8:14]
    later_ref, dq_ref, dk_ref, dv_ref, left_ref, right_ref = rest[14:20]
    load_sem, att_sem = rest[20:22]
    rest = rest[22:]
    sum_refs, att_refs, ds_refs = (rest[i * pieces : (i + 1) * pieces] for i in range(3))
    rest = rest[3 * pieces :]
    step = pl.program_id(0)
    first_step = 2 * chunks + 1
    length = qkv_ref.shape[0]
    width = left_ref.shape[2]
    sequences = left_ref.shape[1] // length
    turns = pairs * sequences
    turn = jnp.maximum(step - first_step, 0)

    place = Place(count, copies)
    parts = []

    def add_part(write, by_level=False):
        at = 6 * len(parts)
        parts.append(Scatter(place, rest[at : at + 6], write, by_level))

    for c in range(chunks):

        def write_up(value, c=c):
            gwu_ref[:, c * width : (c + 1) * width] = value

        add_part(write_up)
    half_rows = gwd_ref.shape[0] // 2
    for h in range(2):

        def write_down(value, h=h):
            gwd_ref[h * half_rows : (h + 1) * half_rows, :] = value

        add_part(write_down, chunks == LEVELS)

    def write_out(value):
        gwo_ref[...] = value

    add_part(write_out)
    for pair in range(pairs - 1, TAIL - 1, -TOGETHER):

        def write_pair(value, pair=pair):
            for at in range(3 * TOGETHER):
                first = (at % 3) * width + (pair - at // 3) * PAIR
                gqkv_ref[:, first : first + PAIR] = value[:, at * PAIR : (at + 1) * PAIR]

        add_part(write_pair)
    small = Reduce(place, rest[6 * len(parts) : 6 * len(parts) + 4], gsmall_ref)
    up_parts, (down0, down1, out_part) = (parts[:chunks], parts[chunks : chunks + 3])
    pair_parts = parts[chunks + 3 :]

    left_slot = [0] * chunks + [(c + 1) % 2 for c in range(chunks)] + [(chunks + 1) % 2]
    right_slot = [c % 2 for c in range(chunks)] + [chunks % 2] * chunks + [(chunks + 1) % 2]

    def chunk_of(ref, c):
        return ref.at[:, pl.ds(c * width, width)]

    left_loads = {0: n2_hbm, 2 * chunks: mixed_hbm}
    right_loads = {chunks: cot_hbm, 2 * chunks: gproj_hbm}
    for c in range(chunks):
        left_loads[chunks + c] = chunk_of(hid_hbm, c)
        right_loads[c] = chunk_of(gb_hbm, c)

    def loads(when):
        found = []
        if when in left_loads:
            at = left_slot[when]
            found.append(
                pltpu.make_async_copy(left_loads[when], left_ref.at[at], load_sem.at[at])
            )
        if when in right_loads:
            at = right_slot[when]
            found.append(
                pltpu.make_async_copy(right_loads[when], right_ref.at[at], load_sem.at[2 + at])
            )
        return found

    n1_slot = chunks % 2

    def load_n1():
        return pltpu.make_async_copy(n1_hbm, left_ref.at[n1_slot], load_sem.at[4])

    def load_att(at, half):
        seq = lax.rem(at, sequences)
        head = 2 * (pairs - 1 - lax.div(at, sequences)) + half
        return [
            pltpu.make_async_copy(
                att_hbms[i].at[seq, head], att_refs[i].at[half], att_sem.at[half * pieces + i]
            )
            for i in range(pieces)
        ]

    def begin():
        for copy in loads(0):
            copy.start()
        place.meet(copies=True)
        small.start(small_ref[...])

    def before_attention():
        load_n1().start()
        for half in range(2):
            for copy in load_att(0, half):
                copy.start()

    entries = [(0, begin), (first_step - 1, before_attention)]
    for c, part in enumerate(up_parts):
        entries += [
            (c + 2, part.after_cores),
            (2 * c + 5, part.after_columns),
            (2 * c + 8, part.after_levels),
            (2 * c + 10, part.after_copies),
        ]
    f = first_step
    late = BACK_TABLE
    names = (down0, down1, out_part) + tuple(pair_parts)
    entries += [
        (3, small.after_cores),
        (6, small.after_columns),
        (10, small.after_levels),
        (13, small.after_copies),
        (f + sequences - 1, load_n1().wait),
    ]
    left_over = []
    for part, whens in zip(names, late):
        actions = (part.after_cores, part.after_columns, part.after_levels, part.after_copies)
        for phase, (when, action) in enumerate(zip(whens, actions)):
            if when < sequences * pairs:
                entries.append((f + when, action))
            else:
                left_over.append((when, phase, action))
    at_steps(step, schedule(*entries))

    @pl.when(step < first_step)
    def _():
        left_at = jnp.zeros((), jnp.int32)
        right_at = jnp.zeros((), jnp.int32)
        for when in range(first_step):

            @pl.when(step == when)
            def _(when=when):
                if when + 1 < first_step:
                    for copy in loads(when + 1):
                        copy.start()
                for copy in loads(when):
                    copy.wait()

            left_at = jnp.where(step == when, left_slot[when], left_at)
            right_at = jnp.where(step == when, right_slot[when], right_at)
        grad = dot_tn(left_ref[left_at], right_ref[right_at]).astype(BF16)
        for when in range(first_step):

            @pl.when(step == when)
            def _(when=when):
                if when < chunks or when == 2 * chunks:
                    part = out_part if when == 2 * chunks else up_parts[when]
                    rows = width // count
                    for block in range(count):
                        part.put(block, grad[block * rows : (block + 1) * rows, :])
                    part.start()
                else:
                    blocks = count // chunks
                    for i in range(blocks):
                        block = (when - chunks) * blocks + i
                        for h, part in enumerate((down0, down1)):
                            at = (2 * i + h) * half_rows
                            part.put(block, grad[at : at + half_rows, :])
                    for part in (down0, down1):
                        if part.by_level:
                            part.core_copies()[when - chunks].start()
                        elif when == 2 * chunks - 1:
                            part.start()

    @pl.when(step >= first_step)
    def _():
        seq = lax.rem(turn, sequences)
        inputs = (qkv_ref, gm_ref, o_ref, inv_ref)
        masks = (slot, pieces, start_ref, length_ref)
        scratch = (sum_refs, att_refs, ds_refs, later_ref, dq_ref, dk_ref, dv_ref)

        @pl.when(turn < sequences)
        def _():
            for ref in sum_refs:
                ref[seq] = jnp.zeros(ref.shape[1:], F32)

        def wait_att(half):
            for copy in load_att(turn, half):
                copy.wait()

        def next_att(half):
            @pl.when(turn < turns - 1)
            def _():
                for copy in load_att(turn + 1, half):
                    copy.start()

        for ref in (dq_ref, dk_ref, dv_ref):
            ref[...] = jnp.zeros_like(ref)
        special = turn >= turns - sequences

        def plain(i, carry):
            half = 1 - i
            wait_att(half)
            head_back(half, False, seq, masks, inputs, scratch)
            next_att(half)
            return carry

        lax.fori_loop(0, jnp.where(special, 1, 2), plain, 0)

        @pl.when(special)
        def _():
            wait_att(0)
            head_back(0, True, seq, masks, inputs, scratch)
            next_att(0)

        grads = (dq_ref[...], jnp.transpose(dk_ref[...]), jnp.transpose(dv_ref[...]))
        keep = pl.ds(pl.multiple_of(seq * length, length), length)
        base = lax.rem(lax.div(turn, sequences), TOGETHER) * (3 * PAIR)
        for which, grad in enumerate(grads):
            low = grad.astype(BF16)
            g_ref[:, which * PAIR : (which + 1) * PAIR] = low
            columns = pl.ds(pl.multiple_of(base + which * PAIR, PAIR), PAIR)
            right_ref[0, keep, columns] = low

    span = TOGETHER * sequences

    @pl.when((step >= first_step) & (lax.rem(turn, span) == span - 1))
    def _():
        @pl.when(turn < (pairs - TAIL) * sequences)
        def _():
            columns = pl.ds(0, TOGETHER * 3 * PAIR)
            grad = dot_tn(left_ref[n1_slot], right_ref[0, :, columns]).astype(BF16)
            rows = width // count
            for i, part in enumerate(pair_parts):

                @pl.when(turn == (i + 1) * span - 1)
                def _(part=part):
                    for block in range(count):
                        part.put(block, grad[block * rows : (block + 1) * rows, :])
                    part.start()

    @pl.when(step == pl.num_programs(0) - 1)
    def _():
        for _, _, action in sorted(left_over, key=lambda item: item[:2]):
            action()
        for part in parts + [small]:
            part.drain()


def head_back(half, first_head, seq, masks, inputs, scratch):
    slot, pieces, start_ref, length_ref = masks
    qkv_ref, gm_ref, o_ref, inv_ref = inputs
    sum_refs, att_refs, ds_refs, later_ref, dq_ref, dk_ref, dv_ref = scratch
    zero = jnp.zeros((), BF16)
    scale = jnp.asarray(SCALE, BF16)
    mask = head_mask(half)

    def scaled_grad(rows):
        return jnp.where(mask, gm_ref[rows, :].astype(F32) * inv_ref[rows, :], 0.0)

    def query_of(rows):
        return jnp.where(mask, qkv_ref[rows, :PAIR], zero) * scale

    if first_head:
        later_ref[...] = jnp.zeros_like(later_ref)
        row = lax.broadcasted_iota(jnp.int32, (ROWS, ROWS), 0)
        col = lax.broadcasted_iota(jnp.int32, (ROWS, ROWS), 1)
        triangle = (col > row).astype(BF16)
    for i in reversed(range(pieces)):
        keys = (i + 1) * slot
        for first in reversed(range(0, slot, ROWS)):
            rows = pl.ds(i * slot + first, ROWS)
            at = pl.ds(first, ROWS)
            scaled = scaled_grad(rows)
            delta = jnp.sum(scaled * o_ref[rows, :].astype(F32), axis=-1, keepdims=True)
            grad_attention = dot_nt(scaled.astype(BF16), qkv_ref[:keys, 2 * PAIR :])
            grad_logits = att_refs[i][half, at, :].astype(F32) * (grad_attention - delta)
            if first_head:
                total = sum_refs[i][seq, at, :] + grad_logits
                grad_selected = -(later_ref[:, :keys] + triangle_sum(triangle, total))
                later_ref[:, :keys] += column_sum(total)
                _, chosen = block_masks(
                    start_ref, length_ref, seq, pieces, i * slot + first, keys
                )
                positive = dot_nt(query_of(rows), qkv_ref[:keys, PAIR : 2 * PAIR]) > 0
                grad_logits = grad_logits + jnp.where(chosen & positive, grad_selected, 0.0)
            else:
                sum_refs[i][seq, at, :] += grad_logits
            ds_refs[i][at, :] = grad_logits.astype(BF16)
        rows = pl.ds(i * slot, slot)
        key = jnp.where(mask, qkv_ref[:keys, PAIR : 2 * PAIR], zero) * scale
        query_part = dot(ds_refs[i][...], key)
        key_part = dot_tn(query_of(rows), ds_refs[i][...])
        value_part = dot_tn(scaled_grad(rows).astype(BF16), att_refs[i][half])
        dq_ref[rows, :] += query_part
        dk_ref[:, :keys] += key_part
        dv_ref[:, :keys] += value_part


def attend_back(
    projected, starts, lengths, grad_mixed, mixed, inverse, attention, kept, small, devices, copies
):
    n1, n2, grad_before, hidden, cotangent, grad_proj = kept
    sequences, pieces = starts.shape
    count, columns = projected.shape
    length = count // sequences
    slot = length // pieces
    width = columns // 3
    pairs = width // PAIR
    chunks = hidden.shape[1] // width
    first_step = 2 * chunks + 1
    rows = width // devices
    down_rows = hidden.shape[1] // devices
    lines = small.shape[0]

    def part(size):
        def index(step, a, b):
            at = jnp.maximum(step - first_step, 0)
            return (lax.rem(at, sequences), pairs - 1 - lax.div(at, sequences))

        return pl.BlockSpec((length, size * PAIR), index)

    anywhere = pl.BlockSpec(memory_space=pl.ANY)

    def fixed(shape):
        return pl.BlockSpec(shape, lambda *_: (0,) * len(shape))

    results = [
        (rows, columns),
        (rows, width),
        (rows, chunks * width),
        (down_rows, width),
        (lines, 1, width),
    ]
    slots = [(slot, (i + 1) * slot) for i in range(pieces)]
    scratch = [
        pltpu.VMEM((1, length), F32),
        pltpu.VMEM((length, PAIR), F32),
        pltpu.VMEM((PAIR, length), F32),
        pltpu.VMEM((PAIR, length), F32),
        pltpu.VMEM((2, count, width), BF16),
        pltpu.VMEM((2, count, width), BF16),
        pltpu.SemaphoreType.DMA((5,)),
        pltpu.SemaphoreType.DMA((2 * pieces,)),
    ]
    scratch += [pltpu.VMEM((sequences,) + shape, F32) for shape in slots]
    scratch += [pltpu.VMEM((2,) + shape, BF16) for shape in slots]
    scratch += [pltpu.VMEM(shape, BF16) for shape in slots]
    for piece_rows in [rows] * chunks + [down_rows // 2] * 2 + [rows]:
        scratch += scatter_scratch(devices, copies, piece_rows, width)
    for _ in range((pairs - TAIL) // TOGETHER):
        scratch += scatter_scratch(devices, copies, rows, TOGETHER * 3 * PAIR)
    scratch += reduce_scratch(devices, copies, lines, width)
    return pl.pallas_call(
        functools.partial(
            attend_back_kernel, slot, pieces, chunks, devices, copies, pairs
        ),
        out_shape=[jax.ShapeDtypeStruct((count, columns), BF16)]
        + [jax.ShapeDtypeStruct(shape, F32) for shape in results],
        grid_spec=pltpu.PrefetchScalarGridSpec(
            num_scalar_prefetch=2,
            grid=(first_step + sequences * pairs,),
            in_specs=[part(3)]
            + [part(1)] * 3
            + [anywhere] * (pieces + 7)
            + [fixed((lines, 1, width))],
            out_specs=[part(3)] + [fixed(shape) for shape in results],
            scratch_shapes=scratch,
        ),
        compiler_params=comm_params(2, "arbitrary"),
        name="attend_back",
    )(
        starts,
        lengths,
        projected,
        grad_mixed,
        mixed,
        inverse,
        *attention,
        n1,
        n2,
        grad_before,
        hidden,
        cotangent,
        mixed,
        grad_proj,
        small,
    )


def gelu_and_slope(values):
    square = values * values
    inner = GELU_IN * values * (1.0 + GELU_CUBE * square)
    bent = jnp.tanh(inner)
    half = 0.5 * (1.0 + bent)
    slope = half + 0.5 * values * (1.0 - bent * bent) * (
        GELU_IN * (1.0 + 3.0 * GELU_CUBE * square)
    )
    return (values * half, slope)


def feed_kernel(
    chunk,
    x_ref,
    mixed_ref,
    cot_ref,
    gain_ref,
    shift_ref,
    up_bias_ref,
    down_bias_ref,
    wo_hbm,
    wu_hbm,
    wd_hbm,
    out_ref,
    gmid_ref,
    gmix_ref,
    small_ref,
    n2_ref,
    hid_ref,
    gb_ref,
    gproj_ref,
    wo_ref,
    wu_ref,
    wd_ref,
    acc_ref,
    gnorm_ref,
    mid_ref,
    load_sem,
):
    step = pl.program_id(0)
    chunks = wu_ref.shape[0]

    def load_out():
        return pltpu.make_async_copy(wo_hbm, wo_ref, load_sem.at[0])

    def load_up(c):
        return pltpu.make_async_copy(
            wu_hbm.at[:, pl.ds(c * chunk, chunk)], wu_ref.at[c], load_sem.at[1 + 2 * c]
        )

    def load_down(c):
        return pltpu.make_async_copy(
            wd_hbm.at[pl.ds(c * chunk, chunk), :], wd_ref.at[c], load_sem.at[2 + 2 * c]
        )

    @pl.when(step == 0)
    def _():
        load_out().start()
        for c in range(chunks):
            load_up(c).start()
            load_down(c).start()
        small_ref[...] = jnp.zeros_like(small_ref)
        load_out().wait()

    mid_ref[...] = x_ref[...].astype(F32) + dot(mixed_ref[...], wo_ref[...])

    @pl.when(step == 0)
    def _():
        for c in range(chunks):
            load_up(c).wait()
            load_down(c).wait()

    normed, _ = normalize(mid_ref[...])
    n2_ref[...] = (normed * gain_ref[...] + shift_ref[...]).astype(BF16)
    def open_chunk(c):
        before = dot(n2_ref[...], wu_ref[c]) + up_bias_ref[c]
        grad_hidden = dot_nt(cot_ref[...], wd_ref[c]).astype(BF16)
        return (before, grad_hidden)

    ahead = open_chunk(0)
    for c in range(chunks):
        before, grad_hidden = ahead
        if c + 1 < chunks:
            ahead = open_chunk(c + 1)
        columns = slice(c * chunk, (c + 1) * chunk)
        hidden, slope = gelu_and_slope(before)
        hidden = hidden.astype(BF16)
        hid_ref[:, columns] = hidden
        grad_before = (grad_hidden.astype(F32) * slope).astype(BF16)
        gb_ref[:, columns] = grad_before
        small_ref[3 + c] += column_sum(grad_before.astype(F32))
        down = dot(hidden, wd_ref[c])
        back = dot_nt(grad_before, wu_ref[c])
        if c == 0:
            acc_ref[...] = down
            gnorm_ref[...] = back
        else:
            acc_ref[...] += down
            gnorm_ref[...] += back

    out_ref[...] = (mid_ref[...] + (acc_ref[...] + down_bias_ref[...])).astype(BF16)
    grad_normed = gnorm_ref[...]
    normed, inverse = normalize(mid_ref[...])
    cot = cot_ref[...].astype(F32)
    small_ref[0] += column_sum(grad_normed * normed)
    small_ref[1] += column_sum(grad_normed)
    small_ref[2] += column_sum(cot)
    grad_middle = cot + norm_back(grad_normed * gain_ref[...], normed, inverse)
    gmid_ref[...] = grad_middle
    grad_proj = grad_middle.astype(BF16)
    gproj_ref[...] = grad_proj
    gmix_ref[...] = dot_nt(grad_proj, wo_ref[...]).astype(BF16)


def vector_line(row):
    return lambda width: pl.BlockSpec((None, 1, width), lambda *_: (row, 0, 0))


def feed(tokens, mixed, cotangent, vectors, wo, wu, wd):
    count, width = tokens.shape
    hidden = wu.shape[1]
    block = 512
    chunk = width
    chunks = hidden // chunk
    rows = pl.BlockSpec((block, width), lambda i: (i, 0))
    anywhere = pl.BlockSpec(memory_space=pl.ANY)
    wide = pl.BlockSpec((block, hidden), lambda i: (i, 0))

    def low(columns):
        return jax.ShapeDtypeStruct((count, columns), BF16)

    return pl.pallas_call(
        functools.partial(feed_kernel, chunk),
        out_shape=[
            low(width),
            jax.ShapeDtypeStruct((count, width), F32),
            low(width),
            jax.ShapeDtypeStruct((3 + chunks, 1, width), F32),
            low(width),
            low(hidden),
            low(hidden),
            low(width),
        ],
        grid=(count // block,),
        in_specs=[
            rows,
            rows,
            rows,
            vector_line(GAIN2)(width),
            vector_line(SHIFT2)(width),
            pl.BlockSpec((chunks, 1, chunk), lambda i: (0, 0, 0)),
            vector_line(DOWN_BIAS)(width),
            anywhere,
            anywhere,
            anywhere,
        ],
        out_specs=[
            rows,
            rows,
            rows,
            pl.BlockSpec((3 + chunks, 1, width), lambda i: (0, 0, 0)),
            rows,
            wide,
            wide,
            rows,
        ],
        scratch_shapes=[
            pltpu.VMEM(wo.shape, BF16),
            pltpu.VMEM((chunks, width, chunk), BF16),
            pltpu.VMEM((chunks, chunk, width), BF16),
            pltpu.VMEM((block, width), F32),
            pltpu.VMEM((block, width), F32),
            pltpu.VMEM((block, width), F32),
            pltpu.SemaphoreType.DMA((1 + 2 * chunks,)),
        ],
        compiler_params=params("arbitrary"),
        name="feed",
    )(
        tokens,
        mixed,
        cotangent,
        vectors,
        vectors,
        vectors,
        vectors,
        wo,
        wu,
        wd,
    )


def input_kernel(
    count,
    copies,
    gmid_ref,
    gain_ref,
    shift_ref,
    rest_ref,
    x_hbm,
    n1_hbm,
    g_hbm,
    w_hbm,
    gx_ref,
    gw_ref,
    gsmall_ref,
    x_ref,
    n1_ref,
    g_ref,
    w_ref,
    small_ref,
    load_sem,
    *rest,
):
    step = pl.program_id(0)
    total, width = x_ref.shape
    columns = w_ref.shape[1]
    block = gx_ref.shape[0]
    first = TAIL * 3 * PAIR
    place = Place(count, copies)

    def write(value):
        gw_ref[...] = rest_ref[...]
        for at in range(3 * TAIL):
            to = (at % 3) * width + (at // 3) * PAIR
            gw_ref[:, to : to + PAIR] = value[:, at * PAIR : (at + 1) * PAIR]

    part = Scatter(place, rest[:6], write)
    small = Reduce(place, rest[6:10], gsmall_ref)

    def loads():
        near, far = (pl.ds(0, first), pl.ds(first, columns - first))
        pairs = [
            (n1_hbm, n1_ref),
            (g_hbm.at[:, near], g_ref.at[:, near]),
            (x_hbm, x_ref),
            (g_hbm.at[:, far], g_ref.at[:, far]),
            (w_hbm, w_ref),
        ]
        return [
            pltpu.make_async_copy(source, target, load_sem.at[i])
            for i, (source, target) in enumerate(pairs)
        ]

    def begin():
        for copy in loads():
            copy.start()
        place.meet(copies=True)
        small_ref[...] = jnp.zeros_like(small_ref)
        for copy in loads()[:2]:
            copy.wait()
        grad = dot_tn(n1_ref[...], g_ref[:, :first]).astype(BF16)
        rows = width // count
        for i in range(count):
            part.put(i, grad[i * rows : (i + 1) * rows, :])
        part.start()
        for copy in loads()[2:]:
            copy.wait()

    steps = total // block
    table = schedule(
        (0, begin),
        (1, part.after_cores),
        (min(3, steps - 1), part.after_columns),
    )
    at_steps(step, table)

    normed, inverse = normalize(
        x_ref[pl.ds(pl.multiple_of(step * block, block), block), :].astype(F32)
    )
    grads = g_ref[pl.ds(pl.multiple_of(step * block, block), block), :]
    grad_normed = dot_nt(grads, w_ref[...])
    small_ref[0] += column_sum(grad_normed * normed)
    small_ref[1] += column_sum(grad_normed)

    @pl.when(step == steps - 1)
    def _():
        small.start(small_ref[...])

    gx_ref[...] = gmid_ref[...] + norm_back(grad_normed * gain_ref[...], normed, inverse)

    @pl.when(step == steps - 1)
    def _():
        small.after_cores()
        part.after_levels()
        small.after_columns()
        part.after_copies()
        small.after_levels()
        small.after_copies()
        part.drain()
        small.drain()


def input_back(tokens, n1, grad_middle, grads, grad_rest, vectors, weight, devices, copies):
    count, width = tokens.shape
    block = 512
    shard = width // devices
    rows = pl.BlockSpec((block, width), lambda i: (i, 0))
    own = pl.BlockSpec((shard, 3 * width), lambda i: (0, 0))
    anywhere = pl.BlockSpec(memory_space=pl.ANY)
    scratch = [
        pltpu.VMEM((count, width), BF16),
        pltpu.VMEM((count, width), BF16),
        pltpu.VMEM((count, 3 * width), BF16),
        pltpu.VMEM(weight.shape, BF16),
        pltpu.VMEM((2, 1, width), F32),
        pltpu.SemaphoreType.DMA((5,)),
    ]
    scratch += scatter_scratch(devices, copies, shard, TAIL * 3 * PAIR)
    scratch += reduce_scratch(devices, copies, 2, width)
    return pl.pallas_call(
        functools.partial(input_kernel, devices, copies),
        out_shape=[
            jax.ShapeDtypeStruct((count, width), F32),
            jax.ShapeDtypeStruct((shard, 3 * width), F32),
            jax.ShapeDtypeStruct((2, 1, width), F32),
        ],
        grid=(count // block,),
        in_specs=[rows, vector_line(GAIN1)(width), vector_line(SHIFT1)(width), own]
        + [anywhere] * 4,
        out_specs=[
            rows,
            own,
            pl.BlockSpec((2, 1, width), lambda i: (0, 0, 0)),
        ],
        scratch_shapes=scratch,
        compiler_params=comm_params(3, "arbitrary"),
        name="input_back",
    )(grad_middle, vectors, vectors, grad_rest, tokens, n1, grads, weight)


def local(
    tokens,
    piece_start,
    piece_length,
    query_key_value,
    output_weight,
    up_weight,
    down_weight,
    first_gain,
    first_shift,
    second_gain,
    second_shift,
    up_bias,
    down_bias,
    cotangent,
):
    width = tokens.shape[1]
    devices, copies = (lax.axis_size("fsdp"), lax.axis_size("rep"))
    index = lax.axis_index("fsdp")

    lines = jnp.stack([first_gain, first_shift, second_gain, second_shift, down_bias])
    own = lax.dynamic_update_slice(
        jnp.zeros((LINES - up_bias.shape[0] * devices // width, width), BF16),
        lines,
        (0, index * lines.shape[1]),
    )
    wide = lax.dynamic_update_slice(
        jnp.zeros((devices * up_bias.shape[0],), BF16), up_bias, (index * up_bias.shape[0],)
    )
    own = jnp.concatenate([wide.reshape(-1, width), own], axis=0)

    (projected, mixed, inverse), attention, (n1, vectors, wqkv, wo, wu, wd) = front(
        tokens,
        piece_start,
        piece_length,
        query_key_value,
        own,
        output_weight,
        up_weight,
        down_weight,
        devices,
        copies,
    )
    block_output, grad_middle, grad_mixed, small2, n2, hidden, grad_before, grad_proj = feed(
        tokens, mixed, cotangent, vectors, wo, wu, wd
    )
    grads, grad_rest, gwo, gwu, gwd, small2 = attend_back(
        projected,
        piece_start,
        piece_length,
        grad_mixed,
        mixed,
        inverse,
        attention,
        (n1, n2, grad_before, hidden, cotangent, grad_proj),
        small2,
        devices,
        copies,
    )
    grad_tokens, gwqkv, small1 = input_back(
        tokens, n1, grad_middle, grads, grad_rest, vectors, wqkv, devices, copies
    )

    def mine(values):
        values = values.reshape(-1)
        size = values.shape[0] // devices
        return lax.dynamic_slice(values, (index * size,), (size,))

    return (
        block_output,
        grad_tokens,
        gwqkv,
        gwo,
        gwu,
        gwd,
        mine(small1[0]),
        mine(small1[1]),
        mine(small2[0]),
        mine(small2[1]),
        mine(small2[3:]),
        mine(small2[2]),
    )


def solution(mesh):
    rows = P(("fsdp", "rep"), None)
    matrix = P("fsdp", None)
    vector = P("fsdp")
    return jax.shard_map(
        local,
        mesh=mesh,
        in_specs=(rows,) * 3 + (matrix,) * 4 + (vector,) * 6 + (rows,),
        out_specs=(rows,) * 2 + (matrix,) * 4 + (vector,) * 6,
        check_vma=False,
    )
```

```python
import functools

import jax
import jax.numpy as jnp
from jax import lax
from jax.experimental import pallas as pl
from jax.experimental.pallas import tpu as pltpu
from jax.sharding import PartitionSpec as P

HEAD_DIM = 64
PAIR = 2 * HEAD_DIM
ROWS = 256
MASKED_VALUE = -1e30
EPSILON = 1e-05
SCALE = HEAD_DIM**-0.5
GAIN1, SHIFT1, GAIN2, SHIFT2, DOWN_BIAS = (4, 5, 6, 7, 8)
LINES = 16
FRONT_TABLE = ((2, 4, 5, 7, 8), (4, 6, 7, 9, 10), (6, 8, 9, 11, 11))
BACK_TABLE = ((0, 3, 7, 9), (0, 5, 9, 11), (1, 6, 10, 11), (5, 9, 11, 12), (10, 11, 12, 13))
GELU_IN = 0.7978845608028654
GELU_CUBE = 0.044715
VMEM_LIMIT = 67043328

F32 = jnp.float32
BF16 = jnp.bfloat16


def dot(left, right):
    return lax.dot_general(left, right, (((1,), (0,)), ((), ())), preferred_element_type=F32)


def dot_nt(left, right):
    return lax.dot_general(left, right, (((1,), (1,)), ((), ())), preferred_element_type=F32)


def dot_tn(left, right):
    return lax.dot_general(left, right, (((0,), (0,)), ((), ())), preferred_element_type=F32)


def row_mean(values):
    return jnp.mean(values, axis=-1, keepdims=True)


def normalize(values):
    center = values - row_mean(values)
    inverse = lax.rsqrt(row_mean(center * center) + EPSILON)
    return (center * inverse, inverse)


def norm_back(grad, normed, inverse):
    return (grad - row_mean(grad) - normed * row_mean(grad * normed)) * inverse


def column_sum(values):
    return jnp.sum(values, axis=0, keepdims=True)


def params(*semantics):
    return pltpu.CompilerParams(dimension_semantics=semantics, vmem_limit_bytes=VMEM_LIMIT)


def comm_params(number, *semantics):
    return pltpu.CompilerParams(
        dimension_semantics=semantics,
        vmem_limit_bytes=VMEM_LIMIT,
        collective_id=number,
        has_side_effects=True,
    )


MESH = pl.DeviceIdType.MESH
LEVELS = 4
CORES = 2


class Place:
    def __init__(self, count, copies):
        self.count, self.copies = (count, copies)
        self.columns = count // (LEVELS * CORES)
        self.index = lax.axis_index("fsdp")
        self.rep = lax.axis_index("rep")
        self.core = lax.rem(self.index, CORES)
        chip = lax.div(self.index, CORES)
        self.column = lax.rem(chip, self.columns)
        self.level = lax.div(chip, self.columns)
        self.half = lax.rem(self.rep, 2)

    def block(self, up=0, across=0, other=0):
        level = lax.rem(self.level + (up + LEVELS), LEVELS)
        column = lax.rem(self.column + (across + self.columns), self.columns)
        core = lax.rem(self.core + other, CORES)
        return (level * self.columns + column) * CORES + core

    def device(self, up=0, across=0, other=0, copy=0):
        return (self.block(up, across, other), lax.rem(self.rep + copy, self.copies))

    def twin(self):
        return (self.index, self.rep + 1 - 2 * self.half)

    def meet(self, twin=False, copies=False):
        others = [self.device(up=up) for up in range(1, LEVELS)]
        others += [self.device(across=across) for across in range(1, self.columns)]
        others += [self.device(other=1)]
        if twin:
            others += [self.twin()]
        if copies:
            others += [self.device(copy=copy) for copy in range(1, self.copies)]
        barrier = pltpu.get_barrier_semaphore()
        for other in others:
            pl.semaphore_signal(barrier, inc=1, device_id=other, device_id_type=MESH)
        pl.semaphore_wait(barrier, len(others))


def send(source, target, sems, slot, device):
    return pltpu.make_async_remote_copy(
        src_ref=source,
        dst_ref=target,
        send_sem=sems.at[2 * slot],
        recv_sem=sems.at[2 * slot + 1],
        device_id=device,
        device_id_type=MESH,
    )


def gather_sems(count):
    across = count // (LEVELS * CORES) - 1
    return 2 * (2 * (LEVELS - 1) + 2 * across + 1) + 1


class Gather:
    def __init__(self, place, source, target, first, columns, shared, sems):
        self.place, self.source, self.target = (place, source, target)
        self.sems, self.shared, self.across = (sems, shared, columns)
        rows = source.shape[0]
        base = place.core * (target.shape[2] // CORES) + first
        third = rows // 3
        half = place.half
        self.whole = pl.ds(pl.multiple_of(base, rows), rows)
        if shared:
            self.near = pl.ds(pl.multiple_of(half * third, third), 2 * third)
            self.part = pl.ds(pl.multiple_of(base + half * third, third), 2 * third)
            self.give = pl.ds(pl.multiple_of(base + half * (2 * third), third), third)
        else:
            self.near, self.part = (pl.ds(0, rows), self.whole)

    def held(self, level, column, rows):
        return self.target.at[level, column, rows, self.across]

    def send(self, ref, slot, device):
        return send(ref, ref, self.sems, slot, device)

    def level_copies(self):
        place = self.place
        return [
            send(
                self.source.at[self.near, :],
                self.held(place.level, place.column, self.part),
                self.sems,
                up - 1,
                place.device(up=up),
            )
            for up in range(1, LEVELS)
        ]

    def column_copies(self):
        place = self.place
        ref = self.held(slice(None), place.column, self.part)
        return [
            self.send(ref, LEVELS - 2 + across, place.device(across=across))
            for across in range(1, place.columns)
        ]

    def twin_copies(self, near):
        if not self.shared:
            return []
        place = self.place
        base = LEVELS - 1 + place.columns - 1
        if near:
            return [
                self.send(
                    self.held(
                        lax.rem(place.level + (LEVELS - up), LEVELS), place.column, self.give
                    ),
                    base + up - 1,
                    place.twin(),
                )
                for up in range(1, LEVELS)
            ]
        return [
            self.send(
                self.held(
                    slice(None),
                    lax.rem(place.column + (place.columns - across), place.columns),
                    self.give,
                ),
                base + LEVELS - 2 + across,
                place.twin(),
            )
            for across in range(1, place.columns)
        ]

    def core_copy(self):
        slot = 2 * (LEVELS - 1) + 2 * (self.place.columns - 1)
        ref = self.held(slice(None), slice(None), self.whole)
        return self.send(ref, slot, self.place.device(other=1))

    def own(self):
        place = self.place
        last = gather_sems(place.count) - 1
        return pltpu.make_async_copy(
            self.source, self.held(place.level, place.column, self.whole), self.sems.at[last]
        )

    def start(self):
        for copy in self.level_copies():
            copy.start()
        self.own().start()

    def after_levels(self):
        self.own().wait()
        for copy in self.level_copies():
            copy.wait_recv()
        for copy in self.column_copies() + self.twin_copies(True):
            copy.start()

    def after_columns(self):
        for copy in self.column_copies():
            copy.wait_recv()
        for copy in self.twin_copies(False):
            copy.start()
        if not self.shared:
            self.core_copy().start()

    def after_twins(self):
        if self.shared:
            for copy in self.twin_copies(True) + self.twin_copies(False):
                copy.wait_recv()
            self.core_copy().start()

    def finish(self):
        self.core_copy().wait_recv()

    def drain(self):
        copies = self.level_copies() + self.column_copies()
        for copy in copies + self.twin_copies(True) + self.twin_copies(False):
            copy.wait_send()
        self.core_copy().wait_send()


def scatter_slots(count, copies):
    across = count // (CORES * LEVELS) - 1
    return LEVELS + across + (LEVELS - 1) + (copies - 1)


def scatter_scratch(count, copies, rows, columns):
    across = count // (CORES * LEVELS)
    return [
        pltpu.VMEM((LEVELS, across, CORES, rows, columns), BF16),
        pltpu.VMEM((LEVELS, across, rows, columns), BF16),
        pltpu.VMEM((max(across - 1, 1), LEVELS, rows, columns), BF16),
        pltpu.VMEM((LEVELS - 1, rows, columns), BF16),
        pltpu.VMEM((copies, rows, columns), BF16),
        pltpu.SemaphoreType.DMA((2 * scatter_slots(count, copies),)),
    ]


def add_low(left, right):
    return (left.astype(F32) + right.astype(F32)).astype(BF16)


class Scatter:
    def __init__(self, place, refs, write, by_level=False):
        self.place, self.write, self.by_level = (place, write, by_level)
        self.held, self.from_core, self.from_column, self.from_level, self.parts, self.sems = refs

    def put(self, block, value):
        chip = block // CORES
        self.held[chip // self.place.columns, chip % self.place.columns, block % CORES] = value

    def core_copies(self):
        place = self.place
        other = 1 - place.core
        if not self.by_level:
            source = self.held.at[:, :, other]
            return [send(source, self.from_core, self.sems, 0, place.device(other=1))]
        return [
            send(
                self.held.at[level, :, other],
                self.from_core.at[level],
                self.sems,
                level,
                place.device(other=1),
            )
            for level in range(LEVELS)
        ]

    def column_copies(self):
        place = self.place
        return [
            send(
                self.held.at[:, lax.rem(place.column + across, place.columns), place.core],
                self.from_column.at[across - 1],
                self.sems,
                LEVELS + across - 1,
                place.device(across=across),
            )
            for across in range(1, place.columns)
        ]

    def level_copies(self):
        place = self.place
        base = LEVELS + place.columns - 1
        return [
            send(
                self.held.at[lax.rem(place.level + up, LEVELS), place.column, place.core],
                self.from_level.at[up - 1],
                self.sems,
                base + up - 1,
                place.device(up=up),
            )
            for up in range(1, LEVELS)
        ]

    def rep_copies(self):
        place = self.place
        base = 2 * LEVELS + place.columns - 2
        mine = self.parts.at[place.rep]
        return [
            send(mine, mine, self.sems, base + copy - 1, place.device(copy=copy))
            for copy in range(1, place.copies)
        ]

    def start(self):
        for copy in self.core_copies():
            copy.start()

    def after_cores(self):
        place = self.place
        for copy in self.core_copies():
            copy.wait_recv()

        def add(i, carry):
            level, column = (lax.div(i, place.columns), lax.rem(i, place.columns))
            self.held[level, column, place.core] = add_low(
                self.held[level, column, place.core], self.from_core[level, column]
            )
            return carry

        lax.fori_loop(0, LEVELS * place.columns, add, 0)
        for copy in self.column_copies():
            copy.start()

    def after_columns(self):
        place = self.place
        for copy in self.column_copies():
            copy.wait_recv()

        def add(level, carry):
            total = self.held[level, place.column, place.core].astype(F32)
            for across in range(place.columns - 1):
                total = total + self.from_column[across, level].astype(F32)
            self.held[level, place.column, place.core] = total.astype(BF16)
            return carry

        lax.fori_loop(0, LEVELS, add, 0)
        for copy in self.level_copies():
            copy.start()

    def after_levels(self):
        place = self.place
        for copy in self.level_copies():
            copy.wait_recv()
        total = self.held[place.level, place.column, place.core].astype(F32)
        for level in range(LEVELS - 1):
            total = total + self.from_level[level].astype(F32)
        self.parts[place.rep] = total.astype(BF16)
        for copy in self.rep_copies():
            copy.start()

    def after_copies(self):
        for copy in self.rep_copies():
            copy.wait_recv()
        total = self.parts[0].astype(F32)
        for rep in range(1, self.place.copies):
            total = total + self.parts[rep].astype(F32)
        self.write(total)

    def drain(self):
        copies = self.core_copies() + self.column_copies() + self.level_copies()
        for copy in copies + self.rep_copies():
            copy.wait_send()


def reduce_scratch(count, copies, lines, width):
    across = count // (CORES * LEVELS)
    slots = 1 + (across - 1) + (LEVELS - 1) + (copies - 1)
    return [
        pltpu.VMEM((3, lines, 1, width), F32),
        pltpu.VMEM((1 + across - 1 + LEVELS - 1, lines, 1, width), F32),
        pltpu.VMEM((copies, lines, 1, width), F32),
        pltpu.SemaphoreType.DMA((2 * slots,)),
    ]


class Reduce:
    def __init__(self, place, refs, out):
        self.place, self.out = (place, out)
        self.sums, self.landed, self.parts, self.sems = refs

    def group(self, phase):
        place = self.place
        if phase == 0:
            targets = [place.device(other=1)]
            first = 0
        elif phase == 1:
            targets = [place.device(across=across) for across in range(1, place.columns)]
            first = 1
        else:
            targets = [place.device(up=up) for up in range(1, LEVELS)]
            first = place.columns
        return [
            send(self.sums.at[phase], self.landed.at[first + i], self.sems, first + i, target)
            for i, target in enumerate(targets)
        ]

    def rep_copies(self):
        place = self.place
        base = place.columns + LEVELS - 1
        mine = self.parts.at[place.rep]
        return [
            send(mine, mine, self.sems, base + copy - 1, place.device(copy=copy))
            for copy in range(1, place.copies)
        ]

    def start(self, value):
        self.sums[0] = value
        for copy in self.group(0):
            copy.start()

    def next(self, phase):
        copies = self.group(phase)
        for copy in copies:
            copy.wait_recv()
        first = (0, 1, self.place.columns)[phase]
        total = self.sums[phase]
        for i in range(len(copies)):
            total = total + self.landed[first + i]
        if phase < 2:
            self.sums[phase + 1] = total
            for copy in self.group(phase + 1):
                copy.start()
        else:
            self.parts[self.place.rep] = total
            for copy in self.rep_copies():
                copy.start()

    def after_cores(self):
        self.next(0)

    def after_columns(self):
        self.next(1)

    def after_levels(self):
        self.next(2)

    def after_copies(self):
        for copy in self.rep_copies():
            copy.wait_recv()
        total = self.parts[0]
        for rep in range(1, self.place.copies):
            total = total + self.parts[rep]
        self.out[...] = total

    def drain(self):
        for copy in self.group(0) + self.group(1) + self.group(2) + self.rep_copies():
            copy.wait_send()


def label_of(position, start_ref, length_ref, seq, pieces):
    label = jnp.zeros(position.shape, jnp.int32)
    for piece in range(pieces):
        start = start_ref[seq, piece]
        inside = (position >= start) & (position < start + length_ref[seq, piece])
        label = jnp.where(inside, piece + 1, label)
    return label


def key_count(first_row, slot):
    return (first_row // slot + 1) * slot


def block_masks(start_ref, length_ref, seq, pieces, first_row, keys):
    query_pos = first_row + lax.broadcasted_iota(jnp.int32, (ROWS, 1), 0)
    key_pos = lax.broadcasted_iota(jnp.int32, (1, keys), 1)
    query_label = label_of(query_pos, start_ref, length_ref, seq, pieces)
    key_label = label_of(key_pos, start_ref, length_ref, seq, pieces)
    query_label = jnp.where(query_label > 0, query_label, -1)
    allowed = (key_pos <= query_pos) | (query_label == key_label)
    chosen = allowed & (key_pos != 0) & (key_pos != query_pos)
    return (allowed, chosen)


def triangle_sum(triangle, values):
    upper = values.astype(BF16)
    rest = values - upper.astype(F32)
    middle = rest.astype(BF16)
    lower = (rest - middle.astype(F32)).astype(BF16)
    return dot(triangle, upper) + dot(triangle, middle) + dot(triangle, lower)


def head_mask(half):
    lane = lax.broadcasted_iota(jnp.int32, (1, PAIR), 1)
    first = half * HEAD_DIM
    return (lane >= first) & (lane < first + HEAD_DIM)


def at_steps(step, table):
    for when in sorted(set(table)):
        @pl.when(step == when)
        def _(when=when):
            for action in table[when]:
                action()


def schedule(*entries):
    table = {}
    for when, action in entries:
        table.setdefault(when, []).append(action)
    return table


def pair_groups(pairs):
    groups, at = ([], 0)
    for size in [1, 1] + [2] * pairs:
        if at < pairs:
            groups.append(range(at, min(at + size, pairs)))
            at += size
    return groups


def front_kernel(
    slot,
    pieces,
    count,
    copies,
    pairs,
    start_ref,
    length_ref,
    x_hbm,
    wqkv_hbm,
    vec_hbm,
    wo_hbm,
    wu_hbm,
    wd_hbm,
    qkv_ref,
    o_ref,
    inv_ref,
    *rest,
):
    att_refs, rest = (rest[:pieces], rest[pieces:])
    n1_hbm, vec_ref, full_w, full_o, full_u, full_d = rest[:6]
    x_ref, n1_ref, all_ref, stage_ref, w_ref, bias_ref, prefix_ref = rest[6:13]
    stage_sems, load_sems, vec_sems, w_sems, rest_sems = rest[13:]
    pair, seq = (pl.program_id(0), pl.program_id(1))
    sequences = pl.num_programs(1)
    step = pair * sequences + seq
    length = qkv_ref.shape[0]
    width = x_ref.shape[1]
    sequence_count = x_ref.shape[0] // length
    lines = vec_hbm.shape[0]
    zero = jnp.zeros((), BF16)
    place = Place(count, copies)
    twins = copies % 2 == 0

    vec = Gather(place, vec_hbm, all_ref, 0, pl.ds(0, width), False, vec_sems)
    groups = pair_groups(pairs)
    gathers = []
    for i, group in enumerate(groups):
        columns = pl.ds(group[0] * 3 * PAIR, len(group) * 3 * PAIR)
        shared = twins and i > 2 and wqkv_hbm.shape[0] % 48 == 0
        source = stage_ref.at[:, columns]
        gathers.append(Gather(place, source, full_w, 0, columns, shared, w_sems.at[i]))
    cuts = []
    for shard, full, cut_rows, cut_columns in (
        (wo_hbm, full_o, 1, 1),
        (wu_hbm, full_u, 1, 2),
        (wd_hbm, full_d, 2, 1),
    ):
        rows, columns = (shard.shape[0] // cut_rows, shard.shape[1] // cut_columns)
        for i in range(cut_rows):
            for j in range(cut_columns):
                across = pl.ds(j * columns, columns)
                source = shard.at[pl.ds(i * rows, rows), across]
                cuts.append(
                    Gather(place, source, full, i * rows, across, twins, rest_sems.at[len(cuts)])
                )

    def stage_copies():
        found = []
        for p in range(pairs):
            for which in range(3):
                at = 3 * p + which
                found.append(
                    pltpu.make_async_copy(
                        wqkv_hbm.at[:, pl.ds(which * width + p * PAIR, PAIR)],
                        stage_ref.at[:, pl.ds(at * PAIR, PAIR)],
                        stage_sems.at[at],
                    )
                )
        return found

    def load_x():
        return pltpu.make_async_copy(x_hbm, x_ref, load_sems.at[0])

    def keep_n1():
        return pltpu.make_async_copy(n1_ref, n1_hbm, load_sems.at[1])

    def load_w(p):
        return pltpu.make_async_copy(
            full_w.at[:, :, :, pl.ds(p * 3 * PAIR, 3 * PAIR)],
            w_ref.at[p % 2],
            load_sems.at[2 + p % 2],
        )

    def norm_rows(which):
        gain, shift = (vec_ref[GAIN1], vec_ref[SHIFT1])

        def body(i, carry):
            at = pl.ds(pl.multiple_of(which * length + i * ROWS, ROWS), ROWS)
            normed, _ = normalize(x_ref[at, :].astype(F32))
            n1_ref[at, :] = (normed * gain + shift).astype(BF16)
            return carry

        lax.fori_loop(0, length // ROWS, body, 0)
        if which == sequence_count - 1:
            keep_n1().start()

    def begin():
        for copy in stage_copies():
            copy.start()
        load_x().start()
        place.meet(twin=twins)
        vec.start()
        for copy in stage_copies():
            copy.wait()
        for gather in gathers + cuts:
            gather.start()
        vec.after_levels()
        gathers[0].after_levels()
        vec.after_columns()
        gathers[0].after_columns()
        gathers[1].after_levels()
        vec.finish()
        vectors = jnp.zeros((lines, width), F32)
        for chip in range(count // CORES):
            both = all_ref[chip // place.columns, chip % place.columns].astype(F32)
            vectors = vectors + both[:lines] + both[lines:]
        for line in range(lines):
            vec_ref[line] = vectors[line : line + 1, :]
        load_x().wait()
        gathers[0].finish()
        load_w(0).start()
        norm_rows(0)
        gathers[1].after_columns()
        load_w(0).wait()

    def ready(p):
        for group, gather in zip(groups, gathers):
            if p == group[0]:
                gather.finish()
        load_w(p).start()

    s = sequence_count
    entries = [(0, begin)]
    entries += [(which, functools.partial(norm_rows, which)) for which in range(1, s)]
    entries += [
        (1, gathers[2].after_levels),
        (2, gathers[2].after_columns),
    ]
    for i, gather in enumerate(gathers[3:]):
        need = groups[3 + i][0] * s - 1
        entries += [
            (need - 4, gather.after_levels),
            (need - 3, gather.after_columns),
            (need - 2, gather.after_twins),
        ]
    for p in range(1, pairs):
        entries.append((p * s - 1, functools.partial(ready, p)))
        entries.append((p * s, load_w(p).wait))
    for i, cut in enumerate(cuts):
        entries += [
            (FRONT_TABLE[0][i], cut.after_levels),
            (FRONT_TABLE[1][i], cut.after_columns),
            (FRONT_TABLE[2][i], cut.after_twins),
        ]
    at_steps(step, schedule(*entries))

    seq_rows = pl.ds(pl.multiple_of(seq * length, length), length)
    weight = w_ref[lax.rem(pair, 2)].reshape(width, 3 * PAIR)
    qkv_ref[...] = dot(n1_ref[seq_rows, :], weight).astype(BF16)

    @pl.when(pair == 0)
    def _():
        prefix_ref[...] = jnp.zeros_like(prefix_ref)
        row = lax.broadcasted_iota(jnp.int32, (ROWS, ROWS), 0)
        col = lax.broadcasted_iota(jnp.int32, (ROWS, ROWS), 1)
        triangle = (col < row).astype(BF16)
        for first_row in range(0, length, ROWS):
            keys = key_count(first_row, slot)
            at = pl.ds(first_row, ROWS)
            query = jnp.where(head_mask(0), qkv_ref[at, :PAIR], zero)
            scores = dot_nt(query, qkv_ref[:keys, PAIR : 2 * PAIR]) * SCALE
            allowed, chosen = block_masks(start_ref, length_ref, seq, pieces, first_row, keys)
            selected = jnp.where(chosen & (scores > 0), scores, 0.0)
            penalty = prefix_ref[:, :keys] + triangle_sum(triangle, selected)
            bias_ref[seq, at, :keys] = jnp.where(allowed, -penalty, MASKED_VALUE)
            prefix_ref[:, :keys] += column_sum(selected)

    def logits_of(first_row, half):
        keys = key_count(first_row, slot)
        at = pl.ds(first_row, ROWS)
        query = jnp.where(head_mask(half), qkv_ref[at, :PAIR], zero) * jnp.asarray(SCALE, BF16)
        return dot_nt(query, qkv_ref[:keys, PAIR : 2 * PAIR]) + bias_ref[seq, at, :keys]

    def raise_and_mix(first_row, half, logits):
        keys = key_count(first_row, slot)
        largest = jnp.max(logits, axis=-1, keepdims=True)
        raised = jnp.exp(logits - largest)
        inverse = 1.0 / jnp.sum(raised, axis=-1, keepdims=True)
        low = raised.astype(BF16)
        att_refs[first_row // slot][half, pl.ds(first_row % slot, ROWS), :] = low
        value = jnp.where(head_mask(half), qkv_ref[:keys, 2 * PAIR :], zero)
        return (dot(low, value), inverse)

    def finish_rows(first_row, halves):
        (mixed0, inverse0), (mixed1, inverse1) = halves
        at = pl.ds(first_row, ROWS)
        inverse = jnp.where(head_mask(0), inverse0, inverse1)
        inv_ref[at, :] = inverse
        o_ref[at, :] = ((mixed0 + mixed1) * inverse).astype(BF16)

    blocks = [(first_row, half) for first_row in range(0, length, ROWS) for half in range(2)]
    halves, ahead = ([], logits_of(*blocks[0]))
    for i, block in enumerate(blocks):
        logits = ahead
        if i + 1 < len(blocks):
            ahead = logits_of(*blocks[i + 1])
        halves.append(raise_and_mix(*block, logits))
        if len(halves) == 2:
            finish_rows(block[0], halves)
            halves = []

    @pl.when(step == pairs * sequence_count - 1)
    def _():
        for cut in cuts:
            cut.finish()
        for gather in [vec] + gathers + cuts:
            gather.drain()
        keep_n1().wait()


def front(tokens, starts, lengths, wqkv, vectors, wo, wu, wd, devices, copies):
    sequences, pieces = starts.shape
    count, width = tokens.shape
    length = count // sequences
    slot = length // pieces
    pairs = width // PAIR
    lines = vectors.shape[0]
    anywhere = pl.BlockSpec(memory_space=pl.ANY)

    def low(*shape):
        return jax.ShapeDtypeStruct(shape, BF16)

    att_shapes = [low(sequences, 2 * pairs, slot, (i + 1) * slot) for i in range(pieces)]
    att_specs = [
        pl.BlockSpec((None, 2, slot, (i + 1) * slot), lambda p, s, a, b: (s, p, 0, 0))
        for i in range(pieces)
    ]
    across = devices // (LEVELS * CORES)

    def spread(array):
        return (LEVELS, across, CORES * array.shape[0], array.shape[1])

    weights = [low(*spread(w)) for w in (wqkv, wo, wu, wd)]
    sems = gather_sems(devices)
    results = pl.pallas_call(
        functools.partial(front_kernel, slot, pieces, devices, copies, pairs),
        out_shape=[
            low(count, 3 * width),
            low(count, width),
            jax.ShapeDtypeStruct((count, width), F32),
        ]
        + att_shapes
        + [low(count, width), jax.ShapeDtypeStruct((lines, 1, width), F32)]
        + weights,
        grid_spec=pltpu.PrefetchScalarGridSpec(
            num_scalar_prefetch=2,
            grid=(pairs, sequences),
            in_specs=[anywhere] * 6,
            out_specs=[
                pl.BlockSpec((length, 3 * PAIR), lambda p, s, a, b: (s, p)),
                pl.BlockSpec((length, PAIR), lambda p, s, a, b: (s, p)),
                pl.BlockSpec((length, PAIR), lambda p, s, a, b: (s, p)),
            ]
            + att_specs
            + [anywhere, pl.BlockSpec((lines, 1, width), lambda *_: (0, 0, 0))]
            + [anywhere] * 4,
            scratch_shapes=[
                pltpu.VMEM((count, width), BF16),
                pltpu.VMEM((count, width), BF16),
                pltpu.VMEM(spread(vectors), BF16),
                pltpu.VMEM(wqkv.shape, BF16),
                pltpu.VMEM((2,) + spread(wqkv)[:3] + (3 * PAIR,), BF16),
                pltpu.VMEM((sequences, length, length), F32),
                pltpu.VMEM((1, length), F32),
                pltpu.SemaphoreType.DMA((3 * pairs,)),
                pltpu.SemaphoreType.DMA((4,)),
                pltpu.SemaphoreType.DMA((sems,)),
                pltpu.SemaphoreType.DMA((len(pair_groups(pairs)), sems)),
                pltpu.SemaphoreType.DMA((5, sems)),
            ],
        ),
        compiler_params=comm_params(1, "arbitrary", "arbitrary"),
        name="front",
    )(starts, lengths, tokens, wqkv, vectors, wo, wu, wd)
    n1, lines, *weights = results[3 + pieces :]
    weights = [w.reshape(-1, w.shape[-1]) for w in weights]
    return (results[:3], results[3 : 3 + pieces], [n1, lines] + weights)


TAIL = 2
TOGETHER = 2


def attend_back_kernel(
    slot,
    pieces,
    chunks,
    count,
    copies,
    pairs,
    start_ref,
    length_ref,
    qkv_ref,
    gm_ref,
    o_ref,
    inv_ref,
    *rest,
):
    att_hbms, rest = (rest[:pieces], rest[pieces:])
    n1_hbm, n2_hbm, gb_hbm, hid_hbm, cot_hbm, mixed_hbm, gproj_hbm, small_ref = rest[:8]
    g_ref, gqkv_ref, gwo_ref, gwu_ref, gwd_ref, gsmall_ref = rest[8:14]
    later_ref, dq_ref, dk_ref, dv_ref, left_ref, right_ref = rest[14:20]
    load_sem, att_sem = rest[20:22]
    rest = rest[22:]
    sum_refs, att_refs, ds_refs = (rest[i * pieces : (i + 1) * pieces] for i in range(3))
    rest = rest[3 * pieces :]
    step = pl.program_id(0)
    first_step = 2 * chunks + 1
    length = qkv_ref.shape[0]
    width = left_ref.shape[2]
    sequences = left_ref.shape[1] // length
    turns = pairs * sequences
    turn = jnp.maximum(step - first_step, 0)

    place = Place(count, copies)
    parts = []

    def add_part(write, by_level=False):
        at = 6 * len(parts)
        parts.append(Scatter(place, rest[at : at + 6], write, by_level))

    for c in range(chunks):

        def write_up(value, c=c):
            gwu_ref[:, c * width : (c + 1) * width] = value

        add_part(write_up)
    half_rows = gwd_ref.shape[0] // 2
    for h in range(2):

        def write_down(value, h=h):
            gwd_ref[h * half_rows : (h + 1) * half_rows, :] = value

        add_part(write_down, chunks == LEVELS)

    def write_out(value):
        gwo_ref[...] = value

    add_part(write_out)
    for pair in range(pairs - 1, TAIL - 1, -TOGETHER):

        def write_pair(value, pair=pair):
            for at in range(3 * TOGETHER):
                first = (at % 3) * width + (pair - at // 3) * PAIR
                gqkv_ref[:, first : first + PAIR] = value[:, at * PAIR : (at + 1) * PAIR]

        add_part(write_pair)
    small = Reduce(place, rest[6 * len(parts) : 6 * len(parts) + 4], gsmall_ref)
    up_parts, (down0, down1, out_part) = (parts[:chunks], parts[chunks : chunks + 3])
    pair_parts = parts[chunks + 3 :]

    left_slot = [0] * chunks + [(c + 1) % 2 for c in range(chunks)] + [(chunks + 1) % 2]
    right_slot = [c % 2 for c in range(chunks)] + [chunks % 2] * chunks + [(chunks + 1) % 2]

    def chunk_of(ref, c):
        return ref.at[:, pl.ds(c * width, width)]

    left_loads = {0: n2_hbm, 2 * chunks: mixed_hbm}
    right_loads = {chunks: cot_hbm, 2 * chunks: gproj_hbm}
    for c in range(chunks):
        left_loads[chunks + c] = chunk_of(hid_hbm, c)
        right_loads[c] = chunk_of(gb_hbm, c)

    def loads(when):
        found = []
        if when in left_loads:
            at = left_slot[when]
            found.append(
                pltpu.make_async_copy(left_loads[when], left_ref.at[at], load_sem.at[at])
            )
        if when in right_loads:
            at = right_slot[when]
            found.append(
                pltpu.make_async_copy(right_loads[when], right_ref.at[at], load_sem.at[2 + at])
            )
        return found

    n1_slot = chunks % 2

    def load_n1():
        return pltpu.make_async_copy(n1_hbm, left_ref.at[n1_slot], load_sem.at[4])

    def load_att(at, half):
        seq = lax.rem(at, sequences)
        head = 2 * (pairs - 1 - lax.div(at, sequences)) + half
        return [
            pltpu.make_async_copy(
                att_hbms[i].at[seq, head], att_refs[i].at[half], att_sem.at[half * pieces + i]
            )
            for i in range(pieces)
        ]

    def begin():
        for copy in loads(0):
            copy.start()
        place.meet(copies=True)
        small.start(small_ref[...])

    def before_attention():
        load_n1().start()
        for half in range(2):
            for copy in load_att(0, half):
                copy.start()

    entries = [(0, begin), (first_step - 1, before_attention)]
    for c, part in enumerate(up_parts):
        entries += [
            (c + 2, part.after_cores),
            (2 * c + 5, part.after_columns),
            (2 * c + 8, part.after_levels),
            (2 * c + 10, part.after_copies),
        ]
    f = first_step
    late = BACK_TABLE
    names = (down0, down1, out_part) + tuple(pair_parts)
    entries += [
        (3, small.after_cores),
        (6, small.after_columns),
        (10, small.after_levels),
        (13, small.after_copies),
        (f + sequences - 1, load_n1().wait),
    ]
    left_over = []
    for part, whens in zip(names, late):
        actions = (part.after_cores, part.after_columns, part.after_levels, part.after_copies)
        for phase, (when, action) in enumerate(zip(whens, actions)):
            if when < sequences * pairs:
                entries.append((f + when, action))
            else:
                left_over.append((when, phase, action))
    at_steps(step, schedule(*entries))

    @pl.when(step < first_step)
    def _():
        left_at = jnp.zeros((), jnp.int32)
        right_at = jnp.zeros((), jnp.int32)
        for when in range(first_step):

            @pl.when(step == when)
            def _(when=when):
                if when + 1 < first_step:
                    for copy in loads(when + 1):
                        copy.start()
                for copy in loads(when):
                    copy.wait()

            left_at = jnp.where(step == when, left_slot[when], left_at)
            right_at = jnp.where(step == when, right_slot[when], right_at)
        grad = dot_tn(left_ref[left_at], right_ref[right_at]).astype(BF16)
        for when in range(first_step):

            @pl.when(step == when)
            def _(when=when):
                if when < chunks or when == 2 * chunks:
                    part = out_part if when == 2 * chunks else up_parts[when]
                    rows = width // count
                    for block in range(count):
                        part.put(block, grad[block * rows : (block + 1) * rows, :])
                    part.start()
                else:
                    blocks = count // chunks
                    for i in range(blocks):
                        block = (when - chunks) * blocks + i
                        for h, part in enumerate((down0, down1)):
                            at = (2 * i + h) * half_rows
                            part.put(block, grad[at : at + half_rows, :])
                    for part in (down0, down1):
                        if part.by_level:
                            part.core_copies()[when - chunks].start()
                        elif when == 2 * chunks - 1:
                            part.start()

    @pl.when(step >= first_step)
    def _():
        seq = lax.rem(turn, sequences)
        inputs = (qkv_ref, gm_ref, o_ref, inv_ref)
        masks = (slot, pieces, start_ref, length_ref)
        scratch = (sum_refs, att_refs, ds_refs, later_ref, dq_ref, dk_ref, dv_ref)

        @pl.when(turn < sequences)
        def _():
            for ref in sum_refs:
                ref[seq] = jnp.zeros(ref.shape[1:], F32)

        def wait_att(half):
            for copy in load_att(turn, half):
                copy.wait()

        def next_att(half):
            @pl.when(turn < turns - 1)
            def _():
                for copy in load_att(turn + 1, half):
                    copy.start()

        for ref in (dq_ref, dk_ref, dv_ref):
            ref[...] = jnp.zeros_like(ref)
        special = turn >= turns - sequences

        def plain(i, carry):
            half = 1 - i
            wait_att(half)
            head_back(half, False, seq, masks, inputs, scratch)
            next_att(half)
            return carry

        lax.fori_loop(0, jnp.where(special, 1, 2), plain, 0)

        @pl.when(special)
        def _():
            wait_att(0)
            head_back(0, True, seq, masks, inputs, scratch)
            next_att(0)

        grads = (dq_ref[...], jnp.transpose(dk_ref[...]), jnp.transpose(dv_ref[...]))
        keep = pl.ds(pl.multiple_of(seq * length, length), length)
        base = lax.rem(lax.div(turn, sequences), TOGETHER) * (3 * PAIR)
        for which, grad in enumerate(grads):
            low = grad.astype(BF16)
            g_ref[:, which * PAIR : (which + 1) * PAIR] = low
            columns = pl.ds(pl.multiple_of(base + which * PAIR, PAIR), PAIR)
            right_ref[0, keep, columns] = low

    span = TOGETHER * sequences

    @pl.when((step >= first_step) & (lax.rem(turn, span) == span - 1))
    def _():
        @pl.when(turn < (pairs - TAIL) * sequences)
        def _():
            columns = pl.ds(0, TOGETHER * 3 * PAIR)
            grad = dot_tn(left_ref[n1_slot], right_ref[0, :, columns]).astype(BF16)
            rows = width // count
            for i, part in enumerate(pair_parts):

                @pl.when(turn == (i + 1) * span - 1)
                def _(part=part):
                    for block in range(count):
                        part.put(block, grad[block * rows : (block + 1) * rows, :])
                    part.start()

    @pl.when(step == pl.num_programs(0) - 1)
    def _():
        for _, _, action in sorted(left_over, key=lambda item: item[:2]):
            action()
        for part in parts + [small]:
            part.drain()


def head_back(half, first_head, seq, masks, inputs, scratch):
    slot, pieces, start_ref, length_ref = masks
    qkv_ref, gm_ref, o_ref, inv_ref = inputs
    sum_refs, att_refs, ds_refs, later_ref, dq_ref, dk_ref, dv_ref = scratch
    zero = jnp.zeros((), BF16)
    scale = jnp.asarray(SCALE, BF16)
    mask = head_mask(half)

    def scaled_grad(rows):
        return jnp.where(mask, gm_ref[rows, :].astype(F32) * inv_ref[rows, :], 0.0)

    def query_of(rows):
        return jnp.where(mask, qkv_ref[rows, :PAIR], zero) * scale

    if first_head:
        later_ref[...] = jnp.zeros_like(later_ref)
        row = lax.broadcasted_iota(jnp.int32, (ROWS, ROWS), 0)
        col = lax.broadcasted_iota(jnp.int32, (ROWS, ROWS), 1)
        triangle = (col > row).astype(BF16)
    for i in reversed(range(pieces)):
        keys = (i + 1) * slot
        for first in reversed(range(0, slot, ROWS)):
            rows = pl.ds(i * slot + first, ROWS)
            at = pl.ds(first, ROWS)
            scaled = scaled_grad(rows)
            delta = jnp.sum(scaled * o_ref[rows, :].astype(F32), axis=-1, keepdims=True)
            grad_attention = dot_nt(scaled.astype(BF16), qkv_ref[:keys, 2 * PAIR :])
            grad_logits = att_refs[i][half, at, :].astype(F32) * (grad_attention - delta)
            if first_head:
                total = sum_refs[i][seq, at, :] + grad_logits
                grad_selected = -(later_ref[:, :keys] + triangle_sum(triangle, total))
                later_ref[:, :keys] += column_sum(total)
                _, chosen = block_masks(
                    start_ref, length_ref, seq, pieces, i * slot + first, keys
                )
                positive = dot_nt(query_of(rows), qkv_ref[:keys, PAIR : 2 * PAIR]) > 0
                grad_logits = grad_logits + jnp.where(chosen & positive, grad_selected, 0.0)
            else:
                sum_refs[i][seq, at, :] += grad_logits
            ds_refs[i][at, :] = grad_logits.astype(BF16)
        rows = pl.ds(i * slot, slot)
        key = jnp.where(mask, qkv_ref[:keys, PAIR : 2 * PAIR], zero) * scale
        query_part = dot(ds_refs[i][...], key)
        key_part = dot_tn(query_of(rows), ds_refs[i][...])
        value_part = dot_tn(scaled_grad(rows).astype(BF16), att_refs[i][half])
        dq_ref[rows, :] += query_part
        dk_ref[:, :keys] += key_part
        dv_ref[:, :keys] += value_part


def attend_back(
    projected, starts, lengths, grad_mixed, mixed, inverse, attention, kept, small, devices, copies
):
    n1, n2, grad_before, hidden, cotangent, grad_proj = kept
    sequences, pieces = starts.shape
    count, columns = projected.shape
    length = count // sequences
    slot = length // pieces
    width = columns // 3
    pairs = width // PAIR
    chunks = hidden.shape[1] // width
    first_step = 2 * chunks + 1
    rows = width // devices
    down_rows = hidden.shape[1] // devices
    lines = small.shape[0]

    def part(size):
        def index(step, a, b):
            at = jnp.maximum(step - first_step, 0)
            return (lax.rem(at, sequences), pairs - 1 - lax.div(at, sequences))

        return pl.BlockSpec((length, size * PAIR), index)

    anywhere = pl.BlockSpec(memory_space=pl.ANY)

    def fixed(shape):
        return pl.BlockSpec(shape, lambda *_: (0,) * len(shape))

    results = [
        (rows, columns),
        (rows, width),
        (rows, chunks * width),
        (down_rows, width),
        (lines, 1, width),
    ]
    slots = [(slot, (i + 1) * slot) for i in range(pieces)]
    scratch = [
        pltpu.VMEM((1, length), F32),
        pltpu.VMEM((length, PAIR), F32),
        pltpu.VMEM((PAIR, length), F32),
        pltpu.VMEM((PAIR, length), F32),
        pltpu.VMEM((2, count, width), BF16),
        pltpu.VMEM((2, count, width), BF16),
        pltpu.SemaphoreType.DMA((5,)),
        pltpu.SemaphoreType.DMA((2 * pieces,)),
    ]
    scratch += [pltpu.VMEM((sequences,) + shape, F32) for shape in slots]
    scratch += [pltpu.VMEM((2,) + shape, BF16) for shape in slots]
    scratch += [pltpu.VMEM(shape, BF16) for shape in slots]
    for piece_rows in [rows] * chunks + [down_rows // 2] * 2 + [rows]:
        scratch += scatter_scratch(devices, copies, piece_rows, width)
    for _ in range((pairs - TAIL) // TOGETHER):
        scratch += scatter_scratch(devices, copies, rows, TOGETHER * 3 * PAIR)
    scratch += reduce_scratch(devices, copies, lines, width)
    return pl.pallas_call(
        functools.partial(
            attend_back_kernel, slot, pieces, chunks, devices, copies, pairs
        ),
        out_shape=[jax.ShapeDtypeStruct((count, columns), BF16)]
        + [jax.ShapeDtypeStruct(shape, F32) for shape in results],
        grid_spec=pltpu.PrefetchScalarGridSpec(
            num_scalar_prefetch=2,
            grid=(first_step + sequences * pairs,),
            in_specs=[part(3)]
            + [part(1)] * 3
            + [anywhere] * (pieces + 7)
            + [fixed((lines, 1, width))],
            out_specs=[part(3)] + [fixed(shape) for shape in results],
            scratch_shapes=scratch,
        ),
        compiler_params=comm_params(2, "arbitrary"),
        name="attend_back",
    )(
        starts,
        lengths,
        projected,
        grad_mixed,
        mixed,
        inverse,
        *attention,
        n1,
        n2,
        grad_before,
        hidden,
        cotangent,
        mixed,
        grad_proj,
        small,
    )


def gelu_and_slope(values):
    square = values * values
    inner = GELU_IN * values * (1.0 + GELU_CUBE * square)
    bent = jnp.tanh(inner)
    half = 0.5 * (1.0 + bent)
    slope = half + 0.5 * values * (1.0 - bent * bent) * (
        GELU_IN * (1.0 + 3.0 * GELU_CUBE * square)
    )
    return (values * half, slope)


def feed_kernel(
    chunk,
    x_ref,
    mixed_ref,
    cot_ref,
    gain_ref,
    shift_ref,
    up_bias_ref,
    down_bias_ref,
    wo_hbm,
    wu_hbm,
    wd_hbm,
    out_ref,
    gmid_ref,
    gmix_ref,
    small_ref,
    n2_ref,
    hid_ref,
    gb_ref,
    gproj_ref,
    wo_ref,
    wu_ref,
    wd_ref,
    acc_ref,
    gnorm_ref,
    mid_ref,
    load_sem,
):
    step = pl.program_id(0)
    chunks = wu_ref.shape[0]

    def load_out():
        return pltpu.make_async_copy(wo_hbm, wo_ref, load_sem.at[0])

    def load_up(c):
        return pltpu.make_async_copy(
            wu_hbm.at[:, pl.ds(c * chunk, chunk)], wu_ref.at[c], load_sem.at[1 + 2 * c]
        )

    def load_down(c):
        return pltpu.make_async_copy(
            wd_hbm.at[pl.ds(c * chunk, chunk), :], wd_ref.at[c], load_sem.at[2 + 2 * c]
        )

    @pl.when(step == 0)
    def _():
        load_out().start()
        for c in range(chunks):
            load_up(c).start()
            load_down(c).start()
        small_ref[...] = jnp.zeros_like(small_ref)
        load_out().wait()

    mid_ref[...] = x_ref[...].astype(F32) + dot(mixed_ref[...], wo_ref[...])

    @pl.when(step == 0)
    def _():
        for c in range(chunks):
            load_up(c).wait()
            load_down(c).wait()

    normed, _ = normalize(mid_ref[...])
    n2_ref[...] = (normed * gain_ref[...] + shift_ref[...]).astype(BF16)
    def open_chunk(c):
        before = dot(n2_ref[...], wu_ref[c]) + up_bias_ref[c]
        grad_hidden = dot_nt(cot_ref[...], wd_ref[c]).astype(BF16)
        return (before, grad_hidden)

    ahead = open_chunk(0)
    for c in range(chunks):
        before, grad_hidden = ahead
        if c + 1 < chunks:
            ahead = open_chunk(c + 1)
        columns = slice(c * chunk, (c + 1) * chunk)
        hidden, slope = gelu_and_slope(before)
        hidden = hidden.astype(BF16)
        hid_ref[:, columns] = hidden
        grad_before = (grad_hidden.astype(F32) * slope).astype(BF16)
        gb_ref[:, columns] = grad_before
        small_ref[3 + c] += column_sum(grad_before.astype(F32))
        down = dot(hidden, wd_ref[c])
        back = dot_nt(grad_before, wu_ref[c])
        if c == 0:
            acc_ref[...] = down
            gnorm_ref[...] = back
        else:
            acc_ref[...] += down
            gnorm_ref[...] += back

    out_ref[...] = (mid_ref[...] + (acc_ref[...] + down_bias_ref[...])).astype(BF16)
    grad_normed = gnorm_ref[...]
    normed, inverse = normalize(mid_ref[...])
    cot = cot_ref[...].astype(F32)
    small_ref[0] += column_sum(grad_normed * normed)
    small_ref[1] += column_sum(grad_normed)
    small_ref[2] += column_sum(cot)
    grad_middle = cot + norm_back(grad_normed * gain_ref[...], normed, inverse)
    gmid_ref[...] = grad_middle
    grad_proj = grad_middle.astype(BF16)
    gproj_ref[...] = grad_proj
    gmix_ref[...] = dot_nt(grad_proj, wo_ref[...]).astype(BF16)


def vector_line(row):
    return lambda width: pl.BlockSpec((None, 1, width), lambda *_: (row, 0, 0))


def feed(tokens, mixed, cotangent, vectors, wo, wu, wd):
    count, width = tokens.shape
    hidden = wu.shape[1]
    block = 512
    chunk = width
    chunks = hidden // chunk
    rows = pl.BlockSpec((block, width), lambda i: (i, 0))
    anywhere = pl.BlockSpec(memory_space=pl.ANY)
    wide = pl.BlockSpec((block, hidden), lambda i: (i, 0))

    def low(columns):
        return jax.ShapeDtypeStruct((count, columns), BF16)

    return pl.pallas_call(
        functools.partial(feed_kernel, chunk),
        out_shape=[
            low(width),
            jax.ShapeDtypeStruct((count, width), F32),
            low(width),
            jax.ShapeDtypeStruct((3 + chunks, 1, width), F32),
            low(width),
            low(hidden),
            low(hidden),
            low(width),
        ],
        grid=(count // block,),
        in_specs=[
            rows,
            rows,
            rows,
            vector_line(GAIN2)(width),
            vector_line(SHIFT2)(width),
            pl.BlockSpec((chunks, 1, chunk), lambda i: (0, 0, 0)),
            vector_line(DOWN_BIAS)(width),
            anywhere,
            anywhere,
            anywhere,
        ],
        out_specs=[
            rows,
            rows,
            rows,
            pl.BlockSpec((3 + chunks, 1, width), lambda i: (0, 0, 0)),
            rows,
            wide,
            wide,
            rows,
        ],
        scratch_shapes=[
            pltpu.VMEM(wo.shape, BF16),
            pltpu.VMEM((chunks, width, chunk), BF16),
            pltpu.VMEM((chunks, chunk, width), BF16),
            pltpu.VMEM((block, width), F32),
            pltpu.VMEM((block, width), F32),
            pltpu.VMEM((block, width), F32),
            pltpu.SemaphoreType.DMA((1 + 2 * chunks,)),
        ],
        compiler_params=params("arbitrary"),
        name="feed",
    )(
        tokens,
        mixed,
        cotangent,
        vectors,
        vectors,
        vectors,
        vectors,
        wo,
        wu,
        wd,
    )


def input_kernel(
    count,
    copies,
    gmid_ref,
    gain_ref,
    shift_ref,
    rest_ref,
    x_hbm,
    n1_hbm,
    g_hbm,
    w_hbm,
    gx_ref,
    gw_ref,
    gsmall_ref,
    x_ref,
    n1_ref,
    g_ref,
    w_ref,
    small_ref,
    load_sem,
    *rest,
):
    step = pl.program_id(0)
    total, width = x_ref.shape
    columns = w_ref.shape[1]
    block = gx_ref.shape[0]
    first = TAIL * 3 * PAIR
    place = Place(count, copies)

    def write(value):
        gw_ref[...] = rest_ref[...]
        for at in range(3 * TAIL):
            to = (at % 3) * width + (at // 3) * PAIR
            gw_ref[:, to : to + PAIR] = value[:, at * PAIR : (at + 1) * PAIR]

    part = Scatter(place, rest[:6], write)
    small = Reduce(place, rest[6:10], gsmall_ref)

    def loads():
        near, far = (pl.ds(0, first), pl.ds(first, columns - first))
        pairs = [
            (n1_hbm, n1_ref),
            (g_hbm.at[:, near], g_ref.at[:, near]),
            (x_hbm, x_ref),
            (g_hbm.at[:, far], g_ref.at[:, far]),
            (w_hbm, w_ref),
        ]
        return [
            pltpu.make_async_copy(source, target, load_sem.at[i])
            for i, (source, target) in enumerate(pairs)
        ]

    def begin():
        for copy in loads():
            copy.start()
        place.meet(copies=True)
        small_ref[...] = jnp.zeros_like(small_ref)
        for copy in loads()[:2]:
            copy.wait()
        grad = dot_tn(n1_ref[...], g_ref[:, :first]).astype(BF16)
        rows = width // count
        for i in range(count):
            part.put(i, grad[i * rows : (i + 1) * rows, :])
        part.start()
        for copy in loads()[2:]:
            copy.wait()

    steps = total // block
    table = schedule(
        (0, begin),
        (1, part.after_cores),
        (min(3, steps - 1), part.after_columns),
    )
    at_steps(step, table)

    normed, inverse = normalize(
        x_ref[pl.ds(pl.multiple_of(step * block, block), block), :].astype(F32)
    )
    grads = g_ref[pl.ds(pl.multiple_of(step * block, block), block), :]
    grad_normed = dot_nt(grads, w_ref[...])
    small_ref[0] += column_sum(grad_normed * normed)
    small_ref[1] += column_sum(grad_normed)

    @pl.when(step == steps - 1)
    def _():
        small.start(small_ref[...])

    gx_ref[...] = gmid_ref[...] + norm_back(grad_normed * gain_ref[...], normed, inverse)

    @pl.when(step == steps - 1)
    def _():
        small.after_cores()
        part.after_levels()
        small.after_columns()
        part.after_copies()
        small.after_levels()
        small.after_copies()
        part.drain()
        small.drain()


def input_back(tokens, n1, grad_middle, grads, grad_rest, vectors, weight, devices, copies):
    count, width = tokens.shape
    block = 512
    shard = width // devices
    rows = pl.BlockSpec((block, width), lambda i: (i, 0))
    own = pl.BlockSpec((shard, 3 * width), lambda i: (0, 0))
    anywhere = pl.BlockSpec(memory_space=pl.ANY)
    scratch = [
        pltpu.VMEM((count, width), BF16),
        pltpu.VMEM((count, width), BF16),
        pltpu.VMEM((count, 3 * width), BF16),
        pltpu.VMEM(weight.shape, BF16),
        pltpu.VMEM((2, 1, width), F32),
        pltpu.SemaphoreType.DMA((5,)),
    ]
    scratch += scatter_scratch(devices, copies, shard, TAIL * 3 * PAIR)
    scratch += reduce_scratch(devices, copies, 2, width)
    return pl.pallas_call(
        functools.partial(input_kernel, devices, copies),
        out_shape=[
            jax.ShapeDtypeStruct((count, width), F32),
            jax.ShapeDtypeStruct((shard, 3 * width), F32),
            jax.ShapeDtypeStruct((2, 1, width), F32),
        ],
        grid=(count // block,),
        in_specs=[rows, vector_line(GAIN1)(width), vector_line(SHIFT1)(width), own]
        + [anywhere] * 4,
        out_specs=[
            rows,
            own,
            pl.BlockSpec((2, 1, width), lambda i: (0, 0, 0)),
        ],
        scratch_shapes=scratch,
        compiler_params=comm_params(3, "arbitrary"),
        name="input_back",
    )(grad_middle, vectors, vectors, grad_rest, tokens, n1, grads, weight)


def local(
    tokens,
    piece_start,
    piece_length,
    query_key_value,
    output_weight,
    up_weight,
    down_weight,
    first_gain,
    first_shift,
    second_gain,
    second_shift,
    up_bias,
    down_bias,
    cotangent,
):
    width = tokens.shape[1]
    devices, copies = (lax.axis_size("fsdp"), lax.axis_size("rep"))
    index = lax.axis_index("fsdp")

    lines = jnp.stack([first_gain, first_shift, second_gain, second_shift, down_bias])
    own = lax.dynamic_update_slice(
        jnp.zeros((LINES - up_bias.shape[0] * devices // width, width), BF16),
        lines,
        (0, index * lines.shape[1]),
    )
    wide = lax.dynamic_update_slice(
        jnp.zeros((devices * up_bias.shape[0],), BF16), up_bias, (index * up_bias.shape[0],)
    )
    own = jnp.concatenate([wide.reshape(-1, width), own], axis=0)

    (projected, mixed, inverse), attention, (n1, vectors, wqkv, wo, wu, wd) = front(
        tokens,
        piece_start,
        piece_length,
        query_key_value,
        own,
        output_weight,
        up_weight,
        down_weight,
        devices,
        copies,
    )
    block_output, grad_middle, grad_mixed, small2, n2, hidden, grad_before, grad_proj = feed(
        tokens, mixed, cotangent, vectors, wo, wu, wd
    )
    grads, grad_rest, gwo, gwu, gwd, small2 = attend_back(
        projected,
        piece_start,
        piece_length,
        grad_mixed,
        mixed,
        inverse,
        attention,
        (n1, n2, grad_before, hidden, cotangent, grad_proj),
        small2,
        devices,
        copies,
    )
    grad_tokens, gwqkv, small1 = input_back(
        tokens, n1, grad_middle, grads, grad_rest, vectors, wqkv, devices, copies
    )

    def mine(values):
        values = values.reshape(-1)
        size = values.shape[0] // devices
        return lax.dynamic_slice(values, (index * size,), (size,))

    return (
        block_output,
        grad_tokens,
        gwqkv,
        gwo,
        gwu,
        gwd,
        mine(small1[0]),
        mine(small1[1]),
        mine(small2[0]),
        mine(small2[1]),
        mine(small2[3:]),
        mine(small2[2]),
    )


def solution(mesh):
    rows = P(("fsdp", "rep"), None)
    matrix = P("fsdp", None)
    vector = P("fsdp")
    return jax.shard_map(
        local,
        mesh=mesh,
        in_specs=(rows,) * 3 + (matrix,) * 4 + (vector,) * 6 + (rows,),
        out_specs=(rows,) * 2 + (matrix,) * 4 + (vector,) * 6,
        check_vma=False,
    )
```
